32 devices in a mesh: batch: 2 (over x), seq: 16 (over z, y, core).
Axes of the slice: x: 2, y: 2, z: 4, core: 2. Of those that a mesh axis runs over, the one named last changes fastest.
Arguments:
- tokens: bfloat16 [4, 1024, 1024], P('batch', 'seq'), may hold values from -6 to 6
- segments: int32 [4, 1024], P('batch', 'seq'), may hold values from 0 to 3, never falling along the last dimension, each value on 1 to 512 neighbouring positions
- norm1_gain: float32 [1024], replicated, may hold values from 0.5 to 1.5
- norm1_bias: float32 [1024], replicated, may hold values from -3 to 3
- decay_log: float32 [1024, 64], replicated, may hold values from -1 to 0.5
- decay_freq: float32 [1024, 64], replicated, may hold values from 0 to 192
- input_re: float32 [1024, 64], replicated, may hold values from -6 to 6
- input_im: float32 [1024, 64], replicated, may hold values from -6 to 6
- output_re: float32 [1024, 64], replicated, may hold values from -6 to 6
- output_im: float32 [1024, 64], replicated, may hold values from -6 to 6
- step_log: float32 [1024], replicated, may hold values from -9.2 to -2.3
- skip_gain: float32 [1024], replicated, may hold values from -6 to 6
- glu_weight: bfloat16 [1024, 2048], replicated, may hold values from -0.1875 to 0.1875
- glu_bias: float32 [2048], replicated, may hold values from -3 to 3
- norm2_gain: float32 [1024], replicated, may hold values from 0.5 to 1.5
- norm2_bias: float32 [1024], replicated, may hold values from -3 to 3
- ffn_in: bfloat16 [1024, 4096], replicated, may hold values from -0.1875 to 0.1875
- ffn_in_bias: float32 [4096], replicated, may hold values from -3 to 3
- ffn_out: bfloat16 [4096, 1024], replicated, may hold values from -0.09375 to 0.09375
- ffn_out_bias: float32 [1024], replicated, may hold values from -3 to 3
- cotangent: bfloat16 [4, 1024, 1024], P('batch', 'seq'), may hold values from -6 to 6
Outputs:
- result: bfloat16 [4, 1024, 1024], P('batch', 'seq')
- grad_tokens: bfloat16 [4, 1024, 1024], P('batch', 'seq')
- grad_norm1_gain: float32 [1024], replicated
- grad_norm1_bias: float32 [1024], replicated
- grad_decay_log: float32 [1024, 64], replicated
- grad_decay_freq: float32 [1024, 64], replicated
- grad_input_re: float32 [1024, 64], replicated
- grad_input_im: float32 [1024, 64], replicated
- grad_output_re: float32 [1024, 64], replicated
- grad_output_im: float32 [1024, 64], replicated
- grad_step_log: float32 [1024], replicated
- grad_skip_gain: float32 [1024], replicated
- grad_glu_weight: float32 [1024, 2048], P('seq')
- grad_glu_bias: float32 [2048], replicated
- grad_norm2_gain: float32 [1024], replicated
- grad_norm2_bias: float32 [1024], replicated
- grad_ffn_in: float32 [1024, 4096], P('seq')
- grad_ffn_in_bias: float32 [4096], replicated
- grad_ffn_out: float32 [4096, 1024], P('seq')
- grad_ffn_out_bias: float32 [1024], replicated
The draws below stay inside these ranges and needn't reach their ends.
Inputs may be any that keep to these rules, and one draw needn't show every extreme that they name: `segments`: within each context the document numbers start at 0 and never fall from one position to the next; a document holds at most min(512, 1021) positions.
All inputs are finite; a program needn't handle non-finite values.
Results may differ from the reference program's by a relative error of at most 0.0061.
Values sent between devices are 32-bit elements; how exact they have to be, the bound alone decides.
No kernel may reach another device: no remote copies, remote signals or barrier semaphores. Data moves between devices by JAX's collectives and lax.ppermute only.
A program may use at most 640 MiB of HBM per device.

```python
import math
import jax
import jax.numpy as jnp
import numpy as np
from jax import lax

H = 1024
N = 64
FF = 4096
SUB = 64
DOC = 256
CONTEXTS = 4
LENGTH = 1024


def block_levels(key, dims, split, least, high):
    def one(dim, shards_of):
        steps = jax.random.uniform(jax.random.fold_in(jax.random.fold_in(key, 6), dim), (shards_of,), jnp.float32, least / len(split), high / len(split))
        return jnp.repeat(jnp.exp(steps), dims[dim] // shards_of).reshape((-1,) + (1,) * (len(dims) - dim - 1))

    loudness = one(*split[0])
    for cut in split[1:]:
        loudness = loudness * one(*cut)
    return loudness


def length_profile(count, total, bound, skew):
    weights = [(1 << 20) // math.isqrt(grade ** skew) + 1 for grade in range(2, count + 1)]
    spare, counts = total - bound - (count - 1), [1] * (count - 1)
    while spare > 0:
        candidates = [i for i in range(count - 1) if counts[i] < bound]
        mass, left = sum([weights[i] for i in candidates]), spare
        for i in candidates:
            more = min(bound - counts[i], max(1, left * weights[i] // mass), spare)
            counts[i] = counts[i] + more
            spare = spare - more
    return np.array([bound] + counts)


def ragged(stream_key, number_of, total, reach, lean):
    if number_of == 2:
        one = jax.random.randint(stream_key, (), max(1, total - reach), min(reach, total - 1) + 1)
        return jnp.stack([one, total - one])
    tallies = jnp.asarray(length_profile(number_of, total, reach, lean), jnp.int32)
    couples = (number_of - 1) // 2
    donor, sink = tallies[1:1 + 2 * couples:2], tallies[2:2 + 2 * couples:2]
    room = jnp.minimum(donor - 1, reach - sink)
    moved = jax.random.randint(jax.random.fold_in(stream_key, 1), (couples,), 0, 1 << 20) % (room + 1)
    tallies = tallies.at[1:1 + 2 * couples:2].set(donor - moved).at[2:2 + 2 * couples:2].set(sink + moved)
    return tallies[jax.random.permutation(jax.random.fold_in(stream_key, 2), number_of)]


def noise(stream_key, extent, width, most, cuts=(), held_as=jnp.bfloat16):
    gain = block_levels(stream_key, extent, cuts, -0.22, 0.18) if cuts else 1.0
    values = jax.random.normal(stream_key, extent, jnp.float32) * width * gain
    return jnp.minimum(jnp.maximum(values, -most), most).astype(held_as)


def setup_inputs(seed: int = 0) -> dict:
    keys = jax.random.split(jax.random.key(seed), 22)
    tokens = noise(keys[0], (CONTEXTS, LENGTH, H), 1.0, 6.0, ((0, 2), (1, 16)))
    segments = jax.vmap(lambda own: jnp.searchsorted(jnp.cumsum(ragged(own, LENGTH // DOC, LENGTH, min(2 * DOC, LENGTH - LENGTH // DOC + 1), 1)), jnp.arange(LENGTH), side="right"))(jax.random.split(keys[1], CONTEXTS)).reshape((CONTEXTS, LENGTH)).astype(jnp.int32)
    norm1_gain = jnp.clip(1.0 + 0.1 * jax.random.normal(keys[2], (H,), jnp.float32), 0.5, 1.5)
    norm1_bias = noise(keys[3], (H,), 0.5, 3.0, (), jnp.float32)
    decay_log = jnp.clip(jax.random.uniform(keys[4], (H, N), jnp.float32, -1.0, 0.5), -1.0, 0.5)
    decay_freq = jnp.clip(jax.random.uniform(keys[5], (H, N), jnp.float32, 0.0, 192.0), 0.0, 192.0)
    input_re = noise(keys[6], (H, N), 1.0, 6.0, (), jnp.float32)
    input_im = noise(keys[7], (H, N), 1.0, 6.0, (), jnp.float32)
    output_re = noise(keys[8], (H, N), 1.0, 6.0, (), jnp.float32)
    output_im = noise(keys[9], (H, N), 1.0, 6.0, (), jnp.float32)
    step_log = jnp.clip(jax.random.uniform(keys[10], (H,), jnp.float32, -9.2, -2.3), -9.2, -2.3)
    skip_gain = noise(keys[11], (H,), 1.0, 6.0, (), jnp.float32)
    glu_weight = noise(keys[12], (H, 2 * H), H ** -0.5, 0.1875)
    glu_bias = noise(keys[13], (2 * H,), 0.5, 3.0, (), jnp.float32)
    norm2_gain = jnp.clip(1.0 + 0.1 * jax.random.normal(keys[14], (H,), jnp.float32), 0.5, 1.5)
    norm2_bias = noise(keys[15], (H,), 0.5, 3.0, (), jnp.float32)
    ffn_in = noise(keys[16], (H, FF), H ** -0.5, 0.1875)
    ffn_in_bias = noise(keys[17], (FF,), 0.5, 3.0, (), jnp.float32)
    ffn_out = noise(keys[18], (FF, H), FF ** -0.5, 0.09375)
    ffn_out_bias = noise(keys[19], (H,), 0.5, 3.0, (), jnp.float32)
    cotangent = noise(keys[20], (CONTEXTS, LENGTH, H), 1.0, 6.0, ((0, 2), (1, 16)))
    return dict(tokens=tokens, segments=segments, norm1_gain=norm1_gain, norm1_bias=norm1_bias, decay_log=decay_log, decay_freq=decay_freq, input_re=input_re, input_im=input_im, output_re=output_re, output_im=output_im, step_log=step_log, skip_gain=skip_gain, glu_weight=glu_weight, glu_bias=glu_bias, norm2_gain=norm2_gain, norm2_bias=norm2_bias, ffn_in=ffn_in, ffn_in_bias=ffn_in_bias, ffn_out=ffn_out, ffn_out_bias=ffn_out_bias, cotangent=cotangent)


@jax.custom_vjp
def low(v):
    return lax.optimization_barrier(v.astype(jnp.bfloat16)).astype(jnp.float32)

@jax.custom_vjp
def low_back(v):
    return v

def low_keep(v):
    return (low(v), None)

def low_pass(kept, grad):
    return (grad,)

def back_keep(v):
    return (v, None)

def back_low(kept, grad):
    return (low(grad),)
low.defvjp(low_keep, low_pass)
low_back.defvjp(back_keep, back_low)
EPSILON = 1e-05

def mode_power(delta_re, delta_im, exponent):
    magnitude = jnp.exp(exponent * delta_re)
    phase_angle = exponent * delta_im
    return (magnitude * jnp.cos(phase_angle), magnitude * jnp.sin(phase_angle))

def mode_tables(params, span_len):
    decay_log, decay_freq, input_re, input_im, output_re, output_im, step_log = params
    step_size = jnp.exp(step_log)[:, None]
    real_part = -jnp.exp(decay_log)
    delta_re = step_size * real_part
    delta_im = step_size * decay_freq
    lam_re, lam_im = mode_power(delta_re, delta_im, 1.0)
    denominator = real_part * real_part + decay_freq * decay_freq
    num_re = lam_re - 1.0
    rat_re = (num_re * real_part + lam_im * decay_freq) / denominator
    rat_im = (lam_im * real_part - num_re * decay_freq) / denominator
    bbar_re = rat_re * input_re - rat_im * input_im
    bbar_im = rat_re * input_im + rat_im * input_re
    prod_re = output_re * bbar_re - output_im * bbar_im
    prod_im = output_re * bbar_im + output_im * bbar_re
    power_steps = jnp.arange(span_len, dtype=jnp.float32)[:, None, None]
    pow_re, pow_im = mode_power(delta_re, delta_im, power_steps)
    kernel = 2.0 * lax.optimization_barrier(jnp.sum(prod_re * pow_re - prod_im * pow_im, axis=2))
    next_re, next_im = mode_power(delta_re, delta_im, power_steps + 1.0)
    cl_re = output_re * next_re - output_im * next_im
    cl_im = output_re * next_im + output_im * next_re
    back_re, back_im = mode_power(delta_re, delta_im, span_len - 1.0 - power_steps)
    lb_re = back_re * bbar_re - back_im * bbar_im
    lb_im = back_re * bbar_im + back_im * bbar_re
    lag_index = jnp.arange(span_len)
    onehot = (lag_index[:, None, None] == lag_index[None, :, None] - lag_index[None, None, :]).astype(jnp.float32)
    toeplitz = jnp.einsum('ktj,kh->tjh', onehot, kernel, precision=lax.Precision.HIGHEST)
    return (toeplitz, cl_re, cl_im, lb_re, lb_im, delta_re, delta_im)

def block_step(consts, state_re, state_im, previous, block_in, block_seg):
    toeplitz, cl_re, cl_im, lb_re, lb_im, delta_re, delta_im = consts
    span_len = block_seg.shape[1]
    lag_index = jnp.arange(span_len)
    causal = lag_index[:, None] >= lag_index[None, :]
    same_doc = ((block_seg[:, :, None] == block_seg[:, None, :]) & causal[None]).astype(jnp.float32)
    weights = toeplitz[None] * same_doc[:, :, :, None]
    local_sum = jnp.einsum('ctjh,cjh->cth', weights, block_in, precision=lax.Precision.HIGHEST)
    carried = (block_seg == previous[:, None]).astype(jnp.float32)
    injected = 2.0 * (jnp.einsum('thn,chn->cth', cl_re, state_re, precision=lax.Precision.HIGHEST) - jnp.einsum('thn,chn->cth', cl_im, state_im, precision=lax.Precision.HIGHEST))
    outcome = local_sum + carried[:, :, None] * injected
    tail_mask = (block_seg == block_seg[:, -1:]).astype(jnp.float32)
    masked = block_in * tail_mask[:, :, None]
    new_re = jnp.einsum('jhn,cjh->chn', lb_re, masked, precision=lax.Precision.HIGHEST)
    new_im = jnp.einsum('jhn,cjh->chn', lb_im, masked, precision=lax.Precision.HIGHEST)
    keep_state = carried[:, -1][:, None, None]
    full_re, full_im = mode_power(delta_re, delta_im, float(span_len))
    new_re = new_re + keep_state * (full_re * state_re - full_im * state_im)
    new_im = new_im + keep_state * (full_re * state_im + full_im * state_re)
    return (outcome, new_re, new_im, block_seg[:, -1])

def state_mixer(params, mixin, segments):
    consts = mode_tables(params, SUB)
    contexts, positions, features = mixin.shape
    blocks = positions // SUB
    block_in = mixin.reshape(contexts, blocks, SUB, features).transpose(1, 0, 2, 3)
    block_seg = segments.reshape(contexts, blocks, SUB).transpose(1, 0, 2)

    def stepper(carry_in, block_items):
        state_re, state_im, previous = carry_in
        outcome, new_re, new_im, last_seg = block_step(consts, state_re, state_im, previous, block_items[0], block_items[1])
        return ((new_re, new_im, last_seg), outcome)
    zero_state = jnp.zeros((contexts,) + consts[1].shape[1:], jnp.float32)
    initial = (zero_state, zero_state, -jnp.ones((contexts,), jnp.int32))
    final_carry, block_outs = lax.scan(jax.checkpoint(stepper), initial, (block_in, block_seg))
    return block_outs.transpose(1, 0, 2, 3).reshape(contexts, positions, features)

def layer_norm(values, norm_gain, norm_shift):
    centre = values - lax.optimization_barrier(jnp.mean(values, axis=-1, keepdims=True))
    spread = lax.optimization_barrier(jnp.mean(centre * centre, axis=-1, keepdims=True))
    return centre * lax.rsqrt(spread + EPSILON) * norm_gain + norm_shift

def gated_unit(values):
    middle = values.shape[-1] // 2
    return values[..., :middle] * jax.nn.sigmoid(values[..., middle:])

def dense(left, right):
    shaped = left.reshape(-1, left.shape[-1])
    product = jnp.dot(shaped, right, precision=lax.Precision.HIGHEST, preferred_element_type=jnp.float32)
    return product.reshape(left.shape[:-1] + (right.shape[1],))

def whole_layer(values, segments):
    floats, norm1_gain, norm1_bias, decay_log, decay_freq, input_re, input_im, output_re, output_im, step_log, skip_gain, glu_weight, glu_bias, norm2_gain, norm2_bias, ffn_in, ffn_in_bias, ffn_out, ffn_out_bias = values
    normed = layer_norm(floats, norm1_gain, norm1_bias)
    params = (decay_log, decay_freq, input_re, input_im, output_re, output_im, step_log)
    mixed_out = state_mixer(params, normed, segments) + skip_gain * normed
    activation = low(jax.nn.gelu(mixed_out, approximate=False))
    glu_pre = low_back(dense(activation, glu_weight) + glu_bias)
    hidden = floats + gated_unit(glu_pre)
    normed_two = low(layer_norm(hidden, norm2_gain, norm2_bias))
    ffn_pre = low_back(dense(normed_two, ffn_in) + ffn_in_bias)
    ffn_act = low(jax.nn.gelu(ffn_pre, approximate=False))
    ffn_res = low_back(dense(ffn_act, ffn_out) + ffn_out_bias)
    return hidden + ffn_res

def reference(tokens, segments, norm1_gain, norm1_bias, decay_log, decay_freq, input_re, input_im, output_re, output_im, step_log, skip_gain, glu_weight, glu_bias, norm2_gain, norm2_bias, ffn_in, ffn_in_bias, ffn_out, ffn_out_bias, cotangent):
    floats = (tokens.astype(jnp.float32), norm1_gain, norm1_bias, decay_log, decay_freq, input_re, input_im, output_re, output_im, step_log, skip_gain, glu_weight.astype(jnp.float32), glu_bias, norm2_gain, norm2_bias, ffn_in.astype(jnp.float32), ffn_in_bias, ffn_out.astype(jnp.float32), ffn_out_bias)

    def forward(*values):
        return whole_layer(values, segments)
    result, pullback = jax.vjp(forward, *floats)
    gradients = pullback(cotangent.astype(jnp.float32))
    return (result.astype(jnp.bfloat16), gradients[0].astype(jnp.bfloat16), gradients[1], gradients[2], gradients[3], gradients[4], gradients[5], gradients[6], gradients[7], gradients[8], gradients[9], gradients[10], gradients[11], gradients[12], gradients[13], gradients[14], gradients[15], gradients[16], gradients[17], gradients[18])
```

```python
import jax, jax.numpy as jnp
from jax import lax
from jax.sharding import PartitionSpec as P
from jax.experimental import pallas as pl
from jax.experimental.pallas import tpu as pltpu
F32, BF16 = jnp.float32, jnp.bfloat16
LANES = 128
HALF = 64
FORWARD_UNROLL = 4
BACKWARD_UNROLL = 2
NN = (((1,), (0,)), ((), ()))
NT = (((1,), (1,)), ((), ()))
TN = (((0,), (0,)), ((), ()))


def halves(value):
    high = value.astype(BF16)
    return high, (value - high.astype(F32)).astype(BF16)


def mm(left, right, dims):
    out = lax.dot_general(left[0], right[0], dims, preferred_element_type=F32)
    out = out + lax.dot_general(left[1], right[0], dims, preferred_element_type=F32)
    return out + lax.dot_general(left[0], right[1], dims, preferred_element_type=F32)


def swap(value):
    return pltpu.roll(value, HALF, value.ndim - 1)


def low_lanes(shape):
    return lax.broadcasted_iota(jnp.int32, shape, len(shape) - 1) < HALF


def as_factor(value):
    turned = swap(value)
    low = low_lanes(value.shape)
    return jnp.where(low, value, turned), jnp.where(low, -turned, value)


def times(value, factor):
    return value * factor[0] + swap(value) * factor[1]


def power_setup(lam, base_ref, fre_ref, fim_ref, steps, channels):
    one = jnp.where(low_lanes(lam.shape), 1.0, 0.0)
    factor = as_factor(lam)
    row = one
    for k in range(8):
        base_ref[pl.ds(k * channels, channels), :] = row
        row = times(row, factor)
    eight = as_factor(row)
    row = one
    for i in range(16):
        fre, fim = as_factor(row)
        fre_ref[pl.ds(i * channels, channels), :] = fre
        fim_ref[pl.ds(i * channels, channels), :] = fim
        row = times(row, eight)
    for s in range(steps):
        fre, fim = as_factor(row)
        fre_ref[pl.ds((16 + s) * channels, channels), :] = fre
        fim_ref[pl.ds((16 + s) * channels, channels), :] = fim
        row = times(row, (fre, fim))


def power_tables(h, base_ref, fre_ref, fim_ref, channels):
    base = base_ref[pl.ds(h, 8, stride=channels), :]
    fre = fre_ref[pl.ds(h, 16, stride=channels), :]
    fim = fim_ref[pl.ds(h, 16, stride=channels), :]
    turned = swap(base)
    power = jnp.concatenate(
        [base * fre[i : i + 1] + turned * fim[i : i + 1] for i in range(16)], axis=0
    )
    return power


def reversed_tables(h, base_ref, fre_ref, fim_ref, channels):
    base = jnp.concatenate(
        [base_ref[pl.ds(h + k * channels, 1), :] for k in range(7, -1, -1)], axis=0
    )
    fre = fre_ref[pl.ds(h, 16, stride=channels), :]
    fim = fim_ref[pl.ds(h, 16, stride=channels), :]
    turned = swap(base)
    return jnp.concatenate(
        [base * fre[i : i + 1] + turned * fim[i : i + 1] for i in range(15, -1, -1)], axis=0
    )


def doc_masks(seg_ref, mask_ref, row, pitch, chunks, docs):
    even = seg_ref[pl.ds(row, chunks, stride=2 * pitch), :]
    odd = seg_ref[pl.ds(row + pitch, chunks, stride=2 * pitch), :]
    pair = join(even, odd)
    for d in range(docs):
        for c in range(2):
            mask_ref[d * 2 + c] = jnp.where(pair[c] == float(d), 1.0, 0.0)


def join(even, odd):
    low = low_lanes(even.shape)
    return jnp.where(low, even, swap(odd)), jnp.where(low, swap(even), odd)


def spread(pair, mask_ref, docs):
    return jnp.concatenate(
        [pair[c] * mask_ref[d * 2 + c] for d in range(docs) for c in range(2)], axis=0
    )


def gathered(rows, mask_ref, chunks, docs):
    out = []
    for c in range(2):
        total = None
        for d in range(docs):
            at = (d * 2 + c) * chunks
            term = rows[at : at + chunks] * mask_ref[d * 2 + c]
            total = term if total is None else total + term
        out.append(total)
    return out


def scan_factors(h, fre_ref, fim_ref, channels, chunks, steps, backward):
    at = lax.broadcasted_iota(jnp.int32, (chunks, LANES), 0)
    out = []
    for s in range(steps):
        keep = at < chunks - (1 << s) if backward else at >= (1 << s)
        fre = fre_ref[pl.ds(h + (16 + s) * channels, 1), :]
        fim = fim_ref[pl.ds(h + (16 + s) * channels, 1), :]
        out.append((jnp.where(keep, fre, 0.0), jnp.where(keep, fim, 0.0)))
    return out


def scan_chunks(rows, factors, chunks, backward):
    at = lax.broadcasted_iota(jnp.int32, (chunks, LANES), 0)
    keep = at < chunks - 1 if backward else at >= 1
    out = []
    for i in range(rows.shape[0] // chunks):
        part = rows[i * chunks : (i + 1) * chunks]
        for s, factor in enumerate(factors):
            moved = pltpu.roll(part, chunks - (1 << s) if backward else 1 << s, 0)
            part = part + times(moved, factor)
        moved = pltpu.roll(part, chunks - 1 if backward else 1, 0)
        out.append(jnp.where(keep, moved, 0.0))
    return jnp.concatenate(out, axis=0)


def toeplitz(row):
    wide = jnp.broadcast_to(row, (LANES, LANES))
    wide = pltpu.roll(wide, 0, 1, stride=1, stride_axis=0)
    j = lax.broadcasted_iota(jnp.int32, (LANES, LANES), 0)
    t = lax.broadcasted_iota(jnp.int32, (LANES, LANES), 1)
    return jnp.where(t >= j, wide, 0.0)


def lag_sums(table):
    out = None
    j = lax.broadcasted_iota(jnp.int32, (8, LANES), 0)
    t = lax.broadcasted_iota(jnp.int32, (8, LANES), 1)
    for i in range(16):
        part = jnp.where(t >= j + 8 * i, table[8 * i : 8 * i + 8], 0.0)
        if i:
            part = pltpu.roll(part, LANES - 8 * i, 1)
        out = part if out is None else out + part
    for bit in (1, 2, 4):
        out = jnp.where((j & bit) != 0, pltpu.roll(out, LANES - bit, 1), out)
    return jnp.sum(out, axis=0, keepdims=True)


def wide_rows(row):
    return jnp.broadcast_to(row, (8, LANES))


def forward_kernel(
    sizes, recv_ref, lam_ref, weight_ref, skip_ref, out_ref, enter_ref, lag_ref,
    base_ref, fre_ref, fim_ref, mask_ref,
):
    channels, chunks, docs, steps, pitch, unroll = sizes
    power_setup(lam_ref[...], base_ref, fre_ref, fim_ref, steps, channels)
    doc_masks(recv_ref, mask_ref, channels, pitch, chunks, docs)

    def one(h):
        pair = join(
            recv_ref[pl.ds(h, chunks, stride=2 * pitch), :],
            recv_ref[pl.ds(h + pitch, chunks, stride=2 * pitch), :],
        )
        rows = halves(spread(pair, mask_ref, docs))
        power = halves(power_tables(h, base_ref, fre_ref, fim_ref, channels))
        back = halves(reversed_tables(h, base_ref, fre_ref, fim_ref, channels))
        weight = weight_ref[pl.ds(h, 1), :]
        low = low_lanes((1, LANES))
        lags = mm(halves(wide_rows(jnp.where(low, weight, -weight))), power, NT)[0:1]
        lag_ref[pl.ds(h, 1), :] = lags
        table = halves(toeplitz(lags))
        local = mm(rows, back, NN)
        enter = scan_chunks(
            local, scan_factors(h, fre_ref, fim_ref, channels, chunks, steps, False), chunks, False
        )
        enter_ref[h] = enter
        lam = as_factor(lam_ref[pl.ds(h, 1), :])
        coef = as_factor(times(weight, lam))
        ready = times(enter, coef)
        ready = jnp.where(low_lanes(ready.shape), ready, -ready)
        mixed = mm(rows, table, NN) + mm(halves(ready), power, NT)
        first, second = gathered(mixed, mask_ref, chunks, docs)
        skip = skip_ref[pl.ds(h, 1), :]
        first = first + skip * pair[0]
        second = second + skip * pair[1]
        even, odd = join(first, second)
        out_ref[pl.ds(h, chunks, stride=2 * channels), :] = even
        out_ref[pl.ds(h + channels, chunks, stride=2 * channels), :] = odd

    def several(i, carry):
        for k in range(unroll):
            one(i * unroll + k)
        return carry

    lax.fori_loop(0, channels // unroll, several, 0)


def backward_kernel(
    sizes, recv_ref, grad_ref, enter_ref, lag_ref, lam_ref, weight_ref, skip_ref, gain_ref, bias_ref,
    out_ref, sum_ref, first_ref, skipg_ref, gaing_ref, biasg_ref,
    base_ref, fre_ref, fim_ref, mask_ref,
):
    channels, chunks, docs, steps, pitch, unroll = sizes
    power_setup(lam_ref[...], base_ref, fre_ref, fim_ref, steps, channels)
    doc_masks(recv_ref, mask_ref, channels, pitch, chunks, docs)
    lag = lax.broadcasted_iota(jnp.int32, (LANES, LANES), 0).astype(F32)

    def one(h):
        pair = join(
            recv_ref[pl.ds(h, chunks, stride=2 * pitch), :],
            recv_ref[pl.ds(h + pitch, chunks, stride=2 * pitch), :],
        )
        gpair = join(
            grad_ref[pl.ds(h, chunks, stride=2 * channels), :],
            grad_ref[pl.ds(h + channels, chunks, stride=2 * channels), :],
        )
        rows = halves(spread(pair, mask_ref, docs))
        grows = halves(spread(gpair, mask_ref, docs))
        power32 = power_tables(h, base_ref, fre_ref, fim_ref, channels)
        back32 = reversed_tables(h, base_ref, fre_ref, fim_ref, channels)
        power, power1 = halves(power32), halves(power32 * lag)
        back, back1 = halves(back32), halves(back32 * (LANES - 1.0 - lag))
        weight = weight_ref[pl.ds(h, 1), :]
        lam = as_factor(lam_ref[pl.ds(h, 1), :])
        table = halves(toeplitz(lag_ref[pl.ds(h, 1), :]))
        enter = enter_ref[h]
        ahead = scan_factors(h, fre_ref, fim_ref, channels, chunks, steps, False)
        astern = scan_factors(h, fre_ref, fim_ref, channels, chunks, steps, True)
        hop = (
            fre_ref[pl.ds(h + 16 * channels, 1), :] * float(LANES),
            fim_ref[pl.ds(h + 16 * channels, 1), :] * float(LANES),
        )
        enter1 = scan_chunks(mm(rows, back1, NN) + times(enter, hop), ahead, chunks, False)
        seen = mm(grows, power, NN)
        seen1 = times(seen + mm(grows, power1, NN), lam)
        seen = times(seen, lam)
        seen_f = as_factor(seen)
        total = times(enter, seen_f)
        total1 = times(enter1, seen_f) + times(enter, as_factor(seen1))
        lags = halves(wide_rows(lag_sums(mm(rows, grows, TN))))
        sums = jnp.sum(total, axis=0, keepdims=True) + mm(lags, power, NN)[0:1]
        sums1 = jnp.sum(total1, axis=0, keepdims=True) + mm(lags, power1, NN)[0:1]
        sum_ref[pl.ds(h, 1), :] = sums
        first_ref[pl.ds(h, 1), :] = sums1
        leave = scan_chunks(times(seen, as_factor(weight)), astern, chunks, True)
        leave = jnp.where(low_lanes(leave.shape), leave, -leave)
        inner = mm(grows, table, NT) + mm(halves(leave), back, NT)
        gfirst, gsecond = gathered(inner, mask_ref, chunks, docs)
        skip = skip_ref[pl.ds(h, 1), :]
        gfirst = gfirst + skip * gpair[0]
        gsecond = gsecond + skip * gpair[1]
        even, odd = join(gfirst, gsecond)
        out_ref[pl.ds(h, chunks, stride=2 * channels), :] = even
        out_ref[pl.ds(h + channels, chunks, stride=2 * channels), :] = odd
        gain = gain_ref[pl.ds(h, 1), :]
        bias = bias_ref[pl.ds(h, 1), :]
        skipg_ref[pl.ds(h, 1), :] = jnp.sum(gpair[0] * pair[0] + gpair[1] * pair[1], axis=0, keepdims=True)
        biasg_ref[pl.ds(h, 1), :] = jnp.sum(gfirst + gsecond, axis=0, keepdims=True)
        gaing_ref[pl.ds(h, 1), :] = jnp.sum(
            gfirst * ((pair[0] - bias) / gain) + gsecond * ((pair[1] - bias) / gain), axis=0, keepdims=True
        )

    def several(i, carry):
        for k in range(unroll):
            one(i * unroll + k)
        return carry

    lax.fori_loop(0, channels // unroll, several, 0)


def kernel_sizes(recv_rows, channels, pieces, docs, unroll):
    chunks = pieces // 2
    steps = max(1, (chunks - 1).bit_length())
    return (channels, chunks, docs, steps, channels + 8, unroll)


def scratch(channels, chunks, docs, steps):
    return [
        pltpu.VMEM((8 * channels, LANES), F32),
        pltpu.VMEM(((16 + steps) * channels, LANES), F32),
        pltpu.VMEM(((16 + steps) * channels, LANES), F32),
        pltpu.VMEM((docs * 2, chunks, LANES), F32),
    ]


def recurrence(recv, lam, weight, skip, pieces, docs, unroll=2):
    channels = lam.shape[0]
    sizes = kernel_sizes(recv.shape[0], channels, pieces, docs, unroll)
    chunks, steps = sizes[1], sizes[3]
    rows = docs * 2 * chunks
    return pl.pallas_call(
        lambda *refs: forward_kernel(sizes, *refs),
        out_shape=(
            jax.ShapeDtypeStruct((pieces * channels, LANES), F32),
            jax.ShapeDtypeStruct((channels, rows, LANES), F32),
            jax.ShapeDtypeStruct((channels, LANES), F32),
        ),
        scratch_shapes=scratch(channels, chunks, docs, steps),
        compiler_params=pltpu.CompilerParams(vmem_limit_bytes=48 << 20),
        name="recurrence",
    )(recv, lam, weight, skip)


def recurrence_back(recv, grad, enter, lags, lam, weight, skip, gain, bias, pieces, docs, unroll=2):
    channels = lam.shape[0]
    sizes = kernel_sizes(recv.shape[0], channels, pieces, docs, unroll)
    chunks, steps = sizes[1], sizes[3]
    row = jax.ShapeDtypeStruct((channels, LANES), F32)
    return pl.pallas_call(
        lambda *refs: backward_kernel(sizes, *refs),
        out_shape=(jax.ShapeDtypeStruct((pieces * channels, LANES), F32), row, row, row, row, row),
        scratch_shapes=scratch(channels, chunks, docs, steps),
        compiler_params=pltpu.CompilerParams(vmem_limit_bytes=48 << 20),
        name="recurrence_back",
    )(recv, grad, enter, lags, lam, weight, skip, gain, bias)


EPSILON = 1e-05


def layer_norm(values, norm_gain, norm_shift):
    centre = values - jnp.mean(values, axis=-1, keepdims=True)
    spread_of = jnp.mean(centre * centre, axis=-1, keepdims=True)
    return centre * lax.rsqrt(spread_of + EPSILON) * norm_gain + norm_shift


def gelu_exact(values):
    return jax.nn.gelu(values, approximate=False)


def gated_unit(values):
    middle = values.shape[-1] // 2
    return values[..., :middle] * jax.nn.sigmoid(values[..., middle:])


def inner_rows(left, right):
    return lax.dot_general(left, right, TN, preferred_element_type=F32)


def outer_cols(left, right):
    return lax.dot_general(left, right, NT, preferred_element_type=F32)


def flipped(value, axis, bit):
    count = lax.axis_size(axis)
    return lax.ppermute(value, axis, [(i, i ^ bit) for i in range(count)])


def summed(value, axes):
    for axis in axes:
        bit = 1
        while bit < lax.axis_size(axis):
            value = value + flipped(value, axis, bit)
            bit *= 2
    return value


def mode_parts(params):
    decay_log, decay_freq, input_re, input_im, output_re, output_im, step_log = params
    step_size = jnp.exp(step_log)[:, None]
    real_part = -jnp.exp(decay_log)
    delta_re = step_size * real_part
    delta_im = step_size * decay_freq
    magnitude = jnp.exp(delta_re)
    lam_re, lam_im = (magnitude * jnp.cos(delta_im), magnitude * jnp.sin(delta_im))
    denominator = real_part * real_part + decay_freq * decay_freq
    num_re = lam_re - 1.0
    rat_re = (num_re * real_part + lam_im * decay_freq) / denominator
    rat_im = (lam_im * real_part - num_re * decay_freq) / denominator
    bbar_re = rat_re * input_re - rat_im * input_im
    bbar_im = rat_re * input_im + rat_im * input_re
    prod_re = 2.0 * (output_re * bbar_re - output_im * bbar_im)
    prod_im = 2.0 * (output_re * bbar_im + output_im * bbar_re)
    return (delta_re, delta_im, prod_re, prod_im), (lam_re, lam_im)


def packed(real, imag):
    return jnp.concatenate([real, imag], axis=1)


def on_device(
    tokens, segments, norm1_gain, norm1_bias, decay_log, decay_freq, input_re, input_im,
    output_re, output_im, step_log, skip_gain, glu_weight, glu_bias, norm2_gain, norm2_bias,
    ffn_in, ffn_in_bias, ffn_out, ffn_out_bias, cotangent,
):
    contexts, piece_len, features = tokens.shape
    rows = contexts * piece_len
    pieces, mine = lax.axis_size("seq"), lax.axis_index("seq")
    channels = features // pieces
    docs = max(1, pieces * piece_len // 256)
    params = (decay_log, decay_freq, input_re, input_im, output_re, output_im, step_log)

    def own(value):
        return lax.dynamic_slice_in_dim(value, mine * channels, channels, 0)

    def row_of(value):
        return jnp.broadcast_to(own(value)[:, None], (channels, LANES))

    parts, lam_pair = mode_parts(tuple(own(p) for p in params))
    lam, weight = packed(*lam_pair), packed(parts[2], parts[3])
    skip = row_of(skip_gain)

    floats = tokens.astype(F32).reshape(rows, features)
    centre = floats - jnp.mean(floats, axis=-1, keepdims=True)
    recip1 = lax.rsqrt(jnp.mean(centre * centre, axis=-1, keepdims=True) + EPSILON)
    unit1 = centre * recip1
    normed = unit1 * norm1_gain + norm1_bias
    turned = normed.T.reshape(pieces, channels, rows)
    seg_rows = jnp.broadcast_to(segments.astype(F32).reshape(1, 1, rows), (pieces, 8, rows))
    recv = lax.all_to_all(jnp.concatenate([turned, seg_rows], axis=1), "seq", 0, 0)
    recv = recv.reshape(pieces * (channels + 8), rows)
    mixed_rows, enter, lags = recurrence(recv, lam, weight, skip, pieces, docs, FORWARD_UNROLL)
    mixed = lax.all_to_all(mixed_rows.reshape(pieces, channels, rows), "seq", 0, 0)
    mixed = mixed.reshape(features, rows).T

    activation, gelu1_pull = jax.vjp(gelu_exact, mixed)
    flat_act = activation.astype(BF16)
    glu_pre = jnp.dot(flat_act, glu_weight, preferred_element_type=F32) + glu_bias
    glu_out, glu_pull = jax.vjp(gated_unit, glu_pre)
    hidden = floats + glu_out
    normed_two, norm2_pull = jax.vjp(layer_norm, hidden, norm2_gain, norm2_bias)
    norm2_low = normed_two.astype(BF16)
    ffn_pre = jnp.dot(norm2_low, ffn_in, preferred_element_type=F32) + ffn_in_bias
    ffn_act, gelu2_pull = jax.vjp(gelu_exact, ffn_pre)
    ffn_low = ffn_act.astype(BF16)
    ffn_res = jnp.dot(ffn_low, ffn_out, preferred_element_type=F32) + ffn_out_bias
    result = (hidden + ffn_res).astype(BF16).reshape(tokens.shape)
    up_low = cotangent.reshape(rows, features)
    upstream = up_low.astype(F32)
    grad_ffn_low = outer_cols(up_low, ffn_out)
    term_out = inner_rows(ffn_low, up_low)
    bias_out = jnp.sum(upstream, axis=0)
    pre_low = gelu2_pull(grad_ffn_low)[0].astype(BF16)
    grad_normed_two = outer_cols(pre_low, ffn_in)
    term_in = inner_rows(norm2_low, pre_low)
    bias_in = jnp.sum(pre_low.astype(F32), axis=0)
    hidden_part, grad_g2, grad_b2 = norm2_pull(grad_normed_two)
    grad_hidden = upstream + hidden_part
    glu_low = glu_pull(grad_hidden)[0].astype(BF16)
    grad_act = outer_cols(glu_low, glu_weight)
    term_glu = inner_rows(flat_act, glu_low)
    bias_glu = jnp.sum(glu_low.astype(F32), axis=0)
    grad_mixed = gelu1_pull(grad_act)[0]

    back = lax.all_to_all(grad_mixed.T.reshape(pieces, channels, rows), "seq", 0, 0)
    grad_rows, sums, firsts, part_skip, part_gain, part_bias = recurrence_back(
        recv, back.reshape(pieces * channels, rows), enter, lags, lam, weight, skip,
        row_of(norm1_gain), row_of(norm1_bias), pieces, docs, BACKWARD_UNROLL,
    )
    grad_normed = lax.all_to_all(grad_rows.reshape(pieces, channels, rows), "seq", 0, 0)
    grad_normed = grad_normed.reshape(features, rows).T
    scaled = grad_normed * norm1_gain
    token_part = recip1 * (
        scaled
        - jnp.mean(scaled, axis=-1, keepdims=True)
        - unit1 * jnp.mean(scaled * unit1, axis=-1, keepdims=True)
    )
    grad_tokens = (grad_hidden + token_part).astype(BF16).reshape(tokens.shape)

    vectors = jnp.stack([jnp.sum(v, axis=1) for v in (part_skip, part_gain, part_bias)], axis=1)
    vectors = jnp.pad(vectors, ((0, 0), (0, LANES - vectors.shape[1])))
    state = summed(jnp.concatenate([sums, firsts, vectors], axis=1), ("batch",))
    state = lax.all_to_all(jnp.broadcast_to(state[None], (pieces,) + state.shape), "seq", 0, 0)
    state = state.reshape(features, state.shape[2])
    half = LANES // 2
    m_re, m_im = state[:, :half], state[:, half:LANES]
    f_re, f_im = state[:, LANES : LANES + half], state[:, LANES + half : 2 * LANES]
    whole_parts, mode_pull = jax.vjp(lambda p: mode_parts(p)[0], params)
    w_re, w_im = whole_parts[2], whole_parts[3]
    grad_params = mode_pull(
        (w_re * f_re - w_im * f_im, -(w_re * f_im + w_im * f_re), m_re, -m_im)
    )[0]
    vectors = state[:, 2 * LANES : 2 * LANES + 3]
    small = summed(
        jnp.concatenate([bias_glu, grad_g2, grad_b2, bias_in, bias_out]).reshape(-1, LANES),
        ("seq", "batch"),
    ).reshape(-1)
    bias_glu, grad_g2, grad_b2, bias_in, bias_out = jnp.split(
        small, [2 * features, 3 * features, 4 * features, small.shape[0] - features]
    )
    row_sums = tuple(
        summed(lax.psum_scatter(term, "seq", scatter_dimension=0, tiled=True), ("batch",))
        for term in (term_out, term_in, term_glu)
    )
    return (
        result, grad_tokens, vectors[:, 1], vectors[:, 2], *grad_params, vectors[:, 0],
        row_sums[2], bias_glu, grad_g2, grad_b2, row_sums[1], bias_in, row_sums[0], bias_out,
    )


def solution(mesh):
    spread_over = P("batch", "seq", None)
    in_specs = (spread_over, P("batch", "seq")) + (P(),) * 18 + (spread_over,)
    rows = P("seq", None)
    out_specs = (spread_over,) * 2 + (P(),) * 10 + (rows,) + (P(),) * 3 + (rows, P(), rows, P())
    return jax.shard_map(
        on_device, mesh=mesh, in_specs=in_specs, out_specs=out_specs, check_vma=False
    )
```

```python
import jax, jax.numpy as jnp
from jax import lax
from jax.sharding import PartitionSpec as P
from jax.experimental import pallas as pl
from jax.experimental.pallas import tpu as pltpu
F32, BF16 = jnp.float32, jnp.bfloat16
LANES = 128
HALF = 64
FORWARD_UNROLL = 16
BACKWARD_UNROLL = 8
NN = (((1,), (0,)), ((), ()))
NT = (((1,), (1,)), ((), ()))
TN = (((0,), (0,)), ((), ()))


def halves(value):
    high = value.astype(BF16)
    return high, (value - high.astype(F32)).astype(BF16)


def dot(left, right, dims):
    return lax.dot_general(left, right, dims, preferred_element_type=F32)


def beside(parts):
    return jnp.concatenate(parts, axis=1)


def below(parts):
    return jnp.concatenate(parts, axis=0)


def mm(left, right):
    table = beside(right)
    out = dot(beside(left), below([table, table]), NN)
    return out[:, :LANES] + out[:, LANES:]


def mm_turned(left, right):
    out = dot(beside(left), below([beside([right[0]] * 2), beside([right[1]] * 2)]), NT)
    return out[:, :LANES] + out[:, LANES:]


def swap(value):
    return pltpu.roll(value, HALF, value.ndim - 1)


def low_lanes(shape):
    return lax.broadcasted_iota(jnp.int32, shape, len(shape) - 1) < HALF


def as_factor(value):
    turned = swap(value)
    low = low_lanes(value.shape)
    return jnp.where(low, value, turned), jnp.where(low, -turned, value)


def times(value, factor):
    return value * factor[0] + swap(value) * factor[1]


def power_setup(lam, base_ref, fre_ref, fim_ref, steps, channels):
    one = jnp.where(low_lanes(lam.shape), 1.0, 0.0)
    factor = as_factor(lam)
    row = one
    for k in range(8):
        base_ref[pl.ds(k * channels, channels), :] = row
        row = times(row, factor)
    eight = as_factor(row)
    row = one
    for i in range(16):
        fre, fim = as_factor(row)
        fre_ref[pl.ds(i * channels, channels), :] = fre
        fim_ref[pl.ds(i * channels, channels), :] = fim
        row = times(row, eight)
    for s in range(steps):
        fre, fim = as_factor(row)
        fre_ref[pl.ds((16 + s) * channels, channels), :] = fre
        fim_ref[pl.ds((16 + s) * channels, channels), :] = fim
        row = times(row, (fre, fim))


def power_tables(h, base_ref, fre_ref, fim_ref, channels):
    base = base_ref[pl.ds(h, 8, stride=channels), :]
    turned = swap(base)
    return below([
        base * fre_ref[pl.ds(h + i * channels, 1), :] + turned * fim_ref[pl.ds(h + i * channels, 1), :]
        for i in range(16)
    ])


def reversed_tables(h, base_ref, fre_ref, fim_ref, channels):
    base = below([base_ref[pl.ds(h + k * channels, 1), :] for k in range(7, -1, -1)])
    turned = swap(base)
    return below([
        base * fre_ref[pl.ds(h + i * channels, 1), :] + turned * fim_ref[pl.ds(h + i * channels, 1), :]
        for i in range(15, -1, -1)
    ])


def doc_masks(seg_ref, mask_ref, row, pitch, chunks, docs, turn):
    even = seg_ref[pl.ds(row, chunks, stride=2 * pitch), :]
    odd = seg_ref[pl.ds(row + pitch, chunks, stride=2 * pitch), :]
    pair = join(even, odd)
    at = lax.broadcasted_iota(jnp.int32, (LANES, LANES), 0)
    to = lax.broadcasted_iota(jnp.int32, (LANES, LANES), 1)
    turning = jnp.where(at + to == LANES - 1, 1.0, 0.0).astype(BF16)
    for d in range(docs):
        for c in range(2):
            mask = jnp.where(pair[c] == float(d), 1.0, 0.0)
            mask_ref[d * 2 + c] = mask
            if turn:
                mask_ref[(docs + d) * 2 + c] = dot(mask.astype(BF16), turning, NN)


def join(even, odd):
    low = low_lanes(even.shape)
    return jnp.where(low, even, swap(odd)), jnp.where(low, swap(even), odd)


def join_turned(even, odd):
    low = low_lanes(even.shape)
    return jnp.where(low, swap(odd), even), jnp.where(low, odd, swap(even))


def apart_turned(first, second):
    low = low_lanes(first.shape)
    return jnp.where(low, swap(second), first), jnp.where(low, second, swap(first))


def spread(pair, mask_ref, docs, base=0):
    return below([pair[c] * mask_ref[base + d * 2 + c] for d in range(docs) for c in range(2)])


def gathered(rows, mask_ref, chunks, docs, base=0):
    out = []
    for c in range(2):
        total = None
        for d in range(docs):
            at = (d * 2 + c) * chunks
            term = rows[at : at + chunks] * mask_ref[base + d * 2 + c]
            total = term if total is None else total + term
        out.append(total)
    return out


def scan_factors(h, fre_ref, fim_ref, channels, chunks, steps, backward):
    at = lax.broadcasted_iota(jnp.int32, (chunks, LANES), 0)
    out = []
    for s in range(steps):
        keep = at < chunks - (1 << s) if backward else at >= (1 << s)
        fre = fre_ref[pl.ds(h + (16 + s) * channels, 1), :]
        fim = fim_ref[pl.ds(h + (16 + s) * channels, 1), :]
        out.append((jnp.where(keep, fre, 0.0), jnp.where(keep, fim, 0.0)))
    return out


def scan_chunks(rows, factors, chunks, backward):
    at = lax.broadcasted_iota(jnp.int32, (chunks, LANES), 0)
    keep = at < chunks - 1 if backward else at >= 1
    out = []
    for i in range(rows.shape[0] // chunks):
        part = rows[i * chunks : (i + 1) * chunks]
        for s, factor in enumerate(factors):
            moved = pltpu.roll(part, chunks - (1 << s) if backward else 1 << s, 0)
            part = part + times(moved, factor)
        moved = pltpu.roll(part, chunks - 1 if backward else 1, 0)
        out.append(jnp.where(keep, moved, 0.0))
    return jnp.concatenate(out, axis=0)


def toeplitz(row):
    wide = jnp.broadcast_to(row, (LANES, LANES))
    wide = pltpu.roll(wide, 0, 1, stride=1, stride_axis=0)
    j = lax.broadcasted_iota(jnp.int32, (LANES, LANES), 0)
    t = lax.broadcasted_iota(jnp.int32, (LANES, LANES), 1)
    return jnp.where(t >= j, wide, 0.0)


def turned_lag_sums(table):
    moved = pltpu.roll(table, 0, 1, stride=1, stride_axis=0)
    at = lax.broadcasted_iota(jnp.int32, (LANES, LANES), 0)
    lane = lax.broadcasted_iota(jnp.int32, (LANES, LANES), 1)
    return jnp.sum(jnp.where(lane >= at, moved, 0.0), axis=0, keepdims=True)


def together(works):
    while works:
        works = [work for work in works if next(work, None)]


def first_rows(first, second):
    at = lax.broadcasted_iota(jnp.int32, (8, LANES), 0)
    return jnp.where(at == 0, first, jnp.where(at == 1, second, 0.0))


def forward_kernel(
    sizes, recv_ref, lam_ref, weight_ref, skip_ref, out_ref, enter_ref, lag_ref,
    base_ref, fre_ref, fim_ref, mask_ref,
):
    channels, chunks, docs, steps, pitch, unroll = sizes
    rows = docs * 2 * chunks
    power_setup(lam_ref[...], base_ref, fre_ref, fim_ref, steps, channels)
    doc_masks(recv_ref, mask_ref, channels, pitch, chunks, docs, False)

    def one(h):
        pair = join(
            recv_ref[pl.ds(h, chunks, stride=2 * pitch), :],
            recv_ref[pl.ds(h + pitch, chunks, stride=2 * pitch), :],
        )
        inputs = halves(spread(pair, mask_ref, docs))
        power = halves(power_tables(h, base_ref, fre_ref, fim_ref, channels))
        yield True
        back = halves(reversed_tables(h, base_ref, fre_ref, fim_ref, channels))
        weight = weight_ref[pl.ds(h, 1), :]
        low = low_lanes((1, LANES))
        signed = halves(jnp.where(low, weight, -weight))
        both = first_rows(signed[0].astype(F32), signed[1].astype(F32)).astype(BF16)
        yield True
        lags = dot(both, below(power), NT)
        lags = lags[0:1] + lags[1:2]
        lags = lags[:, :LANES] + lags[:, LANES:]
        lag_ref[pl.ds(h, 1), :] = lags
        yield True
        table = halves(toeplitz(lags))
        yield True
        out = dot(below(inputs), beside([back[0], table[0]]), NN)
        out = out[:rows] + out[rows:] + dot(inputs[0], beside([back[1], table[1]]), NN)
        yield True
        enter = scan_chunks(
            out[:, :LANES], scan_factors(h, fre_ref, fim_ref, channels, chunks, steps, False), chunks, False
        )
        enter_ref[h] = enter
        yield True
        lam = as_factor(lam_ref[pl.ds(h, 1), :])
        coef = as_factor(times(weight, lam))
        coef = (jnp.where(low, coef[0], -coef[0]), jnp.where(low, coef[1], -coef[1]))
        yield True
        mixed = out[:, LANES:] + mm_turned(halves(times(enter, coef)), power)
        yield True
        first, second = gathered(mixed, mask_ref, chunks, docs)
        skip = skip_ref[pl.ds(h, 1), :]
        even, odd = join(first + skip * pair[0], second + skip * pair[1])
        out_ref[pl.ds(h, chunks, stride=2 * channels), :] = even
        out_ref[pl.ds(h + channels, chunks, stride=2 * channels), :] = odd

    def several(i, carry):
        together([one(i * unroll + k) for k in range(unroll)])
        return carry

    lax.fori_loop(0, channels // unroll, several, 0)


def backward_kernel(
    sizes, recv_ref, grad_ref, enter_ref, lag_ref, lam_ref, weight_ref, skip_ref,
    out_ref, sum_ref, first_ref, lagsum_ref, bias_ref,
    base_ref, fre_ref, fim_ref, mask_ref,
):
    channels, chunks, docs, steps, pitch, unroll = sizes
    rows = docs * 2 * chunks
    power_setup(lam_ref[...], base_ref, fre_ref, fim_ref, steps, channels)
    doc_masks(recv_ref, mask_ref, channels, pitch, chunks, docs, True)
    reach = (LANES - 1 - lax.broadcasted_iota(jnp.int32, (1, LANES), 1)).astype(F32)

    def one(h):
        pair = join(
            recv_ref[pl.ds(h, chunks, stride=2 * pitch), :],
            recv_ref[pl.ds(h + pitch, chunks, stride=2 * pitch), :],
        )
        gpair = join_turned(
            grad_ref[pl.ds(h, chunks, stride=2 * channels), :],
            grad_ref[pl.ds(h + channels, chunks, stride=2 * channels), :],
        )
        inputs = spread(pair, mask_ref, docs)
        grads = spread(gpair, mask_ref, docs, docs * 2)
        ih, il = halves(inputs)
        gh, gl = halves(grads)
        yield True
        lagsum = turned_lag_sums(dot(below([gh, gl, gh]), below([ih, ih, il]), TN))
        lagsum_ref[pl.ds(h, 1), :] = lagsum
        yield True
        power = halves(power_tables(h, base_ref, fre_ref, fim_ref, channels))
        yield True
        back = halves(reversed_tables(h, base_ref, fre_ref, fim_ref, channels))
        weight = weight_ref[pl.ds(h, 1), :]
        lam = as_factor(lam_ref[pl.ds(h, 1), :])
        yield True
        table = halves(toeplitz(lag_ref[pl.ds(h, 1), :]))
        yield True
        enter = enter_ref[h]
        ahead = scan_factors(h, fre_ref, fim_ref, channels, chunks, steps, False)
        astern = scan_factors(h, fre_ref, fim_ref, channels, chunks, steps, True)
        i1h, i1l = halves(inputs * reach)
        g1h, g1l = halves(grads * reach)
        lh, ll = halves(first_rows(lagsum, lagsum * reach))
        yield True
        out = mm((below([i1h, gh, g1h, lh]), below([i1l, gl, g1l, ll])), back)
        yield True
        hop = (
            fre_ref[pl.ds(h + 16 * channels, 1), :] * float(LANES),
            fim_ref[pl.ds(h + 16 * channels, 1), :] * float(LANES),
        )
        turned = swap(enter)
        enter1 = scan_chunks(
            out[:rows] + enter * hop[0] + turned * hop[1], ahead, chunks, False
        )
        yield True
        seen = out[rows : 2 * rows]
        seen1 = seen + out[2 * rows : 3 * rows]
        seen_t = swap(seen)

        def summed_product(plain, crossed):
            plain = jnp.sum(plain, axis=0, keepdims=True)
            crossed = jnp.sum(crossed, axis=0, keepdims=True)
            low = low_lanes((1, LANES))
            plain, crossed = plain - swap(plain), crossed + swap(crossed)
            return times(jnp.where(low, plain, crossed), lam)

        sum_ref[pl.ds(h, 1), :] = (
            summed_product(enter * seen, turned * seen) + out[3 * rows : 3 * rows + 1]
        )
        first_ref[pl.ds(h, 1), :] = summed_product(
            enter1 * seen + enter * seen1, enter1 * seen_t + turned * seen1
        ) + out[3 * rows + 1 : 3 * rows + 2]
        yield True
        coef = as_factor(times(weight, lam))
        leave = scan_chunks(seen * coef[0] + seen_t * coef[1], astern, chunks, True)
        leave = jnp.where(low_lanes(leave.shape), leave, -leave)
        yield True
        inner = mm((gh, gl), table) + mm_turned(halves(leave), power)
        yield True
        gfirst, gsecond = gathered(inner, mask_ref, chunks, docs, docs * 2)
        skip = skip_ref[pl.ds(h, 1), :]
        gfirst = gfirst + skip * gpair[0]
        gsecond = gsecond + skip * gpair[1]
        bias_ref[pl.ds(h, 1), :] = jnp.sum(gfirst + gsecond, axis=0, keepdims=True)
        even, odd = apart_turned(gfirst, gsecond)
        out_ref[pl.ds(h, chunks, stride=2 * channels), :] = even
        out_ref[pl.ds(h + channels, chunks, stride=2 * channels), :] = odd

    def several(i, carry):
        together([one(i * unroll + k) for k in range(unroll)])
        return carry

    lax.fori_loop(0, channels // unroll, several, 0)


REACH = 512


def kernel_sizes(recv_rows, channels, pieces, docs, unroll):
    chunks = pieces // 2
    unroll = min(channels, max(1, unroll * 64 // (docs * 2 * chunks)))
    steps = min((chunks - 1).bit_length(), (REACH // LANES - 1).bit_length())
    return (channels, chunks, docs, steps, channels + 8, unroll)


def scratch(channels, chunks, docs, steps):
    return [
        pltpu.VMEM((8 * channels, LANES), F32),
        pltpu.VMEM(((16 + steps) * channels, LANES), F32),
        pltpu.VMEM(((16 + steps) * channels, LANES), F32),
        pltpu.VMEM((docs * 4, chunks, LANES), F32),
    ]


def recurrence(recv, lam, weight, skip, pieces, docs, unroll=2):
    channels = lam.shape[0]
    sizes = kernel_sizes(recv.shape[0], channels, pieces, docs, unroll)
    chunks, steps = sizes[1], sizes[3]
    rows = docs * 2 * chunks
    return pl.pallas_call(
        lambda *refs: forward_kernel(sizes, *refs),
        out_shape=(
            jax.ShapeDtypeStruct((pieces * channels, LANES), F32),
            jax.ShapeDtypeStruct((channels, rows, LANES), F32),
            jax.ShapeDtypeStruct((channels, LANES), F32),
        ),
        scratch_shapes=scratch(channels, chunks, docs, steps),
        compiler_params=pltpu.CompilerParams(vmem_limit_bytes=48 << 20),
        cost_estimate=estimate(16),
        name="recurrence",
    )(recv, lam, weight, skip)


def recurrence_back(recv, grad, enter, lags, lam, weight, skip, pieces, docs, unroll=2):
    channels = lam.shape[0]
    sizes = kernel_sizes(recv.shape[0], channels, pieces, docs, unroll)
    chunks, steps = sizes[1], sizes[3]
    row = jax.ShapeDtypeStruct((channels, LANES), F32)
    return pl.pallas_call(
        lambda *refs: backward_kernel(sizes, *refs),
        out_shape=(jax.ShapeDtypeStruct((pieces * channels, LANES), F32), row, row, row, row),
        scratch_shapes=scratch(channels, chunks, docs, steps),
        compiler_params=pltpu.CompilerParams(vmem_limit_bytes=48 << 20),
        cost_estimate=estimate(30),
        name="recurrence_back",
    )(recv, grad, enter, lags, lam, weight, skip)


EPSILON = 1e-05
MIB = 1 << 20


def estimate(micros, moved=0):
    return pl.CostEstimate(flops=int(micros * 1e9), transcendentals=0, bytes_accessed=int(moved))


def bell(values):
    share = 0.5 + 0.5 * lax.erf(values * 0.7071067811865476)
    return share, values * jnp.exp(-0.5 * values * values) * 0.3989422804014327


def sent_rows(values, out_ref, channels):
    turned = values.T
    for s in range(out_ref.shape[0]):
        out_ref[s, 0:channels, :] = turned[s * channels : (s + 1) * channels]


def normalize(values):
    centre = values - jnp.mean(values, axis=1, keepdims=True)
    recip = lax.rsqrt(jnp.mean(centre * centre, axis=1, keepdims=True) + EPSILON)
    return centre * recip, recip


def norm_back(grad, unit, recip):
    return recip * (
        grad
        - jnp.mean(grad, axis=1, keepdims=True)
        - unit * jnp.mean(grad * unit, axis=1, keepdims=True)
    )


def turning(size):
    at = lax.broadcasted_iota(jnp.int32, (size, size), 0)
    to = lax.broadcasted_iota(jnp.int32, (size, size), 1)
    return jnp.where(at + to == size - 1, 1.0, 0.0).astype(BF16)


def first_kernel(tokens_ref, cot_ref, seg_ref, gain_ref, bias_ref, send_ref, up_ref):
    pieces, pitch, rows = send_ref.shape
    channels = pitch - 8
    unit, _ = normalize(tokens_ref[...].astype(F32))
    sent_rows(unit * gain_ref[...] + bias_ref[...], send_ref, channels)
    seg = jnp.broadcast_to(seg_ref[...].astype(F32), (8, rows))
    for s in range(pieces):
        send_ref[s, channels:pitch, :] = seg
    up_ref[...] = cot_ref[...].astype(F32)


def last_kernel(back_ref, tokens_ref, gain_ref, hidden_ref, out_ref):
    unit, recip = normalize(tokens_ref[...].astype(F32))
    turn = turning(tokens_ref.shape[0])
    high, low = halves(back_ref[...])
    grad = (dot(turn, high, NT) + dot(turn, low, NT)) * gain_ref[...]
    out_ref[...] = (hidden_ref[...] + norm_back(grad, unit, recip)).astype(BF16)


def fetch(source, target, sems, chunks, rows):
    out = []
    wide = source.shape[0 if rows else 1] // chunks
    for i in range(chunks):
        part = (pl.ds(i * wide, wide), slice(None)) if rows else (slice(None), pl.ds(i * wide, wide))
        copy = pltpu.make_async_copy(source.at[part], target.at[part], sems.at[i])
        copy.start()
        out.append(copy)
    return out


def by_core(values, place_ref, out_ref, at, pieces):
    wide = values.shape[1] // pieces
    for s in range(pieces):
        slot = (s % 2) ^ place_ref[0]
        out_ref[slot, at, :, (s // 2) * wide : (s // 2 + 1) * wide] = values[:, s * wide : (s + 1) * wide]


def upward_kernel(
    pieces, place_ref, mixed_ref, tokens_ref, glu_bias_ref, gain_ref, bias_ref, ffn_bias_ref, glu_ref, ffn_ref,
    acts_ref, keep_ref, pre_ref, hidden_ref, slope1_ref, slope2_ref, low_ref,
    glu_v, ffn_v, glu_sem, ffn_sem,
):
    rows, features = tokens_ref.shape
    glu_copies = fetch(glu_ref, glu_v, glu_sem, 4, False)
    ffn_copies = fetch(ffn_ref, ffn_v, ffn_sem, 8, False)
    mixed = mixed_ref[...].T
    share, steep = bell(mixed)
    slope1_ref[...] = share + steep
    act = (mixed * share).astype(BF16)
    by_core(act.astype(F32), place_ref, acts_ref, 0, pieces)
    wide = glu_ref.shape[1] // 4
    for i in range(4):
        glu_copies[i].wait()
        at = slice(i * wide, (i + 1) * wide)
        pre_ref[:, at] = (
            jnp.dot(act, glu_v[:, at], preferred_element_type=F32) + glu_bias_ref[:, at]
        )
    hidden = tokens_ref[...].astype(F32) + pre_ref[:, :features] * jax.nn.sigmoid(pre_ref[:, features:])
    hidden_ref[...] = hidden
    unit, _ = normalize(hidden)
    normed = (unit * gain_ref[...] + bias_ref[...]).astype(BF16)
    by_core(normed.astype(F32), place_ref, acts_ref, 1, pieces)
    wide = ffn_ref.shape[1] // 8
    block = ffn_ref.shape[1] // pieces // 2
    for i in range(8):
        ffn_copies[i].wait()
        at = slice(i * wide, (i + 1) * wide)
        ffn_pre = jnp.dot(normed, ffn_v[:, at], preferred_element_type=F32) + ffn_bias_ref[:, at]
        share, steep = bell(ffn_pre)
        slope2_ref[:, at] = share + steep
        low = (ffn_pre * share).astype(BF16)
        low_ref[:, at] = low
        wider = low.astype(F32)
        for k in range(wide // block):
            index = (i * wide) // block + k
            piece, half = index // 2, index % 2
            keep_ref[
                half ^ place_ref[1], (piece % 2) ^ place_ref[0], :,
                (piece // 2) * block : (piece // 2 + 1) * block,
            ] = wider[:, k * block : (k + 1) * block]


def downward_kernel(
    place_ref, cot_ref, slope2_ref, hidden_ref, pre_ref, slope1_ref, gain_ref, out_w_ref, in_w_ref, glu_w_ref,
    sent_pre_ref, sent_glu_ref, grad_hidden_ref, turned_ref, in_sum_ref, glu_sum_ref, gain_sum_ref,
    bias_sum_ref, out_sum_ref,
    out_v, in_v, glu_v, out_sem, in_sem, glu_sem,
):
    rows, features = cot_ref.shape
    inner = out_w_ref.shape[0]
    wide = inner // 8
    out_copies = fetch(out_w_ref, out_v, out_sem, 8, True)
    in_copies = fetch(in_w_ref, in_v, in_sem, 8, False)
    glu_copies = fetch(glu_w_ref, glu_v, glu_sem, 1, False)
    cot = cot_ref[...]
    up = cot.astype(F32)
    out_sum_ref[...] = jnp.sum(up, axis=0, keepdims=True)
    total = jnp.zeros((rows, features), F32)
    for i in range(8):
        at = slice(i * wide, (i + 1) * wide)
        out_copies[i].wait()
        grad = lax.dot_general(cot, out_v[at, :], NT, preferred_element_type=F32)
        low = (grad * slope2_ref[:, at]).astype(BF16)
        wider = low.astype(F32)
        in_sum_ref[:, at] = jnp.sum(wider, axis=0, keepdims=True)
        sent_pre_ref[(i // 4) ^ place_ref[1], :, (i % 4) * wide : (i % 4 + 1) * wide] = wider
        in_copies[i].wait()
        total = total + lax.dot_general(low, in_v[:, at], NT, preferred_element_type=F32)
    unit, recip = normalize(hidden_ref[...])
    gain_sum_ref[...] = jnp.sum(total * unit, axis=0, keepdims=True)
    bias_sum_ref[...] = jnp.sum(total, axis=0, keepdims=True)
    grad_hidden = up + norm_back(total * gain_ref[...], unit, recip)
    grad_hidden_ref[...] = grad_hidden
    gate = jax.nn.sigmoid(pre_ref[:, features:])
    first = (grad_hidden * gate).astype(BF16)
    second = (grad_hidden * pre_ref[:, :features] * (gate * (1.0 - gate))).astype(BF16)
    glu_copies[0].wait()
    grad_act = None
    for k, part in enumerate((first, second)):
        wider = part.astype(F32)
        at = slice(k * features, (k + 1) * features)
        glu_sum_ref[:, at] = jnp.sum(wider, axis=0, keepdims=True)
        sent_glu_ref[k ^ place_ref[1]] = wider
        term = lax.dot_general(part, glu_v[:, at], NT, preferred_element_type=F32)
        grad_act = term if grad_act is None else grad_act + term
    turn = turning(rows)
    high, low = halves(grad_act * slope1_ref[...])
    turned_ref[...] = (dot(turn, high, NN) + dot(turn, low, NN)).T


def product_kernel(count, place_ref, *refs):
    lefts, rights = refs[:count], refs[count : 2 * count]
    keep_ref, send_ref, scratch_ref = refs[2 * count :]
    total = None
    for left, right in zip(lefts, rights):
        term = lax.dot_general(
            left[...].astype(BF16), right[...].astype(BF16), TN, preferred_element_type=F32
        )
        total = term if total is None else total + term
    scratch_ref[...] = total
    height = keep_ref.shape[1]
    for i in range(keep_ref.shape[0]):
        for ref, other in ((keep_ref, 0), (send_ref, 1)):
            block = 2 * i + (place_ref[2] ^ other)
            ref[i] = scratch_ref[pl.ds(pl.multiple_of(block * height, 8), height), :]


SMEM = pl.BlockSpec(memory_space=pltpu.SMEM)
VMEM = pl.BlockSpec(memory_space=pltpu.VMEM)
ANY = pl.BlockSpec(memory_space=pl.ANY)


def shaped(*shape, dtype=F32):
    return jax.ShapeDtypeStruct(shape, dtype)


def params_of(mib):
    return pltpu.CompilerParams(vmem_limit_bytes=mib * MIB)


def first_norm(tokens, cot, seg, gain, bias, pieces):
    rows, features = tokens.shape
    return pl.pallas_call(
        first_kernel,
        out_shape=(shaped(pieces, features // pieces + 8, rows), shaped(rows, features)),
        compiler_params=params_of(16), cost_estimate=estimate(4), name="first_norm",
    )(tokens, cot, seg, gain, bias)


def last_norm(back, tokens, gain, grad_hidden):
    return pl.pallas_call(
        last_kernel, out_shape=shaped(*tokens.shape, dtype=BF16),
        compiler_params=params_of(16), cost_estimate=estimate(4), name="last_norm",
    )(back, tokens, gain, grad_hidden)


def upward(place, mixed, tokens, glu_bias, gain, bias, ffn_bias, glu_weight, ffn_in, pieces):
    rows, features = tokens.shape
    inner = ffn_in.shape[1]
    return pl.pallas_call(
        lambda *refs: upward_kernel(pieces, *refs),
        in_specs=[SMEM] + [VMEM] * 6 + [ANY] * 2,
        out_shape=(
            shaped(2, 2, rows, features // 2), shaped(2, 2, rows, inner // 4), shaped(rows, 2 * features),
            shaped(rows, features), shaped(rows, features), shaped(rows, inner), shaped(rows, inner, dtype=BF16),
        ),
        scratch_shapes=[
            pltpu.VMEM(glu_weight.shape, BF16), pltpu.VMEM(ffn_in.shape, BF16),
            pltpu.SemaphoreType.DMA((4,)), pltpu.SemaphoreType.DMA((8,)),
        ],
        compiler_params=params_of(40), cost_estimate=estimate(14), name="upward",
    )(place, mixed, tokens, glu_bias, gain, bias, ffn_bias, glu_weight, ffn_in)


def downward(place, cot, slope2, hidden, pre, slope1, gain, ffn_out, ffn_in, glu_weight):
    rows, features = cot.shape
    inner = ffn_in.shape[1]
    return pl.pallas_call(
        downward_kernel,
        in_specs=[SMEM] + [VMEM] * 6 + [ANY] * 3,
        out_shape=(
            shaped(2, rows, inner // 2), shaped(2, rows, features), shaped(rows, features),
            shaped(features, rows), shaped(1, inner), shaped(1, 2 * features), shaped(1, features),
            shaped(1, features), shaped(1, features),
        ),
        scratch_shapes=[
            pltpu.VMEM(ffn_out.shape, BF16), pltpu.VMEM(ffn_in.shape, BF16), pltpu.VMEM(glu_weight.shape, BF16),
            pltpu.SemaphoreType.DMA((8,)), pltpu.SemaphoreType.DMA((8,)), pltpu.SemaphoreType.DMA((1,)),
        ],
        compiler_params=params_of(48), cost_estimate=estimate(18), name="downward",
    )(place, cot, slope2, hidden, pre, slope1, gain, ffn_out, ffn_in, glu_weight)


def products(place, lefts, rights, blocks):
    count = len(lefts)
    tall, wide = lefts[0].shape[-1], rights[0].shape[-1]
    out = shaped(blocks // 2, tall // blocks, wide)
    return pl.pallas_call(
        lambda *refs: product_kernel(count, *refs),
        in_specs=[SMEM] + [VMEM] * (2 * count),
        out_shape=(out, out),
        scratch_shapes=[pltpu.VMEM((tall, wide), F32)],
        compiler_params=params_of(40), cost_estimate=estimate(4), name="products",
    )(place, *lefts, *rights)


def flipped(value, axis, bit):
    count = lax.axis_size(axis)
    return lax.ppermute(value, axis, [(i, i ^ bit) for i in range(count)])


def summed(value, axes):
    for axis in axes:
        bit = 1
        while bit < lax.axis_size(axis):
            value = value + flipped(value, axis, bit)
            bit *= 2
    return value


def halved(value, dim, which):
    first = lax.index_in_dim(value, 0, dim, keepdims=False)
    second = lax.index_in_dim(value, 1, dim, keepdims=False)
    pick = which == 0
    return jnp.where(pick, first, second), jnp.where(pick, second, first)


def across(value, bit=1):
    return flipped(value, "seq", bit)


def over_batch(value):
    return flipped(value, "batch", 1)


def over_line(blocks, mine):
    bit = 4
    while blocks.shape[0] > 1:
        pairs = blocks.reshape((blocks.shape[0] // 2, 2) + blocks.shape[1:])
        keep, send = halved(pairs, 1, (mine // bit) % 2)
        blocks = keep + across(send, bit)
        bit *= 2
    return blocks[0]


def mode_parts(params):
    decay_log, decay_freq, input_re, input_im, output_re, output_im, step_log = params
    step_size = jnp.exp(step_log)[:, None]
    real_part = -jnp.exp(decay_log)
    delta_re = step_size * real_part
    delta_im = step_size * decay_freq
    magnitude = jnp.exp(delta_re)
    lam_re, lam_im = (magnitude * jnp.cos(delta_im), magnitude * jnp.sin(delta_im))
    denominator = real_part * real_part + decay_freq * decay_freq
    num_re = lam_re - 1.0
    rat_re = (num_re * real_part + lam_im * decay_freq) / denominator
    rat_im = (lam_im * real_part - num_re * decay_freq) / denominator
    bbar_re = rat_re * input_re - rat_im * input_im
    bbar_im = rat_re * input_im + rat_im * input_re
    prod_re = 2.0 * (output_re * bbar_re - output_im * bbar_im)
    prod_im = 2.0 * (output_re * bbar_im + output_im * bbar_re)
    return (delta_re, delta_im, prod_re, prod_im), (lam_re, lam_im)


def packed(real, imag):
    return jnp.concatenate([real, imag], axis=1)


def on_device(
    tokens, segments, norm1_gain, norm1_bias, decay_log, decay_freq, input_re, input_im,
    output_re, output_im, step_log, skip_gain, glu_weight, glu_bias, norm2_gain, norm2_bias,
    ffn_in, ffn_in_bias, ffn_out, ffn_out_bias, cotangent,
):
    contexts, piece_len, features = tokens.shape
    rows = contexts * piece_len
    pieces, mine = lax.axis_size("seq"), lax.axis_index("seq")
    channels = features // pieces
    docs = max(1, pieces * piece_len // 256)
    params = (decay_log, decay_freq, input_re, input_im, output_re, output_im, step_log)
    batch_bit = lax.axis_index("batch") % 2
    place = jnp.stack([mine % 2, batch_bit, (mine // 2) % 2]).astype(jnp.int32)

    def own(value):
        return lax.dynamic_slice_in_dim(value, mine * channels, channels, 0)

    def row_of(value):
        return jnp.broadcast_to(own(value)[:, None], (channels, LANES))

    def line(value):
        return value.reshape(1, -1)

    def by_channel(value):
        return lax.all_to_all(value, "seq", 0, 0)

    parts, lam_pair = mode_parts(tuple(own(p) for p in params))
    lam, weight = packed(*lam_pair), packed(parts[2], parts[3])
    skip = row_of(skip_gain)
    flat = tokens.reshape(rows, features)
    cot = cotangent.reshape(rows, features)

    send, up = first_norm(
        flat, cot, segments.reshape(1, rows), line(norm1_gain), line(norm1_bias), pieces
    )
    recv = by_channel(send).reshape(pieces * (channels + 8), rows)
    up_x = over_batch(up)
    ups = [up, up_x, across(up), across(up_x)]
    mixed_rows, enter, lags = recurrence(recv, lam, weight, skip, pieces, docs, FORWARD_UNROLL)
    mixed = by_channel(mixed_rows.reshape(pieces, channels, rows)).reshape(features, rows)
    acts, ffn_parts, glu_pre, hidden, slope1, slope2, ffn_low = upward(
        place, mixed, flat, line(glu_bias), line(norm2_gain), line(norm2_bias), line(ffn_in_bias),
        glu_weight, ffn_in, pieces,
    )
    pre_parts, glu_parts, grad_hidden, turned, bias_in, bias_glu, grad_g2, grad_b2, bias_out = downward(
        place, cot, slope2, hidden, glu_pre, slope1, line(norm2_gain), ffn_out, ffn_in, glu_weight
    )

    ffn_x = over_batch(ffn_parts[1])
    acts, pre_parts, glu_parts, ffn_x = lax.optimization_barrier((acts, pre_parts, glu_parts, ffn_x))
    lefts = [ffn_parts[0, 0], ffn_x[0], across(ffn_parts[0, 1]), across(ffn_x[1])]
    keep_out, send_out = products(place, lefts, ups, pieces // 2)
    acts_x = over_batch(acts)
    acts_c, acts_cx = across(acts[1]), across(acts_x[1])
    pre_x = over_batch(pre_parts[1])
    rights = [pre_parts[0], pre_x, across(pre_parts[0]), across(pre_x)]
    lefts = [acts[0, 1], acts_x[0, 1], acts_c[1], acts_cx[1]]
    keep_in, send_in = products(place, lefts, rights, pieces // 2)
    glu_x = over_batch(glu_parts[1])
    rights = [glu_parts[0], glu_x, across(glu_parts[0]), across(glu_x)]
    lefts = [acts[0, 0], acts_x[0, 0], acts_c[0], acts_cx[0]]
    keep_glu, send_glu = products(place, lefts, rights, pieces // 2)

    def joined(keep, sent, axis):
        value = over_line(keep + across(sent, 2), mine)
        bit = 2
        while bit < lax.axis_size("batch"):
            value = value + flipped(value, "batch", bit)
            bit *= 2
        other = over_batch(value)
        pick = batch_bit == 0
        return jnp.concatenate(
            [jnp.where(pick, value, other), jnp.where(pick, other, value)], axis=axis
        )

    back = by_channel(turned.reshape(pieces, channels, rows)).reshape(pieces * channels, rows)
    back, send_out = lax.optimization_barrier((back, send_out))
    sum_out = joined(keep_out, send_out, 0)
    grad_rows, sums, firsts, lagsum, bias_part = recurrence_back(
        recv, back, enter, lags, lam, weight, skip, pieces, docs, BACKWARD_UNROLL
    )
    small = jnp.concatenate([bias_glu, grad_g2, grad_b2, bias_in, bias_out], axis=1)
    grad_rows, small, ffn_low = lax.optimization_barrier((grad_rows, small, ffn_low))
    ffn_res = jnp.dot(ffn_low, ffn_out, preferred_element_type=F32) + ffn_out_bias
    result = (hidden + ffn_res).astype(BF16).reshape(tokens.shape)
    grad_normed = by_channel(grad_rows.reshape(pieces, channels, rows)).reshape(features, rows)
    grad_tokens = last_norm(grad_normed, flat, line(norm1_gain), grad_hidden).reshape(tokens.shape)

    sum_in = joined(keep_in, send_in, 1)
    sum_glu = joined(keep_glu, send_glu, 1)

    vectors = jnp.concatenate([lagsum[:, LANES - 1], jnp.sum(bias_part, axis=1)]).reshape(1, -1)
    vectors = jnp.pad(vectors, ((0, 7), (0, 2 * LANES - vectors.shape[1])))
    state = jnp.concatenate([jnp.concatenate([sums, firsts], axis=1), vectors], axis=0)
    state = summed(state, ("batch",))
    state = by_channel(jnp.broadcast_to(state[None], (pieces,) + state.shape))
    vectors = state[:, channels]
    grad_skip = vectors[:, :channels].reshape(features)
    grad_bias1 = vectors[:, channels : 2 * channels].reshape(features)
    state = state[:, :channels].reshape(features, 2 * LANES)
    half = LANES // 2
    m_re, m_im = state[:, :half], state[:, half:LANES]
    f_re, f_im = state[:, LANES : LANES + half], state[:, LANES + half : 2 * LANES]
    whole_parts, mode_pull = jax.vjp(lambda p: mode_parts(p)[0], params)
    w_re, w_im = whole_parts[2], whole_parts[3]
    grad_params = mode_pull(
        (w_re * f_re - w_im * f_im, -(w_re * f_im + w_im * f_re), m_re, -m_im)
    )[0]
    grad_gain1 = (
        jnp.sum(w_re * m_re - w_im * m_im, axis=1) + skip_gain * grad_skip - norm1_bias * grad_bias1
    ) / norm1_gain
    small = summed(small.reshape(-1, LANES), ("seq", "batch")).reshape(-1)
    bias_glu, grad_g2, grad_b2, bias_in, bias_out = jnp.split(
        small, [2 * features, 3 * features, 4 * features, small.shape[0] - features]
    )
    return (
        result, grad_tokens, grad_gain1, grad_bias1, *grad_params, grad_skip,
        sum_glu, bias_glu, grad_g2, grad_b2, sum_in, bias_in, sum_out, bias_out,
    )


def solution(mesh):
    spread_over = P("batch", "seq", None)
    in_specs = (spread_over, P("batch", "seq")) + (P(),) * 18 + (spread_over,)
    rows = P("seq", None)
    out_specs = (spread_over,) * 2 + (P(),) * 10 + (rows,) + (P(),) * 3 + (rows, P(), rows, P())
    return jax.shard_map(
        on_device, mesh=mesh, in_specs=in_specs, out_specs=out_specs, check_vma=False
    )
```

```python
import functools

import jax, jax.numpy as jnp
from jax import lax
from jax.sharding import PartitionSpec as P
from jax.experimental import pallas as pl
from jax.experimental.pallas import tpu as pltpu
F32, BF16 = jnp.float32, jnp.bfloat16
LANES = 128
HALF = 64
FORWARD_UNROLL = 16
BACKWARD_UNROLL = 8
NN = (((1,), (0,)), ((), ()))
NT = (((1,), (1,)), ((), ()))
TN = (((0,), (0,)), ((), ()))


def halves(value):
    high = value.astype(BF16)
    return high, (value - high.astype(F32)).astype(BF16)


def dot(left, right, dims):
    return lax.dot_general(left, right, dims, preferred_element_type=F32)


def beside(parts):
    return jnp.concatenate(parts, axis=1)


def below(parts):
    return jnp.concatenate(parts, axis=0)


def mm(left, right):
    table = beside(right)
    out = dot(beside(left), below([table, table]), NN)
    return out[:, :LANES] + out[:, LANES:]


def mm_turned(left, right):
    out = dot(beside(left), below([beside([right[0]] * 2), beside([right[1]] * 2)]), NT)
    return out[:, :LANES] + out[:, LANES:]


def swap(value):
    return pltpu.roll(value, HALF, value.ndim - 1)


def low_lanes(shape):
    return lax.broadcasted_iota(jnp.int32, shape, len(shape) - 1) < HALF


def as_factor(value):
    turned = swap(value)
    low = low_lanes(value.shape)
    return jnp.where(low, value, turned), jnp.where(low, -turned, value)


def times(value, factor):
    return value * factor[0] + swap(value) * factor[1]


def power_setup(lam, base_ref, fre_ref, fim_ref, steps, channels):
    one = jnp.where(low_lanes(lam.shape), 1.0, 0.0)
    factor = as_factor(lam)
    row = one
    for k in range(8):
        base_ref[pl.ds(k * channels, channels), :] = row
        row = times(row, factor)
    eight = as_factor(row)
    row = one
    for i in range(16):
        fre, fim = as_factor(row)
        fre_ref[pl.ds(i * channels, channels), :] = fre
        fim_ref[pl.ds(i * channels, channels), :] = fim
        row = times(row, eight)
    for s in range(steps):
        fre, fim = as_factor(row)
        fre_ref[pl.ds((16 + s) * channels, channels), :] = fre
        fim_ref[pl.ds((16 + s) * channels, channels), :] = fim
        row = times(row, (fre, fim))


def power_tables(h, base_ref, fre_ref, fim_ref, channels):
    base = base_ref[pl.ds(h, 8, stride=channels), :]
    turned = swap(base)
    return below([
        base * fre_ref[pl.ds(h + i * channels, 1), :] + turned * fim_ref[pl.ds(h + i * channels, 1), :]
        for i in range(16)
    ])


def reversed_tables(h, base_ref, fre_ref, fim_ref, channels):
    base = below([base_ref[pl.ds(h + k * channels, 1), :] for k in range(7, -1, -1)])
    turned = swap(base)
    return below([
        base * fre_ref[pl.ds(h + i * channels, 1), :] + turned * fim_ref[pl.ds(h + i * channels, 1), :]
        for i in range(15, -1, -1)
    ])


def doc_masks(seg_ref, mask_ref, row, pitch, chunks, docs, turn):
    even = seg_ref[pl.ds(row, chunks, stride=2 * pitch), :]
    odd = seg_ref[pl.ds(row + pitch, chunks, stride=2 * pitch), :]
    pair = join(even, odd)
    at = lax.broadcasted_iota(jnp.int32, (LANES, LANES), 0)
    to = lax.broadcasted_iota(jnp.int32, (LANES, LANES), 1)
    turning = jnp.where(at + to == LANES - 1, 1.0, 0.0).astype(BF16)
    for d in range(docs):
        for c in range(2):
            mask = jnp.where(pair[c] == float(d), 1.0, 0.0)
            mask_ref[d * 2 + c] = mask
            if turn:
                mask_ref[(docs + d) * 2 + c] = dot(mask.astype(BF16), turning, NN)


def join(even, odd):
    low = low_lanes(even.shape)
    return jnp.where(low, even, swap(odd)), jnp.where(low, swap(even), odd)


def join_turned(even, odd):
    low = low_lanes(even.shape)
    return jnp.where(low, swap(odd), even), jnp.where(low, odd, swap(even))


def apart_turned(first, second):
    low = low_lanes(first.shape)
    return jnp.where(low, swap(second), first), jnp.where(low, second, swap(first))


def spread(pair, mask_ref, docs, base=0):
    return below([pair[c] * mask_ref[base + d * 2 + c] for d in range(docs) for c in range(2)])


def gathered(rows, mask_ref, chunks, docs, base=0):
    out = []
    for c in range(2):
        total = None
        for d in range(docs):
            at = (d * 2 + c) * chunks
            term = rows[at : at + chunks] * mask_ref[base + d * 2 + c]
            total = term if total is None else total + term
        out.append(total)
    return out


def scan_factors(h, fre_ref, fim_ref, channels, chunks, steps, backward):
    at = lax.broadcasted_iota(jnp.int32, (chunks, LANES), 0)
    out = []
    for s in range(steps):
        keep = at < chunks - (1 << s) if backward else at >= (1 << s)
        fre = fre_ref[pl.ds(h + (16 + s) * channels, 1), :]
        fim = fim_ref[pl.ds(h + (16 + s) * channels, 1), :]
        out.append((jnp.where(keep, fre, 0.0), jnp.where(keep, fim, 0.0)))
    return out


def scan_chunks(rows, factors, chunks, backward):
    at = lax.broadcasted_iota(jnp.int32, (chunks, LANES), 0)
    keep = at < chunks - 1 if backward else at >= 1
    out = []
    for i in range(rows.shape[0] // chunks):
        part = rows[i * chunks : (i + 1) * chunks]
        for s, factor in enumerate(factors):
            moved = pltpu.roll(part, chunks - (1 << s) if backward else 1 << s, 0)
            part = part + times(moved, factor)
        moved = pltpu.roll(part, chunks - 1 if backward else 1, 0)
        out.append(jnp.where(keep, moved, 0.0))
    return jnp.concatenate(out, axis=0)


def toeplitz(row):
    wide = jnp.broadcast_to(row, (LANES, LANES))
    wide = pltpu.roll(wide, 0, 1, stride=1, stride_axis=0)
    j = lax.broadcasted_iota(jnp.int32, (LANES, LANES), 0)
    t = lax.broadcasted_iota(jnp.int32, (LANES, LANES), 1)
    return jnp.where(t >= j, wide, 0.0)


def turned_lag_sums(table):
    moved = pltpu.roll(table, 0, 1, stride=1, stride_axis=0)
    at = lax.broadcasted_iota(jnp.int32, (LANES, LANES), 0)
    lane = lax.broadcasted_iota(jnp.int32, (LANES, LANES), 1)
    return jnp.sum(jnp.where(lane >= at, moved, 0.0), axis=0, keepdims=True)


def together(works):
    while works:
        works = [work for work in works if next(work, None)]


def first_rows(first, second):
    at = lax.broadcasted_iota(jnp.int32, (8, LANES), 0)
    return jnp.where(at == 0, first, jnp.where(at == 1, second, 0.0))


def forward_kernel(
    sizes, recv_ref, lam_ref, weight_ref, skip_ref, out_ref, enter_ref, lag_ref,
    base_ref, fre_ref, fim_ref, mask_ref,
):
    channels, chunks, docs, steps, pitch, unroll = sizes
    rows = docs * 2 * chunks
    power_setup(lam_ref[...], base_ref, fre_ref, fim_ref, steps, channels)
    doc_masks(recv_ref, mask_ref, channels, pitch, chunks, docs, False)

    def one(h):
        pair = join(
            recv_ref[pl.ds(h, chunks, stride=2 * pitch), :],
            recv_ref[pl.ds(h + pitch, chunks, stride=2 * pitch), :],
        )
        inputs = halves(spread(pair, mask_ref, docs))
        power = halves(power_tables(h, base_ref, fre_ref, fim_ref, channels))
        yield True
        back = halves(reversed_tables(h, base_ref, fre_ref, fim_ref, channels))
        weight = weight_ref[pl.ds(h, 1), :]
        low = low_lanes((1, LANES))
        signed = halves(jnp.where(low, weight, -weight))
        both = first_rows(signed[0].astype(F32), signed[1].astype(F32)).astype(BF16)
        yield True
        lags = dot(both, below(power), NT)
        lags = lags[0:1] + lags[1:2]
        lags = lags[:, :LANES] + lags[:, LANES:]
        lag_ref[pl.ds(h, 1), :] = lags
        yield True
        table = halves(toeplitz(lags))
        yield True
        out = dot(below(inputs), beside([back[0], table[0]]), NN)
        out = out[:rows] + out[rows:] + dot(inputs[0], beside([back[1], table[1]]), NN)
        yield True
        enter = scan_chunks(
            out[:, :LANES], scan_factors(h, fre_ref, fim_ref, channels, chunks, steps, False), chunks, False
        )
        enter_ref[h] = enter
        yield True
        lam = as_factor(lam_ref[pl.ds(h, 1), :])
        coef = as_factor(times(weight, lam))
        coef = (jnp.where(low, coef[0], -coef[0]), jnp.where(low, coef[1], -coef[1]))
        yield True
        mixed = out[:, LANES:] + mm_turned(halves(times(enter, coef)), power)
        yield True
        first, second = gathered(mixed, mask_ref, chunks, docs)
        skip = skip_ref[pl.ds(h, 1), :]
        even, odd = join(first + skip * pair[0], second + skip * pair[1])
        out_ref[pl.ds(h, chunks, stride=2 * channels), :] = even
        out_ref[pl.ds(h + channels, chunks, stride=2 * channels), :] = odd

    def several(i, carry):
        together([one(i * unroll + k) for k in range(unroll)])
        return carry

    lax.fori_loop(0, channels // unroll, several, 0)


def backward_kernel(
    sizes, recv_ref, grad_ref, enter_ref, lag_ref, lam_ref, weight_ref, skip_ref,
    out_ref, sum_ref, first_ref, lagsum_ref, bias_ref,
    base_ref, fre_ref, fim_ref, mask_ref,
):
    channels, chunks, docs, steps, pitch, unroll = sizes
    rows = docs * 2 * chunks
    power_setup(lam_ref[...], base_ref, fre_ref, fim_ref, steps, channels)
    doc_masks(recv_ref, mask_ref, channels, pitch, chunks, docs, True)
    reach = (LANES - 1 - lax.broadcasted_iota(jnp.int32, (1, LANES), 1)).astype(F32)

    def one(h):
        pair = join(
            recv_ref[pl.ds(h, chunks, stride=2 * pitch), :],
            recv_ref[pl.ds(h + pitch, chunks, stride=2 * pitch), :],
        )
        gpair = join_turned(
            grad_ref[pl.ds(h, chunks, stride=2 * pitch), :],
            grad_ref[pl.ds(h + pitch, chunks, stride=2 * pitch), :],
        )
        inputs = spread(pair, mask_ref, docs)
        grads = spread(gpair, mask_ref, docs, docs * 2)
        ih, il = halves(inputs)
        gh, gl = halves(grads)
        yield True
        lagsum = turned_lag_sums(dot(below([gh, gl, gh]), below([ih, ih, il]), TN))
        lagsum_ref[pl.ds(h, 1), :] = lagsum
        yield True
        power = halves(power_tables(h, base_ref, fre_ref, fim_ref, channels))
        yield True
        back = halves(reversed_tables(h, base_ref, fre_ref, fim_ref, channels))
        weight = weight_ref[pl.ds(h, 1), :]
        lam = as_factor(lam_ref[pl.ds(h, 1), :])
        yield True
        table = halves(toeplitz(lag_ref[pl.ds(h, 1), :]))
        yield True
        enter = enter_ref[h]
        ahead = scan_factors(h, fre_ref, fim_ref, channels, chunks, steps, False)
        astern = scan_factors(h, fre_ref, fim_ref, channels, chunks, steps, True)
        i1h, i1l = halves(inputs * reach)
        g1h, g1l = halves(grads * reach)
        lh, ll = halves(first_rows(lagsum, lagsum * reach))
        yield True
        out = mm((below([i1h, gh, g1h, lh]), below([i1l, gl, g1l, ll])), back)
        yield True
        hop = (
            fre_ref[pl.ds(h + 16 * channels, 1), :] * float(LANES),
            fim_ref[pl.ds(h + 16 * channels, 1), :] * float(LANES),
        )
        turned = swap(enter)
        enter1 = scan_chunks(
            out[:rows] + enter * hop[0] + turned * hop[1], ahead, chunks, False
        )
        yield True
        seen = out[rows : 2 * rows]
        seen1 = seen + out[2 * rows : 3 * rows]
        seen_t = swap(seen)

        def summed_product(plain, crossed):
            plain = jnp.sum(plain, axis=0, keepdims=True)
            crossed = jnp.sum(crossed, axis=0, keepdims=True)
            low = low_lanes((1, LANES))
            plain, crossed = plain - swap(plain), crossed + swap(crossed)
            return times(jnp.where(low, plain, crossed), lam)

        sum_ref[pl.ds(h, 1), :] = (
            summed_product(enter * seen, turned * seen) + out[3 * rows : 3 * rows + 1]
        )
        first_ref[pl.ds(h, 1), :] = summed_product(
            enter1 * seen + enter * seen1, enter1 * seen_t + turned * seen1
        ) + out[3 * rows + 1 : 3 * rows + 2]
        yield True
        coef = as_factor(times(weight, lam))
        leave = scan_chunks(seen * coef[0] + seen_t * coef[1], astern, chunks, True)
        leave = jnp.where(low_lanes(leave.shape), leave, -leave)
        yield True
        inner = mm((gh, gl), table) + mm_turned(halves(leave), power)
        yield True
        gfirst, gsecond = gathered(inner, mask_ref, chunks, docs, docs * 2)
        skip = skip_ref[pl.ds(h, 1), :]
        gfirst = gfirst + skip * gpair[0]
        gsecond = gsecond + skip * gpair[1]
        bias_ref[pl.ds(h, 1), :] = jnp.sum(gfirst + gsecond, axis=0, keepdims=True)
        even, odd = apart_turned(gfirst, gsecond)
        out_ref[pl.ds(h, chunks, stride=2 * channels), :] = even
        out_ref[pl.ds(h + channels, chunks, stride=2 * channels), :] = odd

    def several(i, carry):
        together([one(i * unroll + k) for k in range(unroll)])
        return carry

    lax.fori_loop(0, channels // unroll, several, 0)


REACH = 512


def kernel_sizes(recv_rows, channels, pieces, docs, unroll):
    chunks = pieces // 2
    unroll = min(channels, max(1, unroll * 64 // (docs * 2 * chunks)))
    steps = min((chunks - 1).bit_length(), (REACH // LANES - 1).bit_length())
    return (channels, chunks, docs, steps, channels + 8, unroll)


def scratch(channels, chunks, docs, steps):
    return [
        pltpu.VMEM((8 * channels, LANES), F32),
        pltpu.VMEM(((16 + steps) * channels, LANES), F32),
        pltpu.VMEM(((16 + steps) * channels, LANES), F32),
        pltpu.VMEM((docs * 4, chunks, LANES), F32),
    ]


def recurrence(recv, lam, weight, skip, pieces, docs, unroll=2):
    channels = lam.shape[0]
    sizes = kernel_sizes(recv.shape[0], channels, pieces, docs, unroll)
    chunks, steps = sizes[1], sizes[3]
    rows = docs * 2 * chunks
    return pl.pallas_call(
        lambda *refs: forward_kernel(sizes, *refs),
        out_shape=(
            jax.ShapeDtypeStruct((pieces * channels, LANES), F32),
            jax.ShapeDtypeStruct((channels, rows, LANES), F32),
            jax.ShapeDtypeStruct((channels, LANES), F32),
        ),
        scratch_shapes=scratch(channels, chunks, docs, steps),
        compiler_params=pltpu.CompilerParams(vmem_limit_bytes=48 << 20),
        cost_estimate=estimate(16),
        name="recurrence",
    )(recv, lam, weight, skip)


def recurrence_back(recv, grad, enter, lags, lam, weight, skip, pieces, docs, unroll=2):
    channels = lam.shape[0]
    sizes = kernel_sizes(recv.shape[0], channels, pieces, docs, unroll)
    chunks, steps = sizes[1], sizes[3]
    row = jax.ShapeDtypeStruct((channels, LANES), F32)
    return pl.pallas_call(
        lambda *refs: backward_kernel(sizes, *refs),
        out_shape=(jax.ShapeDtypeStruct((pieces * channels, LANES), F32), row, row, row, row),
        scratch_shapes=scratch(channels, chunks, docs, steps),
        compiler_params=pltpu.CompilerParams(vmem_limit_bytes=48 << 20),
        cost_estimate=estimate(30),
        name="recurrence_back",
    )(recv, grad, enter, lags, lam, weight, skip)


EPSILON = 1e-05
MIB = 1 << 20


def estimate(micros, moved=0):
    return pl.CostEstimate(flops=int(micros * 1e9), transcendentals=0, bytes_accessed=int(moved))


def bell(values):
    share = 0.5 + 0.5 * lax.erf(values * 0.7071067811865476)
    return share, values * jnp.exp(-0.5 * values * values) * 0.3989422804014327


def sent_rows(values, out_ref, channels):
    turned = values.T
    for s in range(out_ref.shape[0]):
        out_ref[s, 0:channels, :] = turned[s * channels : (s + 1) * channels]


def share_rows(length, pieces):
    share = length // pieces
    return max(1, share // LANES), min(share, LANES)


def share_vectors(refs, out_ref, first):
    pieces = out_ref.shape[0]
    at = first
    for s in range(pieces):
        out_ref[s, first : first + 8, :] = jnp.zeros((8, LANES), F32)
    for ref in refs:
        count, wide = share_rows(ref.shape[1], pieces)
        for s in range(pieces):
            for r in range(count):
                start = (s * count + r) * wide
                out_ref[s, at + r : at + r + 1, :wide] = ref[:, start : start + wide]
        at += count


def normalize(values):
    centre = values - jnp.mean(values, axis=1, keepdims=True)
    recip = lax.rsqrt(jnp.mean(centre * centre, axis=1, keepdims=True) + EPSILON)
    return centre * recip, recip


def norm_back(grad, unit, recip):
    return recip * (
        grad
        - jnp.mean(grad, axis=1, keepdims=True)
        - unit * jnp.mean(grad * unit, axis=1, keepdims=True)
    )


def turning(size):
    at = lax.broadcasted_iota(jnp.int32, (size, size), 0)
    to = lax.broadcasted_iota(jnp.int32, (size, size), 1)
    return jnp.where(at + to == size - 1, 1.0, 0.0).astype(BF16)


def first_kernel(tokens_ref, cot_ref, seg_ref, gain_ref, bias_ref, send_ref, up_ref):
    pieces, pitch, rows = send_ref.shape
    channels = pitch - 8
    unit, _ = normalize(tokens_ref[...].astype(F32))
    sent_rows(unit * gain_ref[...] + bias_ref[...], send_ref, channels)
    seg = jnp.broadcast_to(seg_ref[...].astype(F32), (8, rows))
    for s in range(pieces):
        send_ref[s, channels:pitch, :] = seg
    up_ref[...] = cot_ref[...].astype(F32)


def last_kernel(back_ref, tokens_ref, gain_ref, hidden_ref, out_ref):
    unit, recip = normalize(tokens_ref[...].astype(F32))
    turn = turning(tokens_ref.shape[0])
    high, low = halves(back_ref[...])
    grad = (dot(turn, high, NT) + dot(turn, low, NT)) * gain_ref[...]
    out_ref[...] = (hidden_ref[...] + norm_back(grad, unit, recip)).astype(BF16)


def fetch(source, target, sems, chunks, rows):
    out = []
    wide = source.shape[0 if rows else 1] // chunks
    for i in range(chunks):
        part = (pl.ds(i * wide, wide), slice(None)) if rows else (slice(None), pl.ds(i * wide, wide))
        copy = pltpu.make_async_copy(source.at[part], target.at[part], sems.at[i])
        copy.start()
        out.append(copy)
    return out


def by_core(values, place_ref, out_ref, at, pieces):
    wide = values.shape[1] // pieces
    for s in range(pieces):
        slot = (s % 2) ^ place_ref[0]
        out_ref[slot, at, :, (s // 2) * wide : (s // 2 + 1) * wide] = values[:, s * wide : (s + 1) * wide]


def upward_kernel(
    pieces, place_ref, mixed_ref, tokens_ref, glu_bias_ref, gain_ref, bias_ref, ffn_bias_ref, glu_ref, ffn_ref,
    acts_ref, keep_ref, pre_ref, hidden_ref, slope1_ref, slope2_ref, low_ref,
    glu_v, ffn_v, glu_sem, ffn_sem,
):
    rows, features = tokens_ref.shape
    glu_copies = fetch(glu_ref, glu_v, glu_sem, 4, False)
    ffn_copies = fetch(ffn_ref, ffn_v, ffn_sem, 8, False)
    mixed = mixed_ref[...].T
    share, steep = bell(mixed)
    slope1_ref[...] = share + steep
    act = (mixed * share).astype(BF16)
    by_core(act.astype(F32), place_ref, acts_ref, 0, pieces)
    wide = glu_ref.shape[1] // 4
    for i in range(4):
        glu_copies[i].wait()
        at = slice(i * wide, (i + 1) * wide)
        pre_ref[:, at] = (
            jnp.dot(act, glu_v[:, at], preferred_element_type=F32) + glu_bias_ref[:, at]
        )
    hidden = tokens_ref[...].astype(F32) + pre_ref[:, :features] * jax.nn.sigmoid(pre_ref[:, features:])
    hidden_ref[...] = hidden
    unit, _ = normalize(hidden)
    normed = (unit * gain_ref[...] + bias_ref[...]).astype(BF16)
    by_core(normed.astype(F32), place_ref, acts_ref, 1, pieces)
    wide = ffn_ref.shape[1] // 8
    block = ffn_ref.shape[1] // pieces // 2
    for i in range(8):
        ffn_copies[i].wait()
        at = slice(i * wide, (i + 1) * wide)
        ffn_pre = jnp.dot(normed, ffn_v[:, at], preferred_element_type=F32) + ffn_bias_ref[:, at]
        share, steep = bell(ffn_pre)
        slope2_ref[:, at] = share + steep
        low = (ffn_pre * share).astype(BF16)
        low_ref[:, at] = low
        wider = low.astype(F32)
        for k in range(wide // block):
            index = (i * wide) // block + k
            piece, half = index // 2, index % 2
            keep_ref[
                half ^ place_ref[1], (piece % 2) ^ place_ref[0], :,
                (piece // 2) * block : (piece // 2 + 1) * block,
            ] = wider[:, k * block : (k + 1) * block]


def downward_kernel(
    place_ref, cot_ref, slope2_ref, hidden_ref, pre_ref, slope1_ref, gain_ref, out_w_ref, in_w_ref, glu_w_ref,
    sent_pre_ref, sent_glu_ref, grad_hidden_ref, turned_ref,
    in_sum_ref, glu_sum_ref, gain_sum_ref, bias_sum_ref, out_sum_ref,
    out_v, in_v, glu_v, out_sem, in_sem, glu_sem,
):
    rows, features = cot_ref.shape
    inner = out_w_ref.shape[0]
    wide = inner // 8
    out_copies = fetch(out_w_ref, out_v, out_sem, 8, True)
    in_copies = fetch(in_w_ref, in_v, in_sem, 8, False)
    glu_copies = fetch(glu_w_ref, glu_v, glu_sem, 1, False)
    cot = cot_ref[...]
    up = cot.astype(F32)
    out_sum_ref[...] = jnp.sum(up, axis=0, keepdims=True)
    total = jnp.zeros((rows, features), F32)
    for i in range(8):
        at = slice(i * wide, (i + 1) * wide)
        out_copies[i].wait()
        grad = lax.dot_general(cot, out_v[at, :], NT, preferred_element_type=F32)
        low = (grad * slope2_ref[:, at]).astype(BF16)
        wider = low.astype(F32)
        in_sum_ref[:, at] = jnp.sum(wider, axis=0, keepdims=True)
        sent_pre_ref[(i // 4) ^ place_ref[1], :, (i % 4) * wide : (i % 4 + 1) * wide] = wider
        in_copies[i].wait()
        total = total + lax.dot_general(low, in_v[:, at], NT, preferred_element_type=F32)
    unit, recip = normalize(hidden_ref[...])
    gain_sum_ref[...] = jnp.sum(total * unit, axis=0, keepdims=True)
    bias_sum_ref[...] = jnp.sum(total, axis=0, keepdims=True)
    grad_hidden = up + norm_back(total * gain_ref[...], unit, recip)
    grad_hidden_ref[...] = grad_hidden
    gate = jax.nn.sigmoid(pre_ref[:, features:])
    first = (grad_hidden * gate).astype(BF16)
    second = (grad_hidden * pre_ref[:, :features] * (gate * (1.0 - gate))).astype(BF16)
    glu_copies[0].wait()
    grad_act = None
    for k, part in enumerate((first, second)):
        wider = part.astype(F32)
        at = slice(k * features, (k + 1) * features)
        glu_sum_ref[:, at] = jnp.sum(wider, axis=0, keepdims=True)
        sent_glu_ref[k ^ place_ref[1]] = wider
        term = lax.dot_general(part, glu_v[:, at], NT, preferred_element_type=F32)
        grad_act = term if grad_act is None else grad_act + term
    turn = turning(rows)
    high, low = halves(grad_act * slope1_ref[...])
    sent_rows(dot(turn, high, NN) + dot(turn, low, NN), turned_ref, turned_ref.shape[1] - 8)
    share_vectors(
        (in_sum_ref, glu_sum_ref, gain_sum_ref, bias_sum_ref, out_sum_ref), turned_ref, turned_ref.shape[1] - 8
    )


def product_kernel(count, place_ref, *refs):
    lefts, rights = refs[:count], refs[count : 2 * count]
    outs, scratch_ref = refs[2 * count : -1], refs[-1]
    total = None
    for left, right in zip(lefts, rights):
        term = lax.dot_general(
            left[...].astype(BF16), right[...].astype(BF16), TN, preferred_element_type=F32
        )
        total = term if total is None else total + term
    scratch_ref[...] = total
    blocks, height, wide = outs[0].shape
    for i in range(blocks):
        for k, ref in enumerate(outs):
            block = 2 * i + (place_ref[2] ^ (k % 2))
            columns = slice(k // 2 * wide, (k // 2 + 1) * wide)
            ref[i] = scratch_ref[pl.ds(pl.multiple_of(block * height, 8), height), columns]


SMEM = pl.BlockSpec(memory_space=pltpu.SMEM)
VMEM = pl.BlockSpec(memory_space=pltpu.VMEM)
ANY = pl.BlockSpec(memory_space=pl.ANY)


def shaped(*shape, dtype=F32):
    return jax.ShapeDtypeStruct(shape, dtype)


def params_of(mib):
    return pltpu.CompilerParams(vmem_limit_bytes=mib * MIB)


def first_norm(tokens, cot, seg, gain, bias, pieces):
    rows, features = tokens.shape
    return pl.pallas_call(
        first_kernel,
        out_shape=(shaped(pieces, features // pieces + 8, rows), shaped(rows, features)),
        compiler_params=params_of(16), cost_estimate=estimate(4), name="first_norm",
    )(tokens, cot, seg, gain, bias)


def last_norm(back, tokens, gain, grad_hidden):
    return pl.pallas_call(
        last_kernel, out_shape=shaped(*tokens.shape, dtype=BF16),
        compiler_params=params_of(16), cost_estimate=estimate(4), name="last_norm",
    )(back, tokens, gain, grad_hidden)


def upward(place, mixed, tokens, glu_bias, gain, bias, ffn_bias, glu_weight, ffn_in, pieces):
    rows, features = tokens.shape
    inner = ffn_in.shape[1]
    return pl.pallas_call(
        lambda *refs: upward_kernel(pieces, *refs),
        in_specs=[SMEM] + [VMEM] * 6 + [ANY] * 2,
        out_shape=(
            shaped(2, 2, rows, features // 2), shaped(2, 2, rows, inner // 4), shaped(rows, 2 * features),
            shaped(rows, features), shaped(rows, features), shaped(rows, inner), shaped(rows, inner, dtype=BF16),
        ),
        scratch_shapes=[
            pltpu.VMEM(glu_weight.shape, BF16), pltpu.VMEM(ffn_in.shape, BF16),
            pltpu.SemaphoreType.DMA((4,)), pltpu.SemaphoreType.DMA((8,)),
        ],
        compiler_params=params_of(40), cost_estimate=estimate(14), name="upward",
    )(place, mixed, tokens, glu_bias, gain, bias, ffn_bias, glu_weight, ffn_in)


def downward(place, cot, slope2, hidden, pre, slope1, gain, ffn_out, ffn_in, glu_weight, pieces):
    rows, features = cot.shape
    inner = ffn_in.shape[1]
    return pl.pallas_call(
        downward_kernel,
        in_specs=[SMEM] + [VMEM] * 6 + [ANY] * 3,
        out_shape=(
            shaped(2, rows, inner // 2), shaped(2, rows, features), shaped(rows, features),
            shaped(pieces, features // pieces + 8, rows),
        ),
        scratch_shapes=[
            pltpu.VMEM((1, inner), F32), pltpu.VMEM((1, 2 * features), F32), pltpu.VMEM((1, features), F32),
            pltpu.VMEM((1, features), F32), pltpu.VMEM((1, features), F32),
            pltpu.VMEM(ffn_out.shape, BF16), pltpu.VMEM(ffn_in.shape, BF16), pltpu.VMEM(glu_weight.shape, BF16),
            pltpu.SemaphoreType.DMA((8,)), pltpu.SemaphoreType.DMA((8,)), pltpu.SemaphoreType.DMA((1,)),
        ],
        compiler_params=params_of(48), cost_estimate=estimate(18), name="downward",
    )(place, cot, slope2, hidden, pre, slope1, gain, ffn_out, ffn_in, glu_weight)


def products(place, lefts, rights, blocks, chunks=1):
    count = len(lefts)
    tall, wide = lefts[0].shape[-1], rights[0].shape[-1]
    out = shaped(blocks // 2, tall // blocks, wide // chunks)
    return pl.pallas_call(
        lambda *refs: product_kernel(count, *refs),
        in_specs=[SMEM] + [VMEM] * (2 * count),
        out_shape=(out,) * (2 * chunks),
        scratch_shapes=[pltpu.VMEM((tall, wide), F32)],
        compiler_params=params_of(40), cost_estimate=estimate(4), name="products",
    )(place, *lefts, *rights)


def flipped(value, axis, bit):
    count = lax.axis_size(axis)
    return lax.ppermute(value, axis, [(i, i ^ bit) for i in range(count)])


def summed(value, axes):
    for axis in axes:
        bit = 1
        while bit < lax.axis_size(axis):
            value = value + flipped(value, axis, bit)
            bit *= 2
    return value


def halved(value, dim, which):
    first = lax.index_in_dim(value, 0, dim, keepdims=False)
    second = lax.index_in_dim(value, 1, dim, keepdims=False)
    pick = which == 0
    return jnp.where(pick, first, second), jnp.where(pick, second, first)


def across(value, bit=1):
    return flipped(value, "seq", bit)


def over_batch(value):
    return flipped(value, "batch", 1)


class Halving:
    def __init__(self, keep, got, mine):
        self.keep, self.got, self.mine, self.bit = keep, got, mine, 4

    def step(self):
        blocks = self.keep + self.got
        pairs = blocks.reshape((blocks.shape[0] // 2, 2) + blocks.shape[1:])
        self.keep, send = halved(pairs, 1, (self.mine // self.bit) % 2)
        self.got = across(send, self.bit)
        self.bit *= 2

    def finish(self):
        while self.keep.shape[0] > 1:
            self.step()
        return (self.keep + self.got)[0]


def tied(works, *others):
    out = lax.optimization_barrier(tuple(work.got for work in works) + others)
    for work, got in zip(works, out):
        work.got = got
    return out[len(works) :]


def mode_parts(params):
    decay_log, decay_freq, input_re, input_im, output_re, output_im, step_log = params
    step_size = jnp.exp(step_log)[:, None]
    real_part = -jnp.exp(decay_log)
    delta_re = step_size * real_part
    delta_im = step_size * decay_freq
    magnitude = jnp.exp(delta_re)
    lam_re, lam_im = (magnitude * jnp.cos(delta_im), magnitude * jnp.sin(delta_im))
    denominator = real_part * real_part + decay_freq * decay_freq
    num_re = lam_re - 1.0
    rat_re = (num_re * real_part + lam_im * decay_freq) / denominator
    rat_im = (lam_im * real_part - num_re * decay_freq) / denominator
    bbar_re = rat_re * input_re - rat_im * input_im
    bbar_im = rat_re * input_im + rat_im * input_re
    prod_re = 2.0 * (output_re * bbar_re - output_im * bbar_im)
    prod_im = 2.0 * (output_re * bbar_im + output_im * bbar_re)
    return (delta_re, delta_im, prod_re, prod_im), (lam_re, lam_im)


def packed(real, imag):
    return jnp.concatenate([real, imag], axis=1)


def on_device(
    tokens, segments, norm1_gain, norm1_bias, decay_log, decay_freq, input_re, input_im,
    output_re, output_im, step_log, skip_gain, glu_weight, glu_bias, norm2_gain, norm2_bias,
    ffn_in, ffn_in_bias, ffn_out, ffn_out_bias, cotangent,
):
    contexts, piece_len, features = tokens.shape
    rows = contexts * piece_len
    pieces, mine = lax.axis_size("seq"), lax.axis_index("seq")
    channels = features // pieces
    docs = max(1, pieces * piece_len // 256)
    params = (decay_log, decay_freq, input_re, input_im, output_re, output_im, step_log)
    batch_bit = lax.axis_index("batch") % 2
    place = jnp.stack([mine % 2, batch_bit, (mine // 2) % 2]).astype(jnp.int32)

    def own(value):
        return lax.dynamic_slice_in_dim(value, mine * channels, channels, 0)

    def row_of(value):
        return jnp.broadcast_to(own(value)[:, None], (channels, LANES))

    def line(value):
        return value.reshape(1, -1)

    def by_channel(value):
        return lax.all_to_all(value, "seq", 0, 0)

    parts, lam_pair = mode_parts(tuple(own(p) for p in params))
    lam, weight = packed(*lam_pair), packed(parts[2], parts[3])
    skip = row_of(skip_gain)
    flat = tokens.reshape(rows, features)
    cot = cotangent.reshape(rows, features)

    send, up = first_norm(
        flat, cot, segments.reshape(1, rows), line(norm1_gain), line(norm1_bias), pieces
    )
    recv = by_channel(send).reshape(pieces * (channels + 8), rows)
    up_x = over_batch(up)
    ups = [up, up_x, across(up), across(up_x)]
    mixed_rows, enter, lags = recurrence(recv, lam, weight, skip, pieces, docs, FORWARD_UNROLL)
    mixed = by_channel(mixed_rows.reshape(pieces, channels, rows)).reshape(features, rows)
    acts, ffn_parts, glu_pre, hidden, slope1, slope2, ffn_low = upward(
        place, mixed, flat, line(glu_bias), line(norm2_gain), line(norm2_bias), line(ffn_in_bias),
        glu_weight, ffn_in, pieces,
    )
    pre_parts, glu_parts, grad_hidden, turned = downward(
        place, cot, slope2, hidden, glu_pre, slope1, line(norm2_gain), ffn_out, ffn_in, glu_weight, pieces
    )

    ffn_x = over_batch(ffn_parts[1])
    acts, pre_parts, glu_parts, ffn_x = lax.optimization_barrier((acts, pre_parts, glu_parts, ffn_x))
    acts_x, pre_x, glu_x = over_batch(acts), over_batch(pre_parts[1]), over_batch(glu_parts[1])
    lefts = [ffn_parts[0, 0], ffn_x[0], across(ffn_parts[0, 1]), across(ffn_x[1])]
    keep_out, send_out = products(place, lefts, ups, pieces // 2)
    back = by_channel(turned)
    shares = jnp.sum(back[:, channels:], axis=0)
    back, send_out = lax.optimization_barrier((back, send_out))
    out = Halving(keep_out, across(send_out, 2), mine)
    grad_rows, sums, firsts, lagsum, bias_part = recurrence_back(
        recv, back.reshape(pieces * (channels + 8), rows), enter, lags, lam, weight, skip,
        pieces, docs, BACKWARD_UNROLL,
    )
    (grad_rows,) = tied([out], grad_rows)
    out.step()
    grad_normed = by_channel(grad_rows.reshape(pieces, channels, rows)).reshape(features, rows)
    acts_c, acts_cx = across(acts[1]), across(acts_x[1])
    glu_own, out.keep = lax.optimization_barrier((glu_parts[0], out.keep))
    rights = [glu_own, glu_x, across(glu_parts[0]), across(glu_x)]
    lefts = [acts[0, 0], acts_x[0, 0], acts_c[0], acts_cx[0]]
    keep_glu, send_glu = products(place, lefts, rights, pieces // 2)
    rights = [pre_parts[0], pre_x, across(pre_parts[0]), across(pre_x)]
    lefts = [acts[0, 1], acts_x[0, 1], acts_c[1], acts_cx[1]]
    chunk_in = products(place, lefts, rights, pieces // 2, 2)
    glu = Halving(keep_glu, across(send_glu, 2), mine)
    chunk_in = tied([out], *chunk_in)
    out.step()
    first, second = (
        Halving(keep, across(sent, 2), mine) for keep, sent in (chunk_in[:2], chunk_in[2:])
    )

    vectors = jnp.concatenate([lagsum[:, LANES - 1], jnp.sum(bias_part, axis=1)]).reshape(1, -1)
    vectors = jnp.pad(vectors, ((0, 7), (0, LANES - vectors.shape[1])))
    vectors = jnp.concatenate([vectors, shares], axis=1)
    state = jnp.concatenate([jnp.concatenate([sums, firsts], axis=1), vectors], axis=0)
    state = summed(state, ("batch",))
    state = by_channel(jnp.broadcast_to(state[None], (pieces,) + state.shape))
    glu.step()
    (grad_normed, ffn_low) = tied([first], grad_normed, ffn_low)
    first.step()
    ffn_res = jnp.dot(ffn_low, ffn_out, preferred_element_type=F32) + ffn_out_bias
    result = (hidden + ffn_res).astype(BF16).reshape(tokens.shape)
    grad_tokens = last_norm(grad_normed, flat, line(norm1_gain), grad_hidden).reshape(tokens.shape)

    def all_batches(value):
        bit = 2
        while bit < lax.axis_size("batch"):
            value = value + flipped(value, "batch", bit)
            bit *= 2
        return value, over_batch(value)

    def joined(value, other, axis):
        pick = batch_bit == 0
        return jnp.concatenate(
            [jnp.where(pick, value, other), jnp.where(pick, other, value)], axis=axis
        )

    tied([second, glu])
    second.step()
    glu.step()
    tied([first, out])
    first.step()
    half_out, other_out = all_batches(out.finish())
    (state, other_out) = tied([second, glu], state, other_out)
    second.step()
    half_glu, other_glu = all_batches(glu.finish())
    (other_glu,) = tied([second, first], other_glu)
    half_in, other_in = all_batches(
        jnp.concatenate([first.finish(), second.finish()], axis=1)
    )
    sum_out, sum_glu = joined(half_out, other_out, 0), joined(half_glu, other_glu, 1)
    sum_in = joined(half_in, other_in, 1)
    vectors, shares = state[:, channels, :LANES], state[:, channels:, LANES:]
    grad_skip = vectors[:, :channels].reshape(features)
    grad_bias1 = vectors[:, channels : 2 * channels].reshape(features)
    state = state[:, :channels].reshape(features, 2 * LANES)
    half = LANES // 2
    m_re, m_im = state[:, :half], state[:, half:LANES]
    f_re, f_im = state[:, LANES : LANES + half], state[:, LANES + half : 2 * LANES]
    whole_parts, mode_pull = jax.vjp(lambda p: mode_parts(p)[0], params)
    w_re, w_im = whole_parts[2], whole_parts[3]
    grad_params = mode_pull(
        (w_re * f_re - w_im * f_im, -(w_re * f_im + w_im * f_re), m_re, -m_im)
    )[0]
    grad_gain1 = (
        jnp.sum(w_re * m_re - w_im * m_im, axis=1) + skip_gain * grad_skip - norm1_bias * grad_bias1
    ) / norm1_gain
    small, at = [], 0
    for length in (ffn_in.shape[1], 2 * features, features, features, features):
        count, wide = share_rows(length, pieces)
        small.append(shares[:, at : at + count, :wide].reshape(length))
        at += count
    bias_in, bias_glu, grad_g2, grad_b2, bias_out = small
    return (
        result, grad_tokens, grad_gain1, grad_bias1, *grad_params, grad_skip,
        sum_glu, bias_glu, grad_g2, grad_b2, sum_in, bias_in, sum_out, bias_out,
    )


def solution(mesh):
    spread_over = P("batch", "seq", None)
    in_specs = (spread_over, P("batch", "seq")) + (P(),) * 18 + (spread_over,)
    rows = P("seq", None)
    out_specs = (spread_over,) * 2 + (P(),) * 10 + (rows,) + (P(),) * 3 + (rows, P(), rows, P())
    return jax.shard_map(
        on_device, mesh=mesh, in_specs=in_specs, out_specs=out_specs, check_vma=False
    )
```

```python
import functools

import jax, jax.numpy as jnp
from jax import lax
from jax.sharding import PartitionSpec as P
from jax.experimental import pallas as pl
from jax.experimental.pallas import tpu as pltpu
F32, BF16 = jnp.float32, jnp.bfloat16
LANES = 128
HALF = 64
FORWARD_UNROLL = 16
BACKWARD_UNROLL = 8
NN = (((1,), (0,)), ((), ()))
NT = (((1,), (1,)), ((), ()))
TN = (((0,), (0,)), ((), ()))


def halves(value):
    high = value.astype(BF16)
    return high, (value - high.astype(F32)).astype(BF16)


def dot(left, right, dims):
    return lax.dot_general(left, right, dims, preferred_element_type=F32)


def beside(parts):
    return jnp.concatenate(parts, axis=1)


def below(parts):
    return jnp.concatenate(parts, axis=0)


def mm(left, right):
    table = beside(right)
    out = dot(beside(left), below([table, table]), NN)
    return out[:, :LANES] + out[:, LANES:]


def mm_turned(left, right):
    out = dot(beside(left), below([beside([right[0]] * 2), beside([right[1]] * 2)]), NT)
    return out[:, :LANES] + out[:, LANES:]


def swap(value):
    return pltpu.roll(value, HALF, value.ndim - 1)


def low_lanes(shape):
    return lax.broadcasted_iota(jnp.int32, shape, len(shape) - 1) < HALF


def as_factor(value):
    turned = swap(value)
    low = low_lanes(value.shape)
    return jnp.where(low, value, turned), jnp.where(low, -turned, value)


def times(value, factor):
    return value * factor[0] + swap(value) * factor[1]


def power_setup(lam, base_ref, fre_ref, fim_ref, steps, channels):
    one = jnp.where(low_lanes(lam.shape), 1.0, 0.0)
    factor = as_factor(lam)
    row = one
    for k in range(8):
        base_ref[pl.ds(k * channels, channels), :] = row
        row = times(row, factor)
    eight = as_factor(row)
    row = one
    for i in range(16):
        fre, fim = as_factor(row)
        fre_ref[pl.ds(i * channels, channels), :] = fre
        fim_ref[pl.ds(i * channels, channels), :] = fim
        row = times(row, eight)
    for s in range(steps):
        fre, fim = as_factor(row)
        fre_ref[pl.ds((16 + s) * channels, channels), :] = fre
        fim_ref[pl.ds((16 + s) * channels, channels), :] = fim
        row = times(row, (fre, fim))


def power_tables(h, base_ref, fre_ref, fim_ref, channels):
    base = base_ref[pl.ds(h, 8, stride=channels), :]
    turned = swap(base)
    return below([
        base * fre_ref[pl.ds(h + i * channels, 1), :] + turned * fim_ref[pl.ds(h + i * channels, 1), :]
        for i in range(16)
    ])


def reversed_tables(h, base_ref, fre_ref, fim_ref, channels):
    base = below([base_ref[pl.ds(h + k * channels, 1), :] for k in range(7, -1, -1)])
    turned = swap(base)
    return below([
        base * fre_ref[pl.ds(h + i * channels, 1), :] + turned * fim_ref[pl.ds(h + i * channels, 1), :]
        for i in range(15, -1, -1)
    ])


def doc_masks(seg_ref, mask_ref, row, pitch, chunks, docs, turn):
    even = seg_ref[pl.ds(row, chunks, stride=2 * pitch), :]
    odd = seg_ref[pl.ds(row + pitch, chunks, stride=2 * pitch), :]
    pair = join(even, odd)
    at = lax.broadcasted_iota(jnp.int32, (LANES, LANES), 0)
    to = lax.broadcasted_iota(jnp.int32, (LANES, LANES), 1)
    turning = jnp.where(at + to == LANES - 1, 1.0, 0.0).astype(BF16)
    for d in range(docs):
        for c in range(2):
            mask = jnp.where(pair[c] == float(d), 1.0, 0.0)
            mask_ref[d * 2 + c] = mask
            if turn:
                mask_ref[(docs + d) * 2 + c] = dot(mask.astype(BF16), turning, NN)


def join(even, odd):
    low = low_lanes(even.shape)
    return jnp.where(low, even, swap(odd)), jnp.where(low, swap(even), odd)


def join_turned(even, odd):
    low = low_lanes(even.shape)
    return jnp.where(low, swap(odd), even), jnp.where(low, odd, swap(even))


def apart_turned(first, second):
    low = low_lanes(first.shape)
    return jnp.where(low, swap(second), first), jnp.where(low, second, swap(first))


def spread(pair, mask_ref, docs, base=0):
    return below([pair[c] * mask_ref[base + d * 2 + c] for d in range(docs) for c in range(2)])


def gathered(rows, mask_ref, chunks, docs, base=0):
    out = []
    for c in range(2):
        total = None
        for d in range(docs):
            at = (d * 2 + c) * chunks
            term = rows[at : at + chunks] * mask_ref[base + d * 2 + c]
            total = term if total is None else total + term
        out.append(total)
    return out


def scan_factors(h, fre_ref, fim_ref, channels, chunks, steps, backward):
    at = lax.broadcasted_iota(jnp.int32, (chunks, LANES), 0)
    out = []
    for s in range(steps):
        keep = at < chunks - (1 << s) if backward else at >= (1 << s)
        fre = fre_ref[pl.ds(h + (16 + s) * channels, 1), :]
        fim = fim_ref[pl.ds(h + (16 + s) * channels, 1), :]
        out.append((jnp.where(keep, fre, 0.0), jnp.where(keep, fim, 0.0)))
    return out


def scan_chunks(rows, factors, chunks, backward):
    at = lax.broadcasted_iota(jnp.int32, (chunks, LANES), 0)
    keep = at < chunks - 1 if backward else at >= 1
    out = []
    for i in range(rows.shape[0] // chunks):
        part = rows[i * chunks : (i + 1) * chunks]
        for s, factor in enumerate(factors):
            moved = pltpu.roll(part, chunks - (1 << s) if backward else 1 << s, 0)
            part = part + times(moved, factor)
        moved = pltpu.roll(part, chunks - 1 if backward else 1, 0)
        out.append(jnp.where(keep, moved, 0.0))
    return jnp.concatenate(out, axis=0)


def toeplitz(row):
    wide = jnp.broadcast_to(row, (LANES, LANES))
    wide = pltpu.roll(wide, 0, 1, stride=1, stride_axis=0)
    j = lax.broadcasted_iota(jnp.int32, (LANES, LANES), 0)
    t = lax.broadcasted_iota(jnp.int32, (LANES, LANES), 1)
    return jnp.where(t >= j, wide, 0.0)


def turned_lag_sums(table):
    moved = pltpu.roll(table, 0, 1, stride=1, stride_axis=0)
    at = lax.broadcasted_iota(jnp.int32, (LANES, LANES), 0)
    lane = lax.broadcasted_iota(jnp.int32, (LANES, LANES), 1)
    return jnp.sum(jnp.where(lane >= at, moved, 0.0), axis=0, keepdims=True)


def together(works):
    while works:
        works = [work for work in works if next(work, None)]


def first_rows(first, second):
    at = lax.broadcasted_iota(jnp.int32, (8, LANES), 0)
    return jnp.where(at == 0, first, jnp.where(at == 1, second, 0.0))


def forward_kernel(
    sizes, recv_ref, lam_ref, weight_ref, skip_ref, out_ref, enter_ref, lag_ref,
    base_ref, fre_ref, fim_ref, mask_ref,
):
    channels, chunks, docs, steps, pitch, unroll = sizes
    rows = docs * 2 * chunks
    power_setup(lam_ref[...], base_ref, fre_ref, fim_ref, steps, channels)
    doc_masks(recv_ref, mask_ref, channels, pitch, chunks, docs, False)

    def one(h):
        pair = join(
            recv_ref[pl.ds(h, chunks, stride=2 * pitch), :],
            recv_ref[pl.ds(h + pitch, chunks, stride=2 * pitch), :],
        )
        inputs = halves(spread(pair, mask_ref, docs))
        power = halves(power_tables(h, base_ref, fre_ref, fim_ref, channels))
        yield True
        back = halves(reversed_tables(h, base_ref, fre_ref, fim_ref, channels))
        weight = weight_ref[pl.ds(h, 1), :]
        low = low_lanes((1, LANES))
        signed = halves(jnp.where(low, weight, -weight))
        both = first_rows(signed[0].astype(F32), signed[1].astype(F32)).astype(BF16)
        yield True
        lags = dot(both, below(power), NT)
        lags = lags[0:1] + lags[1:2]
        lags = lags[:, :LANES] + lags[:, LANES:]
        lag_ref[pl.ds(h, 1), :] = lags
        yield True
        table = halves(toeplitz(lags))
        yield True
        out = dot(below(inputs), beside([back[0], table[0]]), NN)
        out = out[:rows] + out[rows:] + dot(inputs[0], beside([back[1], table[1]]), NN)
        yield True
        enter = scan_chunks(
            out[:, :LANES], scan_factors(h, fre_ref, fim_ref, channels, chunks, steps, False), chunks, False
        )
        enter_ref[h] = enter
        yield True
        lam = as_factor(lam_ref[pl.ds(h, 1), :])
        coef = as_factor(times(weight, lam))
        coef = (jnp.where(low, coef[0], -coef[0]), jnp.where(low, coef[1], -coef[1]))
        yield True
        mixed = out[:, LANES:] + mm_turned(halves(times(enter, coef)), power)
        yield True
        first, second = gathered(mixed, mask_ref, chunks, docs)
        skip = skip_ref[pl.ds(h, 1), :]
        even, odd = join(first + skip * pair[0], second + skip * pair[1])
        out_ref[pl.ds(h, chunks, stride=2 * channels), :] = even
        out_ref[pl.ds(h + channels, chunks, stride=2 * channels), :] = odd

    def several(i, carry):
        together([one(i * unroll + k) for k in range(unroll)])
        return carry

    lax.fori_loop(0, channels // unroll, several, 0)


def backward_kernel(
    sizes, recv_ref, grad_ref, enter_ref, lag_ref, lam_ref, weight_ref, skip_ref,
    out_ref, sum_ref, first_ref, lagsum_ref, bias_ref,
    base_ref, fre_ref, fim_ref, mask_ref,
):
    channels, chunks, docs, steps, pitch, unroll = sizes
    rows = docs * 2 * chunks
    power_setup(lam_ref[...], base_ref, fre_ref, fim_ref, steps, channels)
    doc_masks(recv_ref, mask_ref, channels, pitch, chunks, docs, True)
    reach = (LANES - 1 - lax.broadcasted_iota(jnp.int32, (1, LANES), 1)).astype(F32)

    def one(h):
        pair = join(
            recv_ref[pl.ds(h, chunks, stride=2 * pitch), :],
            recv_ref[pl.ds(h + pitch, chunks, stride=2 * pitch), :],
        )
        gpair = join_turned(
            grad_ref[pl.ds(h, chunks, stride=2 * pitch), :],
            grad_ref[pl.ds(h + pitch, chunks, stride=2 * pitch), :],
        )
        inputs = spread(pair, mask_ref, docs)
        grads = spread(gpair, mask_ref, docs, docs * 2)
        ih, il = halves(inputs)
        gh, gl = halves(grads)
        yield True
        lagsum = turned_lag_sums(dot(below([gh, gl, gh]), below([ih, ih, il]), TN))
        lagsum_ref[pl.ds(h, 1), :] = lagsum
        yield True
        power = halves(power_tables(h, base_ref, fre_ref, fim_ref, channels))
        yield True
        back = halves(reversed_tables(h, base_ref, fre_ref, fim_ref, channels))
        weight = weight_ref[pl.ds(h, 1), :]
        lam = as_factor(lam_ref[pl.ds(h, 1), :])
        yield True
        table = halves(toeplitz(lag_ref[pl.ds(h, 1), :]))
        yield True
        enter = enter_ref[h]
        ahead = scan_factors(h, fre_ref, fim_ref, channels, chunks, steps, False)
        astern = scan_factors(h, fre_ref, fim_ref, channels, chunks, steps, True)
        i1h, i1l = halves(inputs * reach)
        g1h, g1l = halves(grads * reach)
        lh, ll = halves(first_rows(lagsum, lagsum * reach))
        yield True
        out = mm((below([i1h, gh, g1h, lh]), below([i1l, gl, g1l, ll])), back)
        yield True
        hop = (
            fre_ref[pl.ds(h + 16 * channels, 1), :] * float(LANES),
            fim_ref[pl.ds(h + 16 * channels, 1), :] * float(LANES),
        )
        turned = swap(enter)
        enter1 = scan_chunks(
            out[:rows] + enter * hop[0] + turned * hop[1], ahead, chunks, False
        )
        yield True
        seen = out[rows : 2 * rows]
        seen1 = seen + out[2 * rows : 3 * rows]
        seen_t = swap(seen)

        def summed_product(plain, crossed):
            plain = jnp.sum(plain, axis=0, keepdims=True)
            crossed = jnp.sum(crossed, axis=0, keepdims=True)
            low = low_lanes((1, LANES))
            plain, crossed = plain - swap(plain), crossed + swap(crossed)
            return times(jnp.where(low, plain, crossed), lam)

        sum_ref[pl.ds(h, 1), :] = (
            summed_product(enter * seen, turned * seen) + out[3 * rows : 3 * rows + 1]
        )
        first_ref[pl.ds(h, 1), :] = summed_product(
            enter1 * seen + enter * seen1, enter1 * seen_t + turned * seen1
        ) + out[3 * rows + 1 : 3 * rows + 2]
        yield True
        coef = as_factor(times(weight, lam))
        leave = scan_chunks(seen * coef[0] + seen_t * coef[1], astern, chunks, True)
        leave = jnp.where(low_lanes(leave.shape), leave, -leave)
        yield True
        inner = mm((gh, gl), table) + mm_turned(halves(leave), power)
        yield True
        gfirst, gsecond = gathered(inner, mask_ref, chunks, docs, docs * 2)
        skip = skip_ref[pl.ds(h, 1), :]
        gfirst = gfirst + skip * gpair[0]
        gsecond = gsecond + skip * gpair[1]
        bias_ref[pl.ds(h, 1), :] = jnp.sum(gfirst + gsecond, axis=0, keepdims=True)
        even, odd = apart_turned(gfirst, gsecond)
        out_ref[pl.ds(h, chunks, stride=2 * channels), :] = even
        out_ref[pl.ds(h + channels, chunks, stride=2 * channels), :] = odd

    def several(i, carry):
        together([one(i * unroll + k) for k in range(unroll)])
        return carry

    lax.fori_loop(0, channels // unroll, several, 0)


REACH = 512


def kernel_sizes(recv_rows, channels, pieces, docs, unroll):
    chunks = pieces // 2
    unroll = min(channels, max(1, unroll * 64 // (docs * 2 * chunks)))
    steps = min((chunks - 1).bit_length(), (REACH // LANES - 1).bit_length())
    return (channels, chunks, docs, steps, channels + 8, unroll)


def scratch(channels, chunks, docs, steps):
    return [
        pltpu.VMEM((8 * channels, LANES), F32),
        pltpu.VMEM(((16 + steps) * channels, LANES), F32),
        pltpu.VMEM(((16 + steps) * channels, LANES), F32),
        pltpu.VMEM((docs * 4, chunks, LANES), F32),
    ]


def recurrence(recv, lam, weight, skip, pieces, docs, unroll=2):
    channels = lam.shape[0]
    sizes = kernel_sizes(recv.shape[0], channels, pieces, docs, unroll)
    chunks, steps = sizes[1], sizes[3]
    rows = docs * 2 * chunks
    return pl.pallas_call(
        lambda *refs: forward_kernel(sizes, *refs),
        out_shape=(
            jax.ShapeDtypeStruct((pieces * channels, LANES), F32),
            jax.ShapeDtypeStruct((channels, rows, LANES), F32),
            jax.ShapeDtypeStruct((channels, LANES), F32),
        ),
        scratch_shapes=scratch(channels, chunks, docs, steps),
        compiler_params=pltpu.CompilerParams(vmem_limit_bytes=48 << 20),
        cost_estimate=estimate(16),
        name="recurrence",
    )(recv, lam, weight, skip)


def recurrence_back(recv, grad, enter, lags, lam, weight, skip, pieces, docs, unroll=2):
    channels = lam.shape[0]
    sizes = kernel_sizes(recv.shape[0], channels, pieces, docs, unroll)
    chunks, steps = sizes[1], sizes[3]
    row = jax.ShapeDtypeStruct((channels, LANES), F32)
    return pl.pallas_call(
        lambda *refs: backward_kernel(sizes, *refs),
        out_shape=(jax.ShapeDtypeStruct((pieces * channels, LANES), F32), row, row, row, row),
        scratch_shapes=scratch(channels, chunks, docs, steps),
        compiler_params=pltpu.CompilerParams(vmem_limit_bytes=48 << 20),
        cost_estimate=estimate(30),
        name="recurrence_back",
    )(recv, grad, enter, lags, lam, weight, skip)


EPSILON = 1e-05
MIB = 1 << 20


def estimate(micros, moved=0):
    return pl.CostEstimate(flops=int(micros * 1e9), transcendentals=0, bytes_accessed=int(moved))


def bell(values):
    share = 0.5 + 0.5 * lax.erf(values * 0.7071067811865476)
    return share, values * jnp.exp(-0.5 * values * values) * 0.3989422804014327


def sent_rows(values, out_ref, channels):
    turned = values.T
    for s in range(out_ref.shape[0]):
        out_ref[s, 0:channels, :] = turned[s * channels : (s + 1) * channels]


def share_rows(length, pieces):
    share = length // pieces
    return max(1, share // LANES), min(share, LANES)


def share_vectors(refs, out_ref, first):
    pieces = out_ref.shape[0]
    at = first
    for s in range(pieces):
        out_ref[s, first : first + 8, :] = jnp.zeros((8, LANES), F32)
    for ref in refs:
        count, wide = share_rows(ref.shape[1], pieces)
        for s in range(pieces):
            for r in range(count):
                start = (s * count + r) * wide
                out_ref[s, at + r : at + r + 1, :wide] = ref[:, start : start + wide]
        at += count


def normalize(values):
    centre = values - jnp.mean(values, axis=1, keepdims=True)
    recip = lax.rsqrt(jnp.mean(centre * centre, axis=1, keepdims=True) + EPSILON)
    return centre * recip, recip


def norm_back(grad, unit, recip):
    return recip * (
        grad
        - jnp.mean(grad, axis=1, keepdims=True)
        - unit * jnp.mean(grad * unit, axis=1, keepdims=True)
    )


def turning(size):
    at = lax.broadcasted_iota(jnp.int32, (size, size), 0)
    to = lax.broadcasted_iota(jnp.int32, (size, size), 1)
    return jnp.where(at + to == size - 1, 1.0, 0.0).astype(BF16)


def first_kernel(tokens_ref, cot_ref, seg_ref, gain_ref, bias_ref, send_ref, up_ref):
    pieces, pitch, rows = send_ref.shape
    channels = pitch - 8
    unit, _ = normalize(tokens_ref[...].astype(F32))
    sent_rows(unit * gain_ref[...] + bias_ref[...], send_ref, channels)
    seg = jnp.broadcast_to(seg_ref[...].astype(F32), (8, rows))
    for s in range(pieces):
        send_ref[s, channels:pitch, :] = seg
    up_ref[...] = cot_ref[...].astype(F32)


def last_kernel(back_ref, tokens_ref, gain_ref, hidden_ref, out_ref):
    unit, recip = normalize(tokens_ref[...].astype(F32))
    turn = turning(tokens_ref.shape[0])
    high, low = halves(back_ref[...])
    grad = (dot(turn, high, NT) + dot(turn, low, NT)) * gain_ref[...]
    out_ref[...] = (hidden_ref[...] + norm_back(grad, unit, recip)).astype(BF16)


def fetch(source, target, sems, chunks, rows):
    out = []
    wide = source.shape[0 if rows else 1] // chunks
    for i in range(chunks):
        part = (pl.ds(i * wide, wide), slice(None)) if rows else (slice(None), pl.ds(i * wide, wide))
        copy = pltpu.make_async_copy(source.at[part], target.at[part], sems.at[i])
        copy.start()
        out.append(copy)
    return out


def by_core(values, place_ref, out_ref, pieces):
    wide = values.shape[1] // pieces
    for s in range(pieces):
        out_ref[(s % 2) ^ place_ref[0], :, (s // 2) * wide : (s // 2 + 1) * wide] = (
            values[:, s * wide : (s + 1) * wide]
        )


def by_pair(values, place_ref, out_ref, pieces):
    wide = values.shape[1] // pieces
    for s in range(pieces):
        at = (s // 8 * 2 + s // 2 % 2) * wide
        out_ref[(s // 4 % 2) ^ place_ref[3], (s % 2) ^ place_ref[0], :, at : at + wide] = (
            values[:, s * wide : (s + 1) * wide]
        )


def upward_kernel(
    pieces, place_ref, mixed_ref, tokens_ref, glu_bias_ref, gain_ref, bias_ref, ffn_bias_ref, glu_ref, ffn_ref,
    act_ref, z2_ref, keep_here_ref, keep_there_ref, send_here_ref, send_there_ref, pre_ref, hidden_ref, slope1_ref, slope2_ref, low_ref,
    glu_v, ffn_v, parts_ref, glu_sem, ffn_sem, out_sem,
):
    rows, features = tokens_ref.shape
    glu_copies = fetch(glu_ref, glu_v, glu_sem, 4, False)
    ffn_copies = fetch(ffn_ref, ffn_v, ffn_sem, 8, False)
    mixed = mixed_ref[...].T
    share, steep = bell(mixed)
    slope1_ref[...] = share + steep
    act = (mixed * share).astype(BF16)
    by_core(act.astype(F32), place_ref, act_ref, pieces)
    wide = glu_ref.shape[1] // 4
    for i in range(4):
        glu_copies[i].wait()
        at = slice(i * wide, (i + 1) * wide)
        pre_ref[:, at] = (
            jnp.dot(act, glu_v[:, at], preferred_element_type=F32) + glu_bias_ref[:, at]
        )
    hidden = tokens_ref[...].astype(F32) + pre_ref[:, :features] * jax.nn.sigmoid(pre_ref[:, features:])
    hidden_ref[...] = hidden
    unit, _ = normalize(hidden)
    normed = (unit * gain_ref[...] + bias_ref[...]).astype(BF16)
    by_pair(normed.astype(F32), place_ref, z2_ref, pieces)
    wide = ffn_ref.shape[1] // 8
    block = ffn_ref.shape[1] // pieces // 2
    for i in range(8):
        ffn_copies[i].wait()
        at = slice(i * wide, (i + 1) * wide)
        ffn_pre = jnp.dot(normed, ffn_v[:, at], preferred_element_type=F32) + ffn_bias_ref[:, at]
        share, steep = bell(ffn_pre)
        slope2_ref[:, at] = share + steep
        low = (ffn_pre * share).astype(BF16)
        low_ref[:, at] = low
        wider = low.astype(F32)
        for k in range(wide // block):
            index = (i * wide) // block + k
            piece, half = index // 2, index % 2
            parts_ref[
                half ^ place_ref[1], (piece % 2) ^ place_ref[0], :,
                (piece // 2) * block : (piece // 2 + 1) * block,
            ] = wider[:, k * block : (k + 1) * block]
    copies = []
    for k, ref in enumerate((keep_here_ref, keep_there_ref, send_here_ref, send_there_ref)):
        copies.append(pltpu.make_async_copy(parts_ref.at[k // 2, k % 2], ref, out_sem.at[k]))
        copies[-1].start()
    for copy in copies:
        copy.wait()


def store(ref, columns, value):
    ref[:, columns] = value


def downward_kernel(
    place_ref, cot_ref, slope2_ref, hidden_ref, pre_ref, slope1_ref, gain_ref, act_ref, z2_ref,
    out_w_ref, in_w_ref, glu_w_ref,
    in_keep_ref, in_send_ref, glu_keep_ref, glu_send_ref, grad_hidden_ref, turned_ref,
    in_sum_ref, glu_sum_ref, gain_sum_ref, bias_sum_ref, out_sum_ref,
    out_v, in_v, glu_v, parts_ref, out_sem, in_sem, glu_sem, keep_sem, send_sem,
):
    rows, features = cot_ref.shape
    inner = out_w_ref.shape[0]
    wide = inner // 8
    out_copies = fetch(out_w_ref, out_v, out_sem, 8, True)
    in_copies = fetch(in_w_ref, in_v, in_sem, 8, False)
    glu_copies = fetch(glu_w_ref, glu_v, glu_sem, 1, False)
    copies = []

    def pass_on(source, target, sem):
        copies.append(pltpu.make_async_copy(source, target, sem))
        copies[-1].start()

    quarter, half = features // 4, features // 2
    for k in range(2):
        columns = slice(features + k * half, features + (k + 1) * half)
        glu_keep_ref[:, columns] = act_ref[k]
        glu_send_ref[:, columns] = act_ref[k]
        columns = pl.ds(inner + k * quarter, quarter)
        pass_on(z2_ref.at[0, k], in_keep_ref.at[:, columns], keep_sem.at[8 + k])
        pass_on(z2_ref.at[1, k], in_send_ref.at[:, columns], send_sem.at[8 + k])
    cot = cot_ref[...]
    up = cot.astype(F32)
    out_sum_ref[...] = jnp.sum(up, axis=0, keepdims=True)
    total = jnp.zeros((rows, features), F32)
    for i in range(8):
        at = slice(i * wide, (i + 1) * wide)
        out_copies[i].wait()
        grad = lax.dot_general(cot, out_v[at, :], NT, preferred_element_type=F32)
        low = (grad * slope2_ref[:, at]).astype(BF16)
        wider = low.astype(F32)
        in_sum_ref[:, at] = jnp.sum(wider, axis=0, keepdims=True)
        parts_ref[:, at] = wider
        columns = pl.ds(i * wide, wide)
        pass_on(parts_ref.at[:, columns], in_keep_ref.at[:, columns], keep_sem.at[i])
        pass_on(parts_ref.at[:, columns], in_send_ref.at[:, columns], send_sem.at[i])
        in_copies[i].wait()
        total = total + lax.dot_general(low, in_v[:, at], NT, preferred_element_type=F32)
    unit, recip = normalize(hidden_ref[...])
    gain_sum_ref[...] = jnp.sum(total * unit, axis=0, keepdims=True)
    bias_sum_ref[...] = jnp.sum(total, axis=0, keepdims=True)
    grad_hidden = up + norm_back(total * gain_ref[...], unit, recip)
    grad_hidden_ref[...] = grad_hidden
    gate = jax.nn.sigmoid(pre_ref[:, features:])
    first = (grad_hidden * gate).astype(BF16)
    second = (grad_hidden * pre_ref[:, :features] * (gate * (1.0 - gate))).astype(BF16)
    glu_copies[0].wait()
    grad_act = None
    for k, part in enumerate((first, second)):
        wider = part.astype(F32)
        at = slice(k * features, (k + 1) * features)
        glu_sum_ref[:, at] = jnp.sum(wider, axis=0, keepdims=True)
        kept = k ^ place_ref[1] == 0
        columns = slice(0, features)
        pl.when(kept)(functools.partial(store, glu_keep_ref, columns, wider))
        pl.when(jnp.logical_not(kept))(functools.partial(store, glu_send_ref, columns, wider))
        term = lax.dot_general(part, glu_v[:, at], NT, preferred_element_type=F32)
        grad_act = term if grad_act is None else grad_act + term
    turn = turning(rows)
    high, low = halves(grad_act * slope1_ref[...])
    sent_rows(dot(turn, high, NN) + dot(turn, low, NN), turned_ref, turned_ref.shape[1] - 8)
    share_vectors(
        (in_sum_ref, glu_sum_ref, gain_sum_ref, bias_sum_ref, out_sum_ref), turned_ref, turned_ref.shape[1] - 8
    )
    for copy in copies:
        copy.wait()


def product_kernel(spans, by_batch, place_ref, *refs):
    many = 1 + max(at for span in spans for at, _ in span)
    values, outs, scratch_ref = refs[:many], refs[many:-1], refs[-1]
    start = 0
    for k in range(len(spans[0]) - 1):
        total = None
        for span in spans:
            (left, rows), (right, columns) = span[0], span[k + 1]
            term = dot(
                values[left][:, rows].astype(BF16), values[right][:, columns].astype(BF16), TN
            )
            total = term if total is None else total + term
        scratch_ref[:, start : start + total.shape[1]] = total
        start += total.shape[1]
    blocks, height, _ = outs[0].shape
    start = 0
    for k, ref in enumerate(outs):
        wide = ref.shape[2]
        for i in range(blocks):
            if by_batch:
                half = scratch_ref.shape[1] // 2
                columns = pl.ds(pl.multiple_of((place_ref[1] ^ (k % 2)) * half + start, LANES), wide)
                ref[i] = scratch_ref[i * height : (i + 1) * height, columns]
            else:
                block = 2 * i + (place_ref[2] ^ (k % 2))
                ref[i] = scratch_ref[
                    pl.ds(pl.multiple_of(block * height, 8), height), start : start + wide
                ]
        start += k % 2 * wide


SMEM = pl.BlockSpec(memory_space=pltpu.SMEM)
VMEM = pl.BlockSpec(memory_space=pltpu.VMEM)
WHOLE = pl.BlockSpec()
HBM = pl.BlockSpec(memory_space=pltpu.HBM)


def shaped(*shape, dtype=F32):
    return jax.ShapeDtypeStruct(shape, dtype)


def params_of(mib):
    return pltpu.CompilerParams(vmem_limit_bytes=mib * MIB)


def first_norm(tokens, cot, seg, gain, bias, pieces):
    rows, features = tokens.shape
    return pl.pallas_call(
        first_kernel,
        out_shape=(shaped(pieces, features // pieces + 8, rows), shaped(rows, features)),
        compiler_params=params_of(16), cost_estimate=estimate(4), name="first_norm",
    )(tokens, cot, seg, gain, bias)


def last_norm(back, tokens, gain, grad_hidden):
    return pl.pallas_call(
        last_kernel, out_shape=shaped(*tokens.shape, dtype=BF16),
        compiler_params=params_of(16), cost_estimate=estimate(4), name="last_norm",
    )(back, tokens, gain, grad_hidden)


def upward(place, mixed, tokens, glu_bias, gain, bias, ffn_bias, glu_weight, ffn_in, pieces):
    rows, features = tokens.shape
    inner = ffn_in.shape[1]
    return pl.pallas_call(
        lambda *refs: upward_kernel(pieces, *refs),
        in_specs=[SMEM] + [VMEM] * 6 + [HBM] * 2,
        out_specs=(WHOLE, WHOLE) + (HBM,) * 4 + (WHOLE,) * 5,
        out_shape=(
            shaped(2, rows, features // 2), shaped(2, 2, rows, features // 4),
            *(shaped(rows, inner // 4),) * 4, shaped(rows, 2 * features),
            shaped(rows, features), shaped(rows, features), shaped(rows, inner), shaped(rows, inner, dtype=BF16),
        ),
        scratch_shapes=[
            pltpu.VMEM(glu_weight.shape, BF16), pltpu.VMEM(ffn_in.shape, BF16),
            pltpu.VMEM((2, 2, rows, inner // 4), F32),
            pltpu.SemaphoreType.DMA((4,)), pltpu.SemaphoreType.DMA((8,)), pltpu.SemaphoreType.DMA((4,)),
        ],
        compiler_params=params_of(56), cost_estimate=estimate(14), name="upward",
    )(place, mixed, tokens, glu_bias, gain, bias, ffn_bias, glu_weight, ffn_in)


def downward(place, cot, slope2, hidden, pre, slope1, gain, act, z2, ffn_out, ffn_in, glu_weight, pieces):
    rows, features = cot.shape
    inner = ffn_in.shape[1]
    return pl.pallas_call(
        downward_kernel,
        in_specs=[SMEM] + [VMEM] * 8 + [HBM] * 3,
        out_specs=(HBM, HBM) + (WHOLE,) * 4,
        out_shape=(
            shaped(rows, inner + features // 2), shaped(rows, inner + features // 2),
            shaped(rows, 2 * features), shaped(rows, 2 * features),
            shaped(rows, features),
            shaped(pieces, features // pieces + 8, rows),
        ),
        scratch_shapes=[
            pltpu.VMEM((1, inner), F32), pltpu.VMEM((1, 2 * features), F32), pltpu.VMEM((1, features), F32),
            pltpu.VMEM((1, features), F32), pltpu.VMEM((1, features), F32),
            pltpu.VMEM(ffn_out.shape, BF16), pltpu.VMEM(ffn_in.shape, BF16), pltpu.VMEM(glu_weight.shape, BF16),
            pltpu.VMEM((rows, inner), F32),
            pltpu.SemaphoreType.DMA((8,)), pltpu.SemaphoreType.DMA((8,)), pltpu.SemaphoreType.DMA((1,)),
            pltpu.SemaphoreType.DMA((10,)), pltpu.SemaphoreType.DMA((10,)),
        ],
        compiler_params=params_of(56), cost_estimate=estimate(18), name="downward",
    )(place, cot, slope2, hidden, pre, slope1, gain, act, z2, ffn_out, ffn_in, glu_weight)


def products(place, values, spans, tall, wide, blocks, chunks=1, by_batch=False):
    if by_batch:
        out = shaped(blocks, tall // blocks, wide // 2 // chunks)
    else:
        out = shaped(blocks // 2, tall // blocks, wide // chunks)
    return pl.pallas_call(
        lambda *refs: product_kernel(spans, by_batch, *refs),
        in_specs=[SMEM] + [VMEM] * len(values),
        out_shape=(out,) * (2 * chunks),
        scratch_shapes=[pltpu.VMEM((tall, wide), F32)],
        compiler_params=params_of(28), cost_estimate=estimate(4), name="products",
    )(place, *values)


def assemble_kernel(axis, place_ref, *refs):
    parts, out_ref = refs[:-1], refs[-1]
    many = len(parts) // 2
    half = out_ref.shape[axis] // 2
    for k in range(2):
        start = (place_ref[1] ^ k) * half
        for part in parts[k * many : (k + 1) * many]:
            size = part.shape[axis]
            if axis:
                out_ref[:, pl.ds(pl.multiple_of(start, LANES), size)] = part[...]
            else:
                out_ref[pl.ds(pl.multiple_of(start, 8), size), :] = part[...]
            start = start + size


def assembled(place, own, others, axis):
    shape = list(own[0].shape)
    shape[axis] = 2 * sum(part.shape[axis] for part in own)
    return pl.pallas_call(
        functools.partial(assemble_kernel, axis),
        in_specs=[SMEM] + [VMEM] * (len(own) + len(others)),
        out_shape=shaped(*shape), compiler_params=params_of(16), cost_estimate=estimate(1), name="assembled",
    )(place, *own, *others)


def pull_kernel(lengths, place_ref, own_ref, other_ref, *refs):
    out_c, out_b, weight, out_d, out_a, gain_in, bias_in, skip_in, step_in, real_in, freq_in = refs[:11]
    decay_ref, freq_ref, in_re_ref, in_im_ref, out_re_ref, out_im_ref = refs[11:17]
    step_ref, skip_ref, gain_ref, bias_ref = refs[17:21]
    vector_refs, products_ref, slopes_ref = refs[21:-2], refs[-2], refs[-1]
    blocks, pitch, _ = own_ref.shape
    channels = pitch - 8
    first_core = place_ref[0] == 0
    half = LANES // 2
    for s in range(2 * blocks):
        own, other = own_ref[s // 2], other_ref[s // 2]
        here = first_core if s % 2 == 0 else jnp.logical_not(first_core)
        state = jnp.where(here, own, other)
        at = slice(s * channels, (s + 1) * channels)
        total = as_factor(state[:channels, :LANES])
        moment = as_factor(state[:channels, LANES:])
        grad_c = times(out_c[at, :], total)
        out_re_ref[at, :] = grad_c[:, :half]
        out_im_ref[at, :] = -grad_c[:, half:]
        grad_b = times(out_b[at, :], total)
        in_re_ref[at, :] = grad_b[:, :half]
        in_im_ref[at, :] = -grad_b[:, half:]
        table = weight[at, :]
        products_ref[at, :] = table * total[0] + swap(table) * total[1]
        grad_d = times(table, moment) + times(out_d[at, :], total)
        grad_a = times(out_a[at, :], total) + step_in[at, :] * grad_d
        decay_ref[at, :] = real_in[at, :half] * grad_a[:, :half]
        freq_ref[at, :] = -grad_a[:, half:]
        slopes_ref[at, :] = step_in[at, :] * (real_in[at, :] * grad_d - freq_in[at, :] * swap(grad_d))
        columns = slice(s * channels, (s + 1) * channels)
        skip_ref[:, columns] = state[channels : channels + 1, :channels]
        bias_ref[:, columns] = state[channels : channels + 1, channels : 2 * channels]
        row = channels
        for ref, length in zip(vector_refs, lengths):
            count, wide = share_rows(length, 2 * blocks)
            for r in range(count):
                start = (s * count + r) * wide
                ref[:, start : start + wide] = state[row + r : row + r + 1, LANES : LANES + wide]
            row += count
    ones = jnp.where(low_lanes((8, LANES)), 1.0, 0.0).astype(BF16)
    sums = []
    for ref in (slopes_ref, products_ref):
        high, low = halves(ref[...])
        sums.append((dot(ones, high, NT) + dot(ones, low, NT))[0:1])
    step_ref[...] = sums[0]
    gain_ref[...] = (sums[1] + skip_in[...] * skip_ref[...] - bias_in[...] * bias_ref[...]) / gain_in[...]


def pulled(place, own, other, tables, gain, bias, skip, step, real, freq, lengths):
    features = tables[0].shape[0]
    row = shaped(1, features)
    table = shaped(features, LANES // 2)
    return pl.pallas_call(
        functools.partial(pull_kernel, lengths),
        in_specs=[SMEM] + [VMEM] * 13,
        out_shape=(table,) * 6 + (row,) * 4 + tuple(shaped(1, length) for length in lengths),
        scratch_shapes=[pltpu.VMEM((features, LANES), F32)] * 2,
        compiler_params=params_of(32), cost_estimate=estimate(4), name="pulled",
    )(place, own, other, *tables, gain, bias, skip, step, real, freq)


def flipped(value, axis, bit):
    count = lax.axis_size(axis)
    return lax.ppermute(value, axis, [(i, i ^ bit) for i in range(count)])


def summed(value, axes):
    for axis in axes:
        bit = 1
        while bit < lax.axis_size(axis):
            value = value + flipped(value, axis, bit)
            bit *= 2
    return value


def halved(value, dim, which):
    first = lax.index_in_dim(value, 0, dim, keepdims=False)
    second = lax.index_in_dim(value, 1, dim, keepdims=False)
    pick = which == 0
    return jnp.where(pick, first, second), jnp.where(pick, second, first)


def across(value, bit=1):
    return flipped(value, "seq", bit)


def over_batch(value):
    return flipped(value, "batch", 1)


class Halving:
    def __init__(self, keep, got, mine, bits):
        self.keep, self.got, self.mine, self.bits = keep, got, mine, list(bits)

    def step(self):
        bit = self.bits.pop(0)
        blocks = self.keep + self.got
        pairs = blocks.reshape((blocks.shape[0] // 2, 2) + blocks.shape[1:])
        self.keep, send = halved(pairs, 1, (self.mine // bit) % 2)
        self.got = across(send, bit)

    def finish(self):
        while self.bits:
            self.step()
        return (self.keep + self.got)[0]


def tied(works, *others):
    out = lax.optimization_barrier(tuple(work.got for work in works) + others)
    for work, got in zip(works, out):
        work.got = got
    return out[len(works) :]


def times_pair(left, right):
    return left[0] * right[0] - left[1] * right[1], left[0] * right[1] + left[1] * right[0]


def mode_tables(params):
    decay_log, decay_freq, input_re, input_im, output_re, output_im, step_log = params
    step_size = jnp.exp(step_log)[:, None]
    real_part = -jnp.exp(decay_log)
    delta_re = step_size * real_part
    delta_im = step_size * decay_freq
    magnitude = jnp.exp(delta_re)
    lam = (magnitude * jnp.cos(delta_im), magnitude * jnp.sin(delta_im))
    denominator = real_part * real_part + decay_freq * decay_freq
    inverse = (real_part / denominator, -decay_freq / denominator)
    num_re = lam[0] - 1.0
    ratio = (
        (num_re * real_part + lam[1] * decay_freq) / denominator,
        (lam[1] * real_part - num_re * decay_freq) / denominator,
    )
    doubled = (2.0 * output_re, 2.0 * output_im)
    bbar = times_pair(ratio, (input_re, input_im))
    weight = times_pair(doubled, bbar)
    both = times_pair(times_pair(doubled, (input_re, input_im)), inverse)
    tables = (
        (2.0 * bbar[0], 2.0 * bbar[1]),
        times_pair(doubled, ratio),
        weight,
        times_pair(both, lam),
        tuple(-part for part in times_pair(both, ratio)),
    )
    return lam, weight, tables, step_size, real_part


def packed(real, imag):
    return jnp.concatenate([real, imag], axis=1)


def on_device(
    tokens, segments, norm1_gain, norm1_bias, decay_log, decay_freq, input_re, input_im,
    output_re, output_im, step_log, skip_gain, glu_weight, glu_bias, norm2_gain, norm2_bias,
    ffn_in, ffn_in_bias, ffn_out, ffn_out_bias, cotangent,
):
    contexts, piece_len, features = tokens.shape
    rows = contexts * piece_len
    pieces, mine = lax.axis_size("seq"), lax.axis_index("seq")
    channels = features // pieces
    docs = max(1, pieces * piece_len // 256)
    params = (decay_log, decay_freq, input_re, input_im, output_re, output_im, step_log)
    batch_bit = lax.axis_index("batch") % 2
    place = jnp.stack([mine % 2, batch_bit, (mine // 2) % 2, (mine // 4) % 2]).astype(jnp.int32)
    high_bits = [1 << k for k in range(3, pieces.bit_length() - 1)]

    def own(value):
        return lax.dynamic_slice_in_dim(value, mine * channels, channels, 0)

    def row_of(value):
        return jnp.broadcast_to(own(value)[:, None], (channels, LANES))

    def line(value):
        return value.reshape(1, -1)

    def by_channel(value):
        return lax.all_to_all(value, "seq", 0, 0)

    lam_pair, weight_pair = mode_tables(tuple(own(p) for p in params))[:2]
    lam, weight = packed(*lam_pair), packed(*weight_pair)
    skip = row_of(skip_gain)
    flat = tokens.reshape(rows, features)
    cot = cotangent.reshape(rows, features)

    send, up = first_norm(
        flat, cot, segments.reshape(1, rows), line(norm1_gain), line(norm1_bias), pieces
    )
    recv = by_channel(send)
    _, _, tables, step_size, real_part = mode_tables(params)
    tables = tuple(packed(*pair) for pair in tables)
    around = (
        jnp.broadcast_to(step_size, tables[0].shape),
        packed(real_part, real_part),
        packed(decay_freq, decay_freq),
    )
    recv = recv.reshape(pieces * (channels + 8), rows)
    up_x = over_batch(up)
    ups = [up, up_x, across(up), across(up_x)]
    mixed_rows, enter, lags = recurrence(recv, lam, weight, skip, pieces, docs, FORWARD_UNROLL)
    mixed = by_channel(mixed_rows.reshape(pieces, channels, rows))
    mixed, *ups = lax.optimization_barrier((mixed, *ups))
    mixed = mixed.reshape(features, rows)
    act_parts, z2_parts, ffn_here, ffn_there, ffn_send_here, ffn_send_there, glu_pre, hidden, slope1, slope2, ffn_low = upward(
        place, mixed, flat, line(glu_bias), line(norm2_gain), line(norm2_bias), line(ffn_in_bias),
        glu_weight, ffn_in, pieces,
    )
    in_keep, in_send, glu_keep, glu_send, grad_hidden, turned = downward(
        place, cot, slope2, hidden, glu_pre, slope1, line(norm2_gain), act_parts, z2_parts, ffn_out, ffn_in, glu_weight, pieces
    )

    inner = ffn_in.shape[1]
    ffn_x, ffn_xo = over_batch(ffn_send_here), over_batch(ffn_send_there)
    in_z = across(in_send, 4)
    glu_send, ffn_x, ffn_xo = lax.optimization_barrier((glu_send, ffn_x, ffn_xo))
    glu_x = over_batch(glu_send)
    every = slice(None)
    values = [ffn_here, ffn_x, across(ffn_there), across(ffn_xo)] + ups
    spans = [[(i, every), (i + 4, every)] for i in range(4)]
    keep_out, send_out = products(place, values, spans, inner // 4, features, pieces // 2)
    back = by_channel(turned)
    lags, send_out = lax.optimization_barrier((lags, send_out))
    shares = jnp.sum(back[:, channels:], axis=0)
    out = Halving(keep_out, across(send_out, 2), mine, [4] + high_bits)
    grad_rows, sums, firsts, lagsum, bias_part = recurrence_back(
        recv, back.reshape(pieces * (channels + 8), rows), enter, lags, lam, weight, skip,
        pieces, docs, BACKWARD_UNROLL,
    )
    vectors = jnp.concatenate([lagsum[:, LANES - 1], jnp.sum(bias_part, axis=1)]).reshape(1, -1)
    vectors = jnp.pad(vectors, ((0, 7), (0, LANES - vectors.shape[1])))
    vectors = jnp.concatenate([vectors, shares], axis=1)
    state = jnp.concatenate([jnp.concatenate([sums, firsts], axis=1), vectors], axis=0)
    state = summed(state, ("batch",))
    in_c = across(in_keep)
    grad_rows, glu_x, in_z, in_c, state, tables, around = tied(
        [out], grad_rows, glu_x, in_z, in_c, state, tables, around
    )
    out.step()
    grad_normed = by_channel(grad_rows.reshape(pieces, channels, rows)).reshape(features, rows)
    in_keep, out.keep = lax.optimization_barrier((in_keep, out.keep))
    quarter, half = features // 4, features // 2
    values = [in_keep, in_z, in_c, across(in_z)]
    low_half, high_half = slice(0, inner // 2), slice(inner // 2, inner)
    here, there = slice(inner, inner + quarter), slice(inner + quarter, inner + half)
    spans = [[(i, here if i < 2 else there), (i, low_half), (i, high_half)] for i in range(4)]
    keep_a, send_a, keep_b, send_b = products(
        place, values, spans, quarter, inner, pieces // 4, 2, by_batch=True
    )
    first = Halving(keep_a, over_batch(send_a), mine, [2] + high_bits)
    second = Halving(keep_b, over_batch(send_b), mine, [2] + high_bits)
    glu_own = glu_keep
    values = [glu_own, glu_x, across(glu_keep), across(glu_x)]
    here, there = slice(features, features + half), slice(features + half, 2 * features)
    spans = [[(i, here if i < 2 else there), (i, slice(0, features))] for i in range(4)]
    keep_glu, send_glu = products(place, values, spans, half, features, pieces // 2)
    (state,) = tied([out], state)
    out.step()
    glu = Halving(keep_glu, across(send_glu, 2), mine, [4] + high_bits)

    def all_batches(value):
        bit = 2
        while bit < lax.axis_size("batch"):
            value = value + flipped(value, "batch", bit)
            bit *= 2
        return value, over_batch(value)

    groups = [[2 * i + c for i in range(pieces // 2)] for c in range(2)]
    state = jnp.broadcast_to(state[None], (pieces // 2,) + state.shape)
    state = lax.all_to_all(state, "seq", 0, 0, axis_index_groups=groups)

    grad_normed, ffn_low = tied([first], grad_normed, ffn_low)
    first.step()
    ffn_res = jnp.dot(ffn_low, ffn_out, preferred_element_type=F32) + ffn_out_bias
    result = (hidden + ffn_res).astype(BF16).reshape(tokens.shape)
    grad_tokens = last_norm(grad_normed, flat, line(norm1_gain), grad_hidden).reshape(tokens.shape)
    (first.keep,) = tied([glu], first.keep)
    glu.step()

    state, result, grad_tokens = tied([second, first, out, glu], state, result, grad_tokens)
    state_c = across(state)
    second.step()
    first.step()
    half_out, other_out = all_batches(out.finish())
    glu.step()

    lengths = (ffn_in.shape[1], 2 * features, features, features, features)
    small = pulled(
        place, state, state_c, tables, line(norm1_gain), line(norm1_bias), line(skip_gain), *around, lengths
    )
    other_out, *small = tied([second, glu, first], other_out, *small)
    grad_params = small[:6]
    vectors = [value.reshape(-1) for value in small[6:]]
    grad_step, grad_skip, grad_gain1, grad_bias1 = vectors[:4]
    bias_in, bias_glu, grad_g2, grad_b2, bias_out = vectors[4:]
    second.step()
    half_a, other_a = all_batches(first.finish())
    half_glu, other_glu = all_batches(glu.finish())

    other_a, other_glu = tied([second], other_a, other_glu)
    half_b, other_b = all_batches(second.finish())
    sum_out = assembled(place, [half_out], [other_out], 0)
    sum_glu = assembled(place, [half_glu], [other_glu], 1)
    sum_in = assembled(place, [half_a, half_b], [other_a, other_b], 1)
    return (
        result, grad_tokens, grad_gain1, grad_bias1, *grad_params, grad_step, grad_skip,
        sum_glu, bias_glu, grad_g2, grad_b2, sum_in, bias_in, sum_out, bias_out,
    )


def solution(mesh):
    spread_over = P("batch", "seq", None)
    in_specs = (spread_over, P("batch", "seq")) + (P(),) * 18 + (spread_over,)
    rows = P("seq", None)
    out_specs = (spread_over,) * 2 + (P(),) * 10 + (rows,) + (P(),) * 3 + (rows, P(), rows, P())
    return jax.shard_map(
        on_device, mesh=mesh, in_specs=in_specs, out_specs=out_specs, check_vma=False
    )
```

```python
import functools

import jax, jax.numpy as jnp
from jax import lax
from jax.sharding import PartitionSpec as P
from jax.experimental import pallas as pl
from jax.experimental.pallas import tpu as pltpu
F32, BF16 = jnp.float32, jnp.bfloat16
LANES = 128
HALF = 64
FORWARD_UNROLL = 16
BACKWARD_UNROLL = 8
NN = (((1,), (0,)), ((), ()))
NT = (((1,), (1,)), ((), ()))
TN = (((0,), (0,)), ((), ()))


def halves(value):
    high = value.astype(BF16)
    return high, (value - high.astype(F32)).astype(BF16)


def dot(left, right, dims):
    return lax.dot_general(left, right, dims, preferred_element_type=F32)


def beside(parts):
    return jnp.concatenate(parts, axis=1)


def below(parts):
    return jnp.concatenate(parts, axis=0)


def mm(left, right):
    table = beside(right)
    out = dot(beside(left), below([table, table]), NN)
    return out[:, :LANES] + out[:, LANES:]


def mm_turned(left, right):
    out = dot(beside(left), below([beside([right[0]] * 2), beside([right[1]] * 2)]), NT)
    return out[:, :LANES] + out[:, LANES:]


def swap(value):
    return pltpu.roll(value, HALF, value.ndim - 1)


def low_lanes(shape):
    return lax.broadcasted_iota(jnp.int32, shape, len(shape) - 1) < HALF


def as_factor(value):
    turned = swap(value)
    low = low_lanes(value.shape)
    return jnp.where(low, value, turned), jnp.where(low, -turned, value)


def times(value, factor):
    return value * factor[0] + swap(value) * factor[1]


def power_setup(lam, base_ref, fre_ref, fim_ref, steps, channels):
    one = jnp.where(low_lanes(lam.shape), 1.0, 0.0)
    factor = as_factor(lam)
    row = one
    for k in range(8):
        base_ref[pl.ds(k * channels, channels), :] = row
        row = times(row, factor)
    eight = as_factor(row)
    row = one
    for i in range(16):
        fre, fim = as_factor(row)
        fre_ref[pl.ds(i * channels, channels), :] = fre
        fim_ref[pl.ds(i * channels, channels), :] = fim
        row = times(row, eight)
    for s in range(steps):
        fre, fim = as_factor(row)
        fre_ref[pl.ds((16 + s) * channels, channels), :] = fre
        fim_ref[pl.ds((16 + s) * channels, channels), :] = fim
        row = times(row, (fre, fim))


def power_tables(h, base_ref, fre_ref, fim_ref, channels):
    base = base_ref[pl.ds(h, 8, stride=channels), :]
    turned = swap(base)
    return below([
        base * fre_ref[pl.ds(h + i * channels, 1), :] + turned * fim_ref[pl.ds(h + i * channels, 1), :]
        for i in range(16)
    ])


def reversed_tables(h, base_ref, fre_ref, fim_ref, channels):
    base = below([base_ref[pl.ds(h + k * channels, 1), :] for k in range(7, -1, -1)])
    turned = swap(base)
    return below([
        base * fre_ref[pl.ds(h + i * channels, 1), :] + turned * fim_ref[pl.ds(h + i * channels, 1), :]
        for i in range(15, -1, -1)
    ])


def doc_masks(seg_ref, mask_ref, row, pitch, chunks, docs, turn):
    even = seg_ref[pl.ds(row, chunks, stride=2 * pitch), :]
    odd = seg_ref[pl.ds(row + pitch, chunks, stride=2 * pitch), :]
    pair = join(even, odd)
    at = lax.broadcasted_iota(jnp.int32, (LANES, LANES), 0)
    to = lax.broadcasted_iota(jnp.int32, (LANES, LANES), 1)
    turning = jnp.where(at + to == LANES - 1, 1.0, 0.0).astype(BF16)
    for d in range(docs):
        for c in range(2):
            mask = jnp.where(pair[c] == float(d), 1.0, 0.0)
            mask_ref[d * 2 + c] = mask
            if turn:
                mask_ref[(docs + d) * 2 + c] = dot(mask.astype(BF16), turning, NN)


def join(even, odd):
    low = low_lanes(even.shape)
    return jnp.where(low, even, swap(odd)), jnp.where(low, swap(even), odd)


def join_turned(even, odd):
    low = low_lanes(even.shape)
    return jnp.where(low, swap(odd), even), jnp.where(low, odd, swap(even))


def apart_turned(first, second):
    low = low_lanes(first.shape)
    return jnp.where(low, swap(second), first), jnp.where(low, second, swap(first))


def spread(pair, mask_ref, docs, base=0):
    return below([pair[c] * mask_ref[base + d * 2 + c] for d in range(docs) for c in range(2)])


def gathered(rows, mask_ref, chunks, docs, base=0):
    out = []
    for c in range(2):
        total = None
        for d in range(docs):
            at = (d * 2 + c) * chunks
            term = rows[at : at + chunks] * mask_ref[base + d * 2 + c]
            total = term if total is None else total + term
        out.append(total)
    return out


def scan_factors(h, fre_ref, fim_ref, channels, chunks, steps, backward):
    at = lax.broadcasted_iota(jnp.int32, (chunks, LANES), 0)
    out = []
    for s in range(steps):
        keep = at < chunks - (1 << s) if backward else at >= (1 << s)
        fre = fre_ref[pl.ds(h + (16 + s) * channels, 1), :]
        fim = fim_ref[pl.ds(h + (16 + s) * channels, 1), :]
        out.append((jnp.where(keep, fre, 0.0), jnp.where(keep, fim, 0.0)))
    return out


def scan_chunks(rows, factors, chunks, backward):
    at = lax.broadcasted_iota(jnp.int32, (chunks, LANES), 0)
    keep = at < chunks - 1 if backward else at >= 1
    out = []
    for i in range(rows.shape[0] // chunks):
        part = rows[i * chunks : (i + 1) * chunks]
        for s, factor in enumerate(factors):
            moved = pltpu.roll(part, chunks - (1 << s) if backward else 1 << s, 0)
            part = part + times(moved, factor)
        moved = pltpu.roll(part, chunks - 1 if backward else 1, 0)
        out.append(jnp.where(keep, moved, 0.0))
    return jnp.concatenate(out, axis=0)


def toeplitz(row):
    wide = jnp.broadcast_to(row, (LANES, LANES))
    wide = pltpu.roll(wide, 0, 1, stride=1, stride_axis=0)
    j = lax.broadcasted_iota(jnp.int32, (LANES, LANES), 0)
    t = lax.broadcasted_iota(jnp.int32, (LANES, LANES), 1)
    return jnp.where(t >= j, wide, 0.0)


def turned_lag_sums(table):
    moved = pltpu.roll(table, 0, 1, stride=1, stride_axis=0)
    at = lax.broadcasted_iota(jnp.int32, (LANES, LANES), 0)
    lane = lax.broadcasted_iota(jnp.int32, (LANES, LANES), 1)
    return jnp.sum(jnp.where(lane >= at, moved, 0.0), axis=0, keepdims=True)


def together(works):
    while works:
        works = [work for work in works if next(work, None)]


def first_rows(first, second):
    at = lax.broadcasted_iota(jnp.int32, (8, LANES), 0)
    return jnp.where(at == 0, first, jnp.where(at == 1, second, 0.0))


def forward_kernel(
    sizes, recv_ref, lam_ref, weight_ref, skip_ref, out_ref, enter_ref, lag_ref,
    base_ref, fre_ref, fim_ref, mask_ref,
):
    channels, chunks, docs, steps, pitch, unroll = sizes
    rows = docs * 2 * chunks
    power_setup(lam_ref[...], base_ref, fre_ref, fim_ref, steps, channels)
    doc_masks(recv_ref, mask_ref, channels, pitch, chunks, docs, False)

    def one(h):
        pair = join(
            recv_ref[pl.ds(h, chunks, stride=2 * pitch), :],
            recv_ref[pl.ds(h + pitch, chunks, stride=2 * pitch), :],
        )
        inputs = halves(spread(pair, mask_ref, docs))
        power = halves(power_tables(h, base_ref, fre_ref, fim_ref, channels))
        yield True
        back = halves(reversed_tables(h, base_ref, fre_ref, fim_ref, channels))
        weight = weight_ref[pl.ds(h, 1), :]
        low = low_lanes((1, LANES))
        signed = halves(jnp.where(low, weight, -weight))
        both = first_rows(signed[0].astype(F32), signed[1].astype(F32)).astype(BF16)
        yield True
        lags = dot(both, below(power), NT)
        lags = lags[0:1] + lags[1:2]
        lags = lags[:, :LANES] + lags[:, LANES:]
        lag_ref[pl.ds(h, 1), :] = lags
        yield True
        table = halves(toeplitz(lags))
        yield True
        out = dot(below(inputs), beside([back[0], table[0]]), NN)
        out = out[:rows] + out[rows:] + dot(inputs[0], beside([back[1], table[1]]), NN)
        yield True
        enter = scan_chunks(
            out[:, :LANES], scan_factors(h, fre_ref, fim_ref, channels, chunks, steps, False), chunks, False
        )
        enter_ref[h] = enter
        yield True
        lam = as_factor(lam_ref[pl.ds(h, 1), :])
        coef = as_factor(times(weight, lam))
        coef = (jnp.where(low, coef[0], -coef[0]), jnp.where(low, coef[1], -coef[1]))
        yield True
        mixed = out[:, LANES:] + mm_turned(halves(times(enter, coef)), power)
        yield True
        first, second = gathered(mixed, mask_ref, chunks, docs)
        skip = skip_ref[pl.ds(h, 1), :]
        even, odd = join(first + skip * pair[0], second + skip * pair[1])
        out_ref[pl.ds(h, chunks, stride=2 * channels), :] = even
        out_ref[pl.ds(h + channels, chunks, stride=2 * channels), :] = odd

    def several(i, carry):
        together([one(i * unroll + k) for k in range(unroll)])
        return carry

    lax.fori_loop(0, channels // unroll, several, 0)


def backward_kernel(
    sizes, recv_ref, grad_ref, enter_ref, lag_ref, lam_ref, weight_ref, skip_ref,
    out_ref, sum_ref, first_ref, lagsum_ref, bias_ref,
    base_ref, fre_ref, fim_ref, mask_ref,
):
    channels, chunks, docs, steps, pitch, unroll = sizes
    rows = docs * 2 * chunks
    power_setup(lam_ref[...], base_ref, fre_ref, fim_ref, steps, channels)
    doc_masks(recv_ref, mask_ref, channels, pitch, chunks, docs, True)
    reach = (LANES - 1 - lax.broadcasted_iota(jnp.int32, (1, LANES), 1)).astype(F32)

    def one(h):
        pair = join(
            recv_ref[pl.ds(h, chunks, stride=2 * pitch), :],
            recv_ref[pl.ds(h + pitch, chunks, stride=2 * pitch), :],
        )
        gpair = join_turned(
            grad_ref[pl.ds(h, chunks, stride=2 * pitch), :],
            grad_ref[pl.ds(h + pitch, chunks, stride=2 * pitch), :],
        )
        inputs = spread(pair, mask_ref, docs)
        grads = spread(gpair, mask_ref, docs, docs * 2)
        ih, il = halves(inputs)
        gh, gl = halves(grads)
        yield True
        lagsum = turned_lag_sums(dot(below([gh, gl, gh]), below([ih, ih, il]), TN))
        lagsum_ref[pl.ds(h, 1), :] = lagsum
        yield True
        power = halves(power_tables(h, base_ref, fre_ref, fim_ref, channels))
        yield True
        back = halves(reversed_tables(h, base_ref, fre_ref, fim_ref, channels))
        weight = weight_ref[pl.ds(h, 1), :]
        lam = as_factor(lam_ref[pl.ds(h, 1), :])
        yield True
        table = halves(toeplitz(lag_ref[pl.ds(h, 1), :]))
        yield True
        enter = enter_ref[h]
        ahead = scan_factors(h, fre_ref, fim_ref, channels, chunks, steps, False)
        astern = scan_factors(h, fre_ref, fim_ref, channels, chunks, steps, True)
        i1h, i1l = halves(inputs * reach)
        g1h, g1l = halves(grads * reach)
        lh, ll = halves(first_rows(lagsum, lagsum * reach))
        yield True
        out = mm((below([i1h, gh, g1h, lh]), below([i1l, gl, g1l, ll])), back)
        yield True
        hop = (
            fre_ref[pl.ds(h + 16 * channels, 1), :] * float(LANES),
            fim_ref[pl.ds(h + 16 * channels, 1), :] * float(LANES),
        )
        turned = swap(enter)
        enter1 = scan_chunks(
            out[:rows] + enter * hop[0] + turned * hop[1], ahead, chunks, False
        )
        yield True
        seen = out[rows : 2 * rows]
        seen1 = seen + out[2 * rows : 3 * rows]
        seen_t = swap(seen)

        def summed_product(plain, crossed):
            plain = jnp.sum(plain, axis=0, keepdims=True)
            crossed = jnp.sum(crossed, axis=0, keepdims=True)
            low = low_lanes((1, LANES))
            plain, crossed = plain - swap(plain), crossed + swap(crossed)
            return times(jnp.where(low, plain, crossed), lam)

        sum_ref[pl.ds(h, 1), :] = (
            summed_product(enter * seen, turned * seen) + out[3 * rows : 3 * rows + 1]
        )
        first_ref[pl.ds(h, 1), :] = summed_product(
            enter1 * seen + enter * seen1, enter1 * seen_t + turned * seen1
        ) + out[3 * rows + 1 : 3 * rows + 2]
        yield True
        coef = as_factor(times(weight, lam))
        leave = scan_chunks(seen * coef[0] + seen_t * coef[1], astern, chunks, True)
        leave = jnp.where(low_lanes(leave.shape), leave, -leave)
        yield True
        inner = mm((gh, gl), table) + mm_turned(halves(leave), power)
        yield True
        gfirst, gsecond = gathered(inner, mask_ref, chunks, docs, docs * 2)
        skip = skip_ref[pl.ds(h, 1), :]
        gfirst = gfirst + skip * gpair[0]
        gsecond = gsecond + skip * gpair[1]
        bias_ref[pl.ds(h, 1), :] = jnp.sum(gfirst + gsecond, axis=0, keepdims=True)
        even, odd = apart_turned(gfirst, gsecond)
        out_ref[pl.ds(h, chunks, stride=2 * channels), :] = even
        out_ref[pl.ds(h + channels, chunks, stride=2 * channels), :] = odd

    def several(i, carry):
        together([one(i * unroll + k) for k in range(unroll)])
        return carry

    lax.fori_loop(0, channels // unroll, several, 0)


REACH = 512


def kernel_sizes(recv_rows, channels, pieces, docs, unroll):
    chunks = pieces // 2
    unroll = min(channels, max(1, unroll * 64 // (docs * 2 * chunks)))
    steps = min((chunks - 1).bit_length(), (REACH // LANES - 1).bit_length())
    return (channels, chunks, docs, steps, channels + 8, unroll)


def scratch(channels, chunks, docs, steps):
    return [
        pltpu.VMEM((8 * channels, LANES), F32),
        pltpu.VMEM(((16 + steps) * channels, LANES), F32),
        pltpu.VMEM(((16 + steps) * channels, LANES), F32),
        pltpu.VMEM((docs * 4, chunks, LANES), F32),
    ]


def recurrence(recv, lam, weight, skip, pieces, docs, unroll=2):
    channels = lam.shape[0]
    sizes = kernel_sizes(recv.shape[0], channels, pieces, docs, unroll)
    chunks, steps = sizes[1], sizes[3]
    rows = docs * 2 * chunks
    return pl.pallas_call(
        lambda *refs: forward_kernel(sizes, *refs),
        out_shape=(
            jax.ShapeDtypeStruct((pieces * channels, LANES), F32),
            jax.ShapeDtypeStruct((channels, rows, LANES), F32),
            jax.ShapeDtypeStruct((channels, LANES), F32),
        ),
        scratch_shapes=scratch(channels, chunks, docs, steps),
        compiler_params=pltpu.CompilerParams(vmem_limit_bytes=48 << 20),
        cost_estimate=estimate(16),
        name="recurrence",
    )(recv, lam, weight, skip)


def recurrence_back(recv, grad, enter, lags, lam, weight, skip, pieces, docs, unroll=2):
    channels = lam.shape[0]
    sizes = kernel_sizes(recv.shape[0], channels, pieces, docs, unroll)
    chunks, steps = sizes[1], sizes[3]
    row = jax.ShapeDtypeStruct((channels, LANES), F32)
    return pl.pallas_call(
        lambda *refs: backward_kernel(sizes, *refs),
        out_shape=(jax.ShapeDtypeStruct((pieces * channels, LANES), F32), row, row, row, row),
        scratch_shapes=scratch(channels, chunks, docs, steps),
        compiler_params=pltpu.CompilerParams(vmem_limit_bytes=48 << 20),
        cost_estimate=estimate(30),
        name="recurrence_back",
    )(recv, grad, enter, lags, lam, weight, skip)


EPSILON = 1e-05
MIB = 1 << 20


def estimate(micros, moved=0):
    return pl.CostEstimate(flops=int(micros * 1e9), transcendentals=0, bytes_accessed=int(moved))


def bell(values):
    share = 0.5 + 0.5 * lax.erf(values * 0.7071067811865476)
    return share, values * jnp.exp(-0.5 * values * values) * 0.3989422804014327


def sent_rows(values, out_ref, channels):
    turned = values.T
    for s in range(out_ref.shape[0]):
        out_ref[s, 0:channels, :] = turned[s * channels : (s + 1) * channels]


def share_rows(length, pieces):
    share = length // pieces
    return max(1, share // LANES), min(share, LANES)


def share_vectors(refs, out_ref, first):
    pieces = out_ref.shape[0]
    at = first
    for s in range(pieces):
        out_ref[s, first : first + 8, :] = jnp.zeros((8, LANES), F32)
    for ref in refs:
        count, wide = share_rows(ref.shape[1], pieces)
        for s in range(pieces):
            for r in range(count):
                start = (s * count + r) * wide
                out_ref[s, at + r : at + r + 1, :wide] = ref[:, start : start + wide]
        at += count


def normalize(values):
    centre = values - jnp.mean(values, axis=1, keepdims=True)
    recip = lax.rsqrt(jnp.mean(centre * centre, axis=1, keepdims=True) + EPSILON)
    return centre * recip, recip


def norm_back(grad, unit, recip):
    return recip * (
        grad
        - jnp.mean(grad, axis=1, keepdims=True)
        - unit * jnp.mean(grad * unit, axis=1, keepdims=True)
    )


def turning(size):
    at = lax.broadcasted_iota(jnp.int32, (size, size), 0)
    to = lax.broadcasted_iota(jnp.int32, (size, size), 1)
    return jnp.where(at + to == size - 1, 1.0, 0.0).astype(BF16)


def first_kernel(tokens_ref, cot_ref, seg_ref, gain_ref, bias_ref, send_ref, up_ref):
    pieces, pitch, rows = send_ref.shape
    channels = pitch - 8
    unit, _ = normalize(tokens_ref[...].astype(F32))
    sent_rows(unit * gain_ref[...] + bias_ref[...], send_ref, channels)
    seg = jnp.broadcast_to(seg_ref[...].astype(F32), (8, rows))
    for s in range(pieces):
        send_ref[s, channels:pitch, :] = seg
    up_ref[...] = cot_ref[...].astype(F32)


def last_kernel(back_ref, tokens_ref, gain_ref, hidden_ref, out_ref):
    unit, recip = normalize(tokens_ref[...].astype(F32))
    turn = turning(tokens_ref.shape[0])
    high, low = halves(back_ref[...])
    grad = (dot(turn, high, NT) + dot(turn, low, NT)) * gain_ref[...]
    out_ref[...] = (hidden_ref[...] + norm_back(grad, unit, recip)).astype(BF16)


def pieces_of(source, target, sems, chunks, rows):
    out = []
    wide = source.shape[0 if rows else 1] // chunks
    for i in range(chunks):
        part = (pl.ds(i * wide, wide), slice(None)) if rows else (slice(None), pl.ds(i * wide, wide))
        out.append(pltpu.make_async_copy(source.at[part], target.at[part], sems.at[i]))
    return out


class Sender:
    def __init__(self, sems):
        self.sems, self.copies = sems, []

    def send(self, source, target):
        self.copies.append(pltpu.make_async_copy(source, target, self.sems.at[len(self.copies)]))
        self.copies[-1].start()

    def finish(self):
        for copy in self.copies:
            copy.wait()


def by_core(values, place_ref, out_ref, pieces):
    wide = values.shape[1] // pieces
    for s in range(pieces):
        out_ref[(s % 2) ^ place_ref[0], :, (s // 2) * wide : (s // 2 + 1) * wide] = (
            values[:, s * wide : (s + 1) * wide]
        )


def by_pair(values, place_ref, out_ref, pieces):
    wide = values.shape[1] // pieces
    for s in range(pieces):
        at = (s // 8 * 2 + s // 2 % 2) * wide
        out_ref[(s // 4 % 2) ^ place_ref[3], (s % 2) ^ place_ref[0], :, at : at + wide] = (
            values[:, s * wide : (s + 1) * wide]
        )


def upward_kernel(
    pieces, place_ref, mixed_ref, tokens_ref, glu_bias_ref, gain_ref, bias_ref, ffn_bias_ref, glu_ref, ffn_ref,
    act_ref, z2_ref, keep_here_ref, keep_there_ref, send_here_ref, send_there_ref, pre_ref, hidden_ref,
    slope1_ref, slope2_ref, low_ref,
    glu_v, ffn_v, parts_v, act_v, z2_v, pre_v, hidden_v, slope1_v, slope2_v, low_v, glu_sem, ffn_sem, out_sem,
):
    rows, features = tokens_ref.shape
    glu_copies = pieces_of(glu_ref, glu_v, glu_sem, 4, False)
    ffn_copies = pieces_of(ffn_ref, ffn_v, ffn_sem, 8, False)
    for copy in glu_copies + ffn_copies[:2]:
        copy.start()
    sender = Sender(out_sem)
    mixed = mixed_ref[...].T
    share, steep = bell(mixed)
    slope1_v[...] = share + steep
    sender.send(slope1_v, slope1_ref)
    act = (mixed * share).astype(BF16)
    by_core(act.astype(F32), place_ref, act_v, pieces)
    sender.send(act_v, act_ref)
    wide = glu_ref.shape[1] // 4
    for i in range(4):
        glu_copies[i].wait()
        ffn_copies[i + 2].start()
        at = slice(i * wide, (i + 1) * wide)
        pre_v[:, at] = jnp.dot(act, glu_v[:, at], preferred_element_type=F32) + glu_bias_ref[:, at]
    sender.send(pre_v, pre_ref)
    hidden = tokens_ref[...].astype(F32) + pre_v[:, :features] * jax.nn.sigmoid(pre_v[:, features:])
    hidden_v[...] = hidden
    sender.send(hidden_v, hidden_ref)
    unit, _ = normalize(hidden)
    normed = (unit * gain_ref[...] + bias_ref[...]).astype(BF16)
    by_pair(normed.astype(F32), place_ref, z2_v, pieces)
    sender.send(z2_v, z2_ref)
    wide = ffn_ref.shape[1] // 8
    block = ffn_ref.shape[1] // pieces // 2
    for i in range(8):
        ffn_copies[i].wait()
        if 6 <= i + 6 < 8:
            ffn_copies[i + 6].start()
        at = slice(i * wide, (i + 1) * wide)
        ffn_pre = jnp.dot(normed, ffn_v[:, at], preferred_element_type=F32) + ffn_bias_ref[:, at]
        share, steep = bell(ffn_pre)
        slope2_v[:, at] = share + steep
        low = (ffn_pre * share).astype(BF16)
        low_v[:, at] = low
        columns = pl.ds(i * wide, wide)
        sender.send(slope2_v.at[:, columns], slope2_ref.at[:, columns])
        sender.send(low_v.at[:, columns], low_ref.at[:, columns])
        wider = low.astype(F32)
        for k in range(wide // block):
            index = (i * wide) // block + k
            piece, half = index // 2, index % 2
            parts_v[
                half ^ place_ref[1], (piece % 2) ^ place_ref[0], :,
                (piece // 2) * block : (piece // 2 + 1) * block,
            ] = wider[:, k * block : (k + 1) * block]
    for k, ref in enumerate((keep_here_ref, keep_there_ref, send_here_ref, send_there_ref)):
        sender.send(parts_v.at[k // 2, k % 2], ref)
    sender.finish()


def downward_kernel(
    place_ref, cot_ref, slope2_ref, hidden_ref, pre_ref, slope1_ref, gain_ref, act_ref, z2_ref,
    out_w_ref, in_w_ref, glu_w_ref,
    in_keep_ref, in_send_ref, glu_keep_ref, glu_send_ref, grad_hidden_ref, turned_ref,
    in_sum_ref, glu_sum_ref, gain_sum_ref, bias_sum_ref, out_sum_ref,
    out_v, in_v, glu_v, slope2_v, hidden_v, pre_v, slope1_v, parts_v, halves_v, grad_v,
    out_sem, in_sem, slope_sem, one_sem, send_sem, half_sem,
):
    rows, features = cot_ref.shape
    inner = out_w_ref.shape[0]
    wide = inner // 8
    out_copies = pieces_of(out_w_ref, out_v, out_sem, 8, True)
    in_copies = pieces_of(in_w_ref, in_v, in_sem, 8, False)
    slope_copies = pieces_of(slope2_ref, slope2_v, slope_sem, 8, False)
    late = [
        pltpu.make_async_copy(source, target, one_sem.at[k])
        for k, (source, target) in enumerate(
            ((hidden_ref, hidden_v), (pre_ref, pre_v), (slope1_ref, slope1_v), (glu_w_ref, glu_v))
        )
    ]
    ahead = 3
    for i in range(ahead):
        out_copies[i].start()
        slope_copies[i].start()
        in_copies[i].start()
    sender = Sender(send_sem)
    quarter, half = features // 4, features // 2
    for k in range(2):
        columns = pl.ds(features + k * half, half)
        sender.send(act_ref.at[k], glu_keep_ref.at[:, columns])
        sender.send(act_ref.at[k], glu_send_ref.at[:, columns])
        columns = pl.ds(inner + k * quarter, quarter)
        sender.send(z2_ref.at[0, k], in_keep_ref.at[:, columns])
        sender.send(z2_ref.at[1, k], in_send_ref.at[:, columns])
    cot = cot_ref[...]
    up = cot.astype(F32)
    out_sum_ref[...] = jnp.sum(up, axis=0, keepdims=True)
    total = jnp.zeros((rows, features), F32)
    for i in range(8):
        at = slice(i * wide, (i + 1) * wide)
        out_copies[i].wait()
        slope_copies[i].wait()
        in_copies[i].wait()
        if i + ahead < 8:
            out_copies[i + ahead].start()
            slope_copies[i + ahead].start()
            in_copies[i + ahead].start()
        elif i + ahead == 8:
            for copy in late:
                copy.start()
        grad = dot(cot, out_v[at, :], NT)
        low = (grad * slope2_v[:, at]).astype(BF16)
        wider = low.astype(F32)
        in_sum_ref[:, at] = jnp.sum(wider, axis=0, keepdims=True)
        parts_v[:, at] = wider
        columns = pl.ds(i * wide, wide)
        sender.send(parts_v.at[:, columns], in_keep_ref.at[:, columns])
        sender.send(parts_v.at[:, columns], in_send_ref.at[:, columns])
        total = total + dot(low, in_v[:, at], NT)
    for copy in late:
        copy.wait()
    unit, recip = normalize(hidden_v[...])
    gain_sum_ref[...] = jnp.sum(total * unit, axis=0, keepdims=True)
    bias_sum_ref[...] = jnp.sum(total, axis=0, keepdims=True)
    grad_hidden = up + norm_back(total * gain_ref[...], unit, recip)
    grad_v[...] = grad_hidden
    sender.send(grad_v, grad_hidden_ref)
    gate = jax.nn.sigmoid(pre_v[:, features:])
    first = (grad_hidden * gate).astype(BF16)
    second = (grad_hidden * pre_v[:, :features] * (gate * (1.0 - gate))).astype(BF16)
    grad_act = None
    for k, part in enumerate((first, second)):
        wider = part.astype(F32)
        at = slice(k * features, (k + 1) * features)
        glu_sum_ref[:, at] = jnp.sum(wider, axis=0, keepdims=True)
        halves_v[k] = wider
        kept = k ^ place_ref[1] == 0
        for ref, chosen in ((glu_keep_ref, kept), (glu_send_ref, jnp.logical_not(kept))):
            copy = pltpu.make_async_copy(halves_v.at[k], ref.at[:, pl.ds(0, features)], half_sem.at[k])
            pl.when(chosen)(copy.start)
        term = dot(part, glu_v[:, at], NT)
        grad_act = term if grad_act is None else grad_act + term
    turn = turning(rows)
    high, low = halves(grad_act * slope1_v[...])
    sent_rows(dot(turn, high, NN) + dot(turn, low, NN), turned_ref, turned_ref.shape[1] - 8)
    share_vectors(
        (in_sum_ref, glu_sum_ref, gain_sum_ref, bias_sum_ref, out_sum_ref), turned_ref, turned_ref.shape[1] - 8
    )
    for k in range(2):
        pltpu.make_async_copy(halves_v.at[k], glu_keep_ref.at[:, pl.ds(0, features)], half_sem.at[k]).wait()
    sender.finish()


def product_kernel(spans, by_batch, place_ref, *refs):
    many = 1 + max(at for span in spans for at, _ in span)
    values, outs, scratch_ref = refs[:many], refs[many:-1], refs[-1]
    start = 0
    for k in range(len(spans[0]) - 1):
        total = None
        for span in spans:
            (left, rows), (right, columns) = span[0], span[k + 1]
            term = dot(
                values[left][:, rows].astype(BF16), values[right][:, columns].astype(BF16), TN
            )
            total = term if total is None else total + term
        scratch_ref[:, start : start + total.shape[1]] = total
        start += total.shape[1]
    blocks, height, _ = outs[0].shape
    start = 0
    for k, ref in enumerate(outs):
        wide = ref.shape[2]
        for i in range(blocks):
            if by_batch:
                half = scratch_ref.shape[1] // 2
                columns = pl.ds(pl.multiple_of((place_ref[1] ^ (k % 2)) * half + start, LANES), wide)
                ref[i] = scratch_ref[i * height : (i + 1) * height, columns]
            else:
                block = 2 * i + (place_ref[2] ^ (k % 2))
                ref[i] = scratch_ref[
                    pl.ds(pl.multiple_of(block * height, 8), height), start : start + wide
                ]
        start += k % 2 * wide


SMEM = pl.BlockSpec(memory_space=pltpu.SMEM)
VMEM = pl.BlockSpec(memory_space=pltpu.VMEM)
WHOLE = pl.BlockSpec()
HBM = pl.BlockSpec(memory_space=pltpu.HBM)


def shaped(*shape, dtype=F32):
    return jax.ShapeDtypeStruct(shape, dtype)


def params_of(mib):
    return pltpu.CompilerParams(vmem_limit_bytes=mib * MIB)


def first_norm(tokens, cot, seg, gain, bias, pieces):
    rows, features = tokens.shape
    return pl.pallas_call(
        first_kernel,
        out_shape=(shaped(pieces, features // pieces + 8, rows), shaped(rows, features)),
        compiler_params=params_of(16), cost_estimate=estimate(4), name="first_norm",
    )(tokens, cot, seg, gain, bias)


def last_norm(back, tokens, gain, grad_hidden):
    return pl.pallas_call(
        last_kernel, out_shape=shaped(*tokens.shape, dtype=BF16),
        compiler_params=params_of(16), cost_estimate=estimate(4), name="last_norm",
    )(back, tokens, gain, grad_hidden)


def upward(place, mixed, tokens, glu_bias, gain, bias, ffn_bias, glu_weight, ffn_in, pieces):
    rows, features = tokens.shape
    inner = ffn_in.shape[1]
    return pl.pallas_call(
        lambda *refs: upward_kernel(pieces, *refs),
        in_specs=[SMEM] + [VMEM] * 6 + [HBM] * 2,
        out_specs=(HBM,) * 11,
        out_shape=(
            shaped(2, rows, features // 2), shaped(2, 2, rows, features // 4),
            *(shaped(rows, inner // 4),) * 4, shaped(rows, 2 * features),
            shaped(rows, features), shaped(rows, features), shaped(rows, inner), shaped(rows, inner, dtype=BF16),
        ),
        scratch_shapes=[
            pltpu.VMEM(glu_weight.shape, BF16), pltpu.VMEM(ffn_in.shape, BF16),
            pltpu.VMEM((2, 2, rows, inner // 4), F32), pltpu.VMEM((2, rows, features // 2), F32),
            pltpu.VMEM((2, 2, rows, features // 4), F32), pltpu.VMEM((rows, 2 * features), F32),
            pltpu.VMEM((rows, features), F32), pltpu.VMEM((rows, features), F32),
            pltpu.VMEM((rows, inner), F32), pltpu.VMEM((rows, inner), BF16),
            pltpu.SemaphoreType.DMA((4,)), pltpu.SemaphoreType.DMA((8,)), pltpu.SemaphoreType.DMA((25,)),
        ],
        compiler_params=params_of(56), cost_estimate=estimate(14), name="upward",
    )(place, mixed, tokens, glu_bias, gain, bias, ffn_bias, glu_weight, ffn_in)


def downward(place, cot, slope2, hidden, pre, slope1, gain, act, z2, ffn_out, ffn_in, glu_weight, pieces):
    rows, features = cot.shape
    inner = ffn_in.shape[1]
    return pl.pallas_call(
        downward_kernel,
        in_specs=[SMEM, VMEM] + [HBM] * 4 + [VMEM] * 3 + [HBM] * 3,
        out_specs=(HBM,) * 5 + (WHOLE,),
        out_shape=(
            shaped(rows, inner + features // 2), shaped(rows, inner + features // 2),
            shaped(rows, 2 * features), shaped(rows, 2 * features),
            shaped(rows, features),
            shaped(pieces, features // pieces + 8, rows),
        ),
        scratch_shapes=[
            pltpu.VMEM((1, inner), F32), pltpu.VMEM((1, 2 * features), F32), pltpu.VMEM((1, features), F32),
            pltpu.VMEM((1, features), F32), pltpu.VMEM((1, features), F32),
            pltpu.VMEM(ffn_out.shape, BF16), pltpu.VMEM(ffn_in.shape, BF16), pltpu.VMEM(glu_weight.shape, BF16),
            pltpu.VMEM((rows, inner), F32), pltpu.VMEM((rows, features), F32),
            pltpu.VMEM((rows, 2 * features), F32), pltpu.VMEM((rows, features), F32),
            pltpu.VMEM((rows, inner), F32), pltpu.VMEM((2, rows, features), F32), pltpu.VMEM((rows, features), F32),
            pltpu.SemaphoreType.DMA((8,)), pltpu.SemaphoreType.DMA((8,)), pltpu.SemaphoreType.DMA((8,)),
            pltpu.SemaphoreType.DMA((4,)), pltpu.SemaphoreType.DMA((25,)), pltpu.SemaphoreType.DMA((2,)),
        ],
        compiler_params=params_of(56), cost_estimate=estimate(18), name="downward",
    )(place, cot, slope2, hidden, pre, slope1, gain, act, z2, ffn_out, ffn_in, glu_weight)


def products(place, values, spans, tall, wide, blocks, chunks=1, by_batch=False):
    if by_batch:
        out = shaped(blocks, tall // blocks, wide // 2 // chunks)
    else:
        out = shaped(blocks // 2, tall // blocks, wide // chunks)
    return pl.pallas_call(
        lambda *refs: product_kernel(spans, by_batch, *refs),
        in_specs=[SMEM] + [VMEM] * len(values),
        out_shape=(out,) * (2 * chunks),
        scratch_shapes=[pltpu.VMEM((tall, wide), F32)],
        compiler_params=params_of(28), cost_estimate=estimate(4), name="products",
    )(place, *values)


def assemble_kernel(axis, place_ref, *refs):
    parts, out_ref = refs[:-1], refs[-1]
    many = len(parts) // 2
    half = out_ref.shape[axis] // 2
    for k in range(2):
        start = (place_ref[1] ^ k) * half
        for part in parts[k * many : (k + 1) * many]:
            size = part.shape[axis]
            if axis:
                out_ref[:, pl.ds(pl.multiple_of(start, LANES), size)] = part[...]
            else:
                out_ref[pl.ds(pl.multiple_of(start, 8), size), :] = part[...]
            start = start + size


def assembled(place, own, others, axis):
    shape = list(own[0].shape)
    shape[axis] = 2 * sum(part.shape[axis] for part in own)
    return pl.pallas_call(
        functools.partial(assemble_kernel, axis),
        in_specs=[SMEM] + [VMEM] * (len(own) + len(others)),
        out_shape=shaped(*shape), compiler_params=params_of(16), cost_estimate=estimate(1), name="assembled",
    )(place, *own, *others)


def pull_kernel(lengths, place_ref, own_ref, other_ref, *refs):
    out_c, out_b, weight, out_d, out_a, gain_in, bias_in, skip_in, step_in, real_in, freq_in = refs[:11]
    decay_ref, freq_ref, in_re_ref, in_im_ref, out_re_ref, out_im_ref = refs[11:17]
    step_ref, skip_ref, gain_ref, bias_ref = refs[17:21]
    vector_refs, products_ref, slopes_ref = refs[21:-2], refs[-2], refs[-1]
    blocks, pitch, _ = own_ref.shape
    channels = pitch - 8
    first_core = place_ref[0] == 0
    half = LANES // 2
    for s in range(2 * blocks):
        own, other = own_ref[s // 2], other_ref[s // 2]
        here = first_core if s % 2 == 0 else jnp.logical_not(first_core)
        state = jnp.where(here, own, other)
        at = slice(s * channels, (s + 1) * channels)
        total = as_factor(state[:channels, :LANES])
        moment = as_factor(state[:channels, LANES:])
        grad_c = times(out_c[at, :], total)
        out_re_ref[at, :] = grad_c[:, :half]
        out_im_ref[at, :] = -grad_c[:, half:]
        grad_b = times(out_b[at, :], total)
        in_re_ref[at, :] = grad_b[:, :half]
        in_im_ref[at, :] = -grad_b[:, half:]
        table = weight[at, :]
        products_ref[at, :] = table * total[0] + swap(table) * total[1]
        grad_d = times(table, moment) + times(out_d[at, :], total)
        grad_a = times(out_a[at, :], total) + step_in[at, :] * grad_d
        decay_ref[at, :] = real_in[at, :half] * grad_a[:, :half]
        freq_ref[at, :] = -grad_a[:, half:]
        slopes_ref[at, :] = step_in[at, :] * (real_in[at, :] * grad_d - freq_in[at, :] * swap(grad_d))
        columns = slice(s * channels, (s + 1) * channels)
        skip_ref[:, columns] = state[channels : channels + 1, :channels]
        bias_ref[:, columns] = state[channels : channels + 1, channels : 2 * channels]
        row = channels
        for ref, length in zip(vector_refs, lengths):
            count, wide = share_rows(length, 2 * blocks)
            for r in range(count):
                start = (s * count + r) * wide
                ref[:, start : start + wide] = state[row + r : row + r + 1, LANES : LANES + wide]
            row += count
    ones = jnp.where(low_lanes((8, LANES)), 1.0, 0.0).astype(BF16)
    sums = []
    for ref in (slopes_ref, products_ref):
        high, low = halves(ref[...])
        sums.append((dot(ones, high, NT) + dot(ones, low, NT))[0:1])
    step_ref[...] = sums[0]
    gain_ref[...] = (sums[1] + skip_in[...] * skip_ref[...] - bias_in[...] * bias_ref[...]) / gain_in[...]


def pulled(place, own, other, tables, gain, bias, skip, step, real, freq, lengths):
    features = tables[0].shape[0]
    row = shaped(1, features)
    table = shaped(features, LANES // 2)
    return pl.pallas_call(
        functools.partial(pull_kernel, lengths),
        in_specs=[SMEM] + [VMEM] * 13,
        out_shape=(table,) * 6 + (row,) * 4 + tuple(shaped(1, length) for length in lengths),
        scratch_shapes=[pltpu.VMEM((features, LANES), F32)] * 2,
        compiler_params=params_of(32), cost_estimate=estimate(4), name="pulled",
    )(place, own, other, *tables, gain, bias, skip, step, real, freq)


def flipped(value, axis, bit):
    count = lax.axis_size(axis)
    return lax.ppermute(value, axis, [(i, i ^ bit) for i in range(count)])


def summed(value, axes):
    for axis in axes:
        bit = 1
        while bit < lax.axis_size(axis):
            value = value + flipped(value, axis, bit)
            bit *= 2
    return value


def halved(value, dim, which):
    first = lax.index_in_dim(value, 0, dim, keepdims=False)
    second = lax.index_in_dim(value, 1, dim, keepdims=False)
    pick = which == 0
    return jnp.where(pick, first, second), jnp.where(pick, second, first)


def across(value, bit=1):
    return flipped(value, "seq", bit)


def over_batch(value):
    return flipped(value, "batch", 1)


class Halving:
    def __init__(self, keep, got, mine, bits):
        self.keep, self.got, self.mine, self.bits = keep, got, mine, list(bits)

    def step(self):
        bit = self.bits.pop(0)
        blocks = self.keep + self.got
        pairs = blocks.reshape((blocks.shape[0] // 2, 2) + blocks.shape[1:])
        self.keep, send = halved(pairs, 1, (self.mine // bit) % 2)
        self.got = across(send, bit)

    def finish(self):
        while self.bits:
            self.step()
        return (self.keep + self.got)[0]


def tied(works, *others):
    out = lax.optimization_barrier(tuple(work.got for work in works) + others)
    for work, got in zip(works, out):
        work.got = got
    return out[len(works) :]


def times_pair(left, right):
    return left[0] * right[0] - left[1] * right[1], left[0] * right[1] + left[1] * right[0]


def mode_tables(params):
    decay_log, decay_freq, input_re, input_im, output_re, output_im, step_log = params
    step_size = jnp.exp(step_log)[:, None]
    real_part = -jnp.exp(decay_log)
    delta_re = step_size * real_part
    delta_im = step_size * decay_freq
    magnitude = jnp.exp(delta_re)
    lam = (magnitude * jnp.cos(delta_im), magnitude * jnp.sin(delta_im))
    denominator = real_part * real_part + decay_freq * decay_freq
    inverse = (real_part / denominator, -decay_freq / denominator)
    num_re = lam[0] - 1.0
    ratio = (
        (num_re * real_part + lam[1] * decay_freq) / denominator,
        (lam[1] * real_part - num_re * decay_freq) / denominator,
    )
    doubled = (2.0 * output_re, 2.0 * output_im)
    bbar = times_pair(ratio, (input_re, input_im))
    weight = times_pair(doubled, bbar)
    both = times_pair(times_pair(doubled, (input_re, input_im)), inverse)
    tables = (
        (2.0 * bbar[0], 2.0 * bbar[1]),
        times_pair(doubled, ratio),
        weight,
        times_pair(both, lam),
        tuple(-part for part in times_pair(both, ratio)),
    )
    return lam, weight, tables, step_size, real_part


def packed(real, imag):
    return jnp.concatenate([real, imag], axis=1)


def on_device(
    tokens, segments, norm1_gain, norm1_bias, decay_log, decay_freq, input_re, input_im,
    output_re, output_im, step_log, skip_gain, glu_weight, glu_bias, norm2_gain, norm2_bias,
    ffn_in, ffn_in_bias, ffn_out, ffn_out_bias, cotangent,
):
    contexts, piece_len, features = tokens.shape
    rows = contexts * piece_len
    pieces, mine = lax.axis_size("seq"), lax.axis_index("seq")
    channels = features // pieces
    docs = max(1, pieces * piece_len // 256)
    params = (decay_log, decay_freq, input_re, input_im, output_re, output_im, step_log)
    batch_bit = lax.axis_index("batch") % 2
    place = jnp.stack([mine % 2, batch_bit, (mine // 2) % 2, (mine // 4) % 2]).astype(jnp.int32)
    high_bits = [1 << k for k in range(3, pieces.bit_length() - 1)]

    def own(value):
        return lax.dynamic_slice_in_dim(value, mine * channels, channels, 0)

    def row_of(value):
        return jnp.broadcast_to(own(value)[:, None], (channels, LANES))

    def line(value):
        return value.reshape(1, -1)

    def by_channel(value):
        return lax.all_to_all(value, "seq", 0, 0)

    lam_pair, weight_pair = mode_tables(tuple(own(p) for p in params))[:2]
    lam, weight = packed(*lam_pair), packed(*weight_pair)
    skip = row_of(skip_gain)
    flat = tokens.reshape(rows, features)
    cot = cotangent.reshape(rows, features)

    send, up = first_norm(
        flat, cot, segments.reshape(1, rows), line(norm1_gain), line(norm1_bias), pieces
    )
    recv = by_channel(send)
    _, _, tables, step_size, real_part = mode_tables(params)
    recv = recv.reshape(pieces * (channels + 8), rows)
    up_x = over_batch(up)
    ups = [up, up_x, across(up), across(up_x)]
    mixed_rows, enter, lags = recurrence(recv, lam, weight, skip, pieces, docs, FORWARD_UNROLL)
    mixed = by_channel(mixed_rows.reshape(pieces, channels, rows))
    mixed, tables, *ups = lax.optimization_barrier((mixed, tables, *ups))
    mixed = mixed.reshape(features, rows)
    act_parts, z2_parts, ffn_here, ffn_there, ffn_send_here, ffn_send_there, glu_pre, hidden, slope1, slope2, ffn_low = upward(
        place, mixed, flat, line(glu_bias), line(norm2_gain), line(norm2_bias), line(ffn_in_bias),
        glu_weight, ffn_in, pieces,
    )
    in_keep, in_send, glu_keep, glu_send, grad_hidden, turned = downward(
        place, cot, slope2, hidden, glu_pre, slope1, line(norm2_gain), act_parts, z2_parts, ffn_out, ffn_in, glu_weight, pieces
    )

    inner = ffn_in.shape[1]
    ffn_x, ffn_xo = over_batch(ffn_send_here), over_batch(ffn_send_there)
    in_z = across(in_send, 4)
    glu_send, ffn_x, ffn_xo = lax.optimization_barrier((glu_send, ffn_x, ffn_xo))
    glu_x = over_batch(glu_send)
    every = slice(None)
    values = [ffn_here, ffn_x, across(ffn_there), across(ffn_xo)] + ups
    spans = [[(i, every), (i + 4, every)] for i in range(4)]
    keep_out, send_out = products(place, values, spans, inner // 4, features, pieces // 2)
    back = by_channel(turned)
    lags, send_out = lax.optimization_barrier((lags, send_out))
    shares = jnp.sum(back[:, channels:], axis=0)
    out = Halving(keep_out, across(send_out, 2), mine, [4] + high_bits)
    grad_rows, sums, firsts, lagsum, bias_part = recurrence_back(
        recv, back.reshape(pieces * (channels + 8), rows), enter, lags, lam, weight, skip,
        pieces, docs, BACKWARD_UNROLL,
    )
    sums, tables, step_size, real_part = lax.optimization_barrier((sums, tables, step_size, real_part))
    tables = tuple(packed(*pair) for pair in tables)
    around = (
        jnp.broadcast_to(step_size, tables[0].shape),
        packed(real_part, real_part),
        packed(decay_freq, decay_freq),
    )
    vectors = jnp.concatenate([lagsum[:, LANES - 1], jnp.sum(bias_part, axis=1)]).reshape(1, -1)
    vectors = jnp.pad(vectors, ((0, 7), (0, LANES - vectors.shape[1])))
    vectors = jnp.concatenate([vectors, shares], axis=1)
    state = jnp.concatenate([jnp.concatenate([sums, firsts], axis=1), vectors], axis=0)
    state = summed(state, ("batch",))
    in_c = across(in_keep)
    grad_rows, glu_x, in_z, in_c, state, tables, around = tied(
        [out], grad_rows, glu_x, in_z, in_c, state, tables, around
    )
    out.step()
    grad_normed = by_channel(grad_rows.reshape(pieces, channels, rows)).reshape(features, rows)
    in_keep, out.keep = lax.optimization_barrier((in_keep, out.keep))
    quarter, half = features // 4, features // 2
    values = [in_keep, in_z, in_c, across(in_z)]
    low_half, high_half = slice(0, inner // 2), slice(inner // 2, inner)
    here, there = slice(inner, inner + quarter), slice(inner + quarter, inner + half)
    spans = [[(i, here if i < 2 else there), (i, low_half), (i, high_half)] for i in range(4)]
    keep_a, send_a, keep_b, send_b = products(
        place, values, spans, quarter, inner, pieces // 4, 2, by_batch=True
    )
    first = Halving(keep_a, over_batch(send_a), mine, [2] + high_bits)
    second = Halving(keep_b, over_batch(send_b), mine, [2] + high_bits)
    glu_own = glu_keep
    values = [glu_own, glu_x, across(glu_keep), across(glu_x)]
    here, there = slice(features, features + half), slice(features + half, 2 * features)
    spans = [[(i, here if i < 2 else there), (i, slice(0, features))] for i in range(4)]
    keep_glu, send_glu = products(place, values, spans, half, features, pieces // 2)
    (state,) = tied([out], state)
    out.step()
    glu = Halving(keep_glu, across(send_glu, 2), mine, [4] + high_bits)

    def all_batches(value):
        bit = 2
        while bit < lax.axis_size("batch"):
            value = value + flipped(value, "batch", bit)
            bit *= 2
        return value, over_batch(value)

    groups = [[2 * i + c for i in range(pieces // 2)] for c in range(2)]
    state = jnp.broadcast_to(state[None], (pieces // 2,) + state.shape)
    state = lax.all_to_all(state, "seq", 0, 0, axis_index_groups=groups)

    grad_normed, ffn_low = tied([first], grad_normed, ffn_low)
    first.step()
    ffn_res = jnp.dot(ffn_low, ffn_out, preferred_element_type=F32) + ffn_out_bias
    result = (hidden + ffn_res).astype(BF16).reshape(tokens.shape)
    grad_tokens = last_norm(grad_normed, flat, line(norm1_gain), grad_hidden).reshape(tokens.shape)
    (first.keep,) = tied([glu], first.keep)
    glu.step()

    state, result, grad_tokens = tied([second, first, out, glu], state, result, grad_tokens)
    state_c = across(state)
    second.step()
    first.step()
    half_out, other_out = all_batches(out.finish())
    glu.step()

    lengths = (ffn_in.shape[1], 2 * features, features, features, features)
    small = pulled(
        place, state, state_c, tables, line(norm1_gain), line(norm1_bias), line(skip_gain), *around, lengths
    )
    other_out, *small = tied([second, glu, first], other_out, *small)
    grad_params = small[:6]
    vectors = [value.reshape(-1) for value in small[6:]]
    grad_step, grad_skip, grad_gain1, grad_bias1 = vectors[:4]
    bias_in, bias_glu, grad_g2, grad_b2, bias_out = vectors[4:]
    second.step()
    half_a, other_a = all_batches(first.finish())
    half_glu, other_glu = all_batches(glu.finish())

    other_a, other_glu = tied([second], other_a, other_glu)
    half_b, other_b = all_batches(second.finish())
    sum_out = assembled(place, [half_out], [other_out], 0)
    sum_glu = assembled(place, [half_glu], [other_glu], 1)
    sum_in = assembled(place, [half_a, half_b], [other_a, other_b], 1)
    return (
        result, grad_tokens, grad_gain1, grad_bias1, *grad_params, grad_step, grad_skip,
        sum_glu, bias_glu, grad_g2, grad_b2, sum_in, bias_in, sum_out, bias_out,
    )


def solution(mesh):
    spread_over = P("batch", "seq", None)
    in_specs = (spread_over, P("batch", "seq")) + (P(),) * 18 + (spread_over,)
    rows = P("seq", None)
    out_specs = (spread_over,) * 2 + (P(),) * 10 + (rows,) + (P(),) * 3 + (rows, P(), rows, P())
    return jax.shard_map(
        on_device, mesh=mesh, in_specs=in_specs, out_specs=out_specs, check_vma=False
    )
```

```python
import functools

import jax, jax.numpy as jnp
from jax import lax
from jax.sharding import PartitionSpec as P
from jax.experimental import pallas as pl
from jax.experimental.pallas import tpu as pltpu
F32, BF16 = jnp.float32, jnp.bfloat16
LANES = 128
HALF = 64
FORWARD_UNROLL = 16
BACKWARD_UNROLL = 8
NN = (((1,), (0,)), ((), ()))
NT = (((1,), (1,)), ((), ()))
TN = (((0,), (0,)), ((), ()))


def halves(value):
    high = value.astype(BF16)
    return high, (value - high.astype(F32)).astype(BF16)


def dot(left, right, dims):
    return lax.dot_general(left, right, dims, preferred_element_type=F32)


def beside(parts):
    return jnp.concatenate(parts, axis=1)


def below(parts):
    return jnp.concatenate(parts, axis=0)


def mm(left, right):
    table = beside(right)
    out = dot(beside(left), below([table, table]), NN)
    return out[:, :LANES] + out[:, LANES:]


def mm_turned(left, right):
    out = dot(beside(left), below([beside([right[0]] * 2), beside([right[1]] * 2)]), NT)
    return out[:, :LANES] + out[:, LANES:]


def swap(value):
    return pltpu.roll(value, HALF, value.ndim - 1)


def low_lanes(shape):
    return lax.broadcasted_iota(jnp.int32, shape, len(shape) - 1) < HALF


def as_factor(value):
    turned = swap(value)
    low = low_lanes(value.shape)
    return jnp.where(low, value, turned), jnp.where(low, -turned, value)


def times(value, factor):
    return value * factor[0] + swap(value) * factor[1]


def power_setup(lam, base_ref, fre_ref, fim_ref, steps, channels):
    one = jnp.where(low_lanes(lam.shape), 1.0, 0.0)
    factor = as_factor(lam)
    row = one
    for k in range(8):
        base_ref[pl.ds(k * channels, channels), :] = row
        row = times(row, factor)
    eight = as_factor(row)
    row = one
    for i in range(16):
        fre, fim = as_factor(row)
        fre_ref[pl.ds(i * channels, channels), :] = fre
        fim_ref[pl.ds(i * channels, channels), :] = fim
        row = times(row, eight)
    for s in range(steps):
        fre, fim = as_factor(row)
        fre_ref[pl.ds((16 + s) * channels, channels), :] = fre
        fim_ref[pl.ds((16 + s) * channels, channels), :] = fim
        row = times(row, (fre, fim))


def power_tables(h, base_ref, fre_ref, fim_ref, channels):
    base = base_ref[pl.ds(h, 8, stride=channels), :]
    turned = swap(base)
    return below([
        base * fre_ref[pl.ds(h + i * channels, 1), :] + turned * fim_ref[pl.ds(h + i * channels, 1), :]
        for i in range(16)
    ])


def reversed_tables(h, base_ref, fre_ref, fim_ref, channels):
    base = below([base_ref[pl.ds(h + k * channels, 1), :] for k in range(7, -1, -1)])
    turned = swap(base)
    return below([
        base * fre_ref[pl.ds(h + i * channels, 1), :] + turned * fim_ref[pl.ds(h + i * channels, 1), :]
        for i in range(15, -1, -1)
    ])


def doc_masks(seg_ref, mask_ref, row, pitch, chunks, docs, turn):
    even = seg_ref[pl.ds(row, chunks, stride=2 * pitch), :]
    odd = seg_ref[pl.ds(row + pitch, chunks, stride=2 * pitch), :]
    pair = join(even, odd)
    at = lax.broadcasted_iota(jnp.int32, (LANES, LANES), 0)
    to = lax.broadcasted_iota(jnp.int32, (LANES, LANES), 1)
    turning = jnp.where(at + to == LANES - 1, 1.0, 0.0).astype(BF16)
    for d in range(docs):
        for c in range(2):
            mask = jnp.where(pair[c] == float(d), 1.0, 0.0)
            mask_ref[d * 2 + c] = mask
            if turn:
                mask_ref[(docs + d) * 2 + c] = dot(mask.astype(BF16), turning, NN)


def join(even, odd):
    low = low_lanes(even.shape)
    return jnp.where(low, even, swap(odd)), jnp.where(low, swap(even), odd)


def join_turned(even, odd):
    low = low_lanes(even.shape)
    return jnp.where(low, swap(odd), even), jnp.where(low, odd, swap(even))


def apart_turned(first, second):
    low = low_lanes(first.shape)
    return jnp.where(low, swap(second), first), jnp.where(low, second, swap(first))


def spread(pair, mask_ref, docs, base=0):
    return below([pair[c] * mask_ref[base + d * 2 + c] for d in range(docs) for c in range(2)])


def gathered(rows, mask_ref, chunks, docs, base=0):
    out = []
    for c in range(2):
        total = None
        for d in range(docs):
            at = (d * 2 + c) * chunks
            term = rows[at : at + chunks] * mask_ref[base + d * 2 + c]
            total = term if total is None else total + term
        out.append(total)
    return out


def scan_factors(h, fre_ref, fim_ref, channels, chunks, steps, backward):
    at = lax.broadcasted_iota(jnp.int32, (chunks, LANES), 0)
    out = []
    for s in range(steps):
        keep = at < chunks - (1 << s) if backward else at >= (1 << s)
        fre = fre_ref[pl.ds(h + (16 + s) * channels, 1), :]
        fim = fim_ref[pl.ds(h + (16 + s) * channels, 1), :]
        out.append((jnp.where(keep, fre, 0.0), jnp.where(keep, fim, 0.0)))
    return out


def scan_chunks(rows, factors, chunks, backward):
    at = lax.broadcasted_iota(jnp.int32, (chunks, LANES), 0)
    keep = at < chunks - 1 if backward else at >= 1
    out = []
    for i in range(rows.shape[0] // chunks):
        part = rows[i * chunks : (i + 1) * chunks]
        for s, factor in enumerate(factors):
            moved = pltpu.roll(part, chunks - (1 << s) if backward else 1 << s, 0)
            part = part + times(moved, factor)
        moved = pltpu.roll(part, chunks - 1 if backward else 1, 0)
        out.append(jnp.where(keep, moved, 0.0))
    return jnp.concatenate(out, axis=0)


def toeplitz(row):
    wide = jnp.broadcast_to(row, (LANES, LANES))
    wide = pltpu.roll(wide, 0, 1, stride=1, stride_axis=0)
    j = lax.broadcasted_iota(jnp.int32, (LANES, LANES), 0)
    t = lax.broadcasted_iota(jnp.int32, (LANES, LANES), 1)
    return jnp.where(t >= j, wide, 0.0)


def turned_lag_sums(table):
    moved = pltpu.roll(table, 0, 1, stride=1, stride_axis=0)
    at = lax.broadcasted_iota(jnp.int32, (LANES, LANES), 0)
    lane = lax.broadcasted_iota(jnp.int32, (LANES, LANES), 1)
    return jnp.sum(jnp.where(lane >= at, moved, 0.0), axis=0, keepdims=True)


def together(works):
    while works:
        works = [work for work in works if next(work, None)]


def first_rows(first, second):
    at = lax.broadcasted_iota(jnp.int32, (8, LANES), 0)
    return jnp.where(at == 0, first, jnp.where(at == 1, second, 0.0))


def forward_kernel(
    sizes, recv_ref, lam_ref, weight_ref, skip_ref, out_ref, enter_ref, lag_ref,
    base_ref, fre_ref, fim_ref, mask_ref,
):
    channels, chunks, docs, steps, pitch, unroll = sizes
    rows = docs * 2 * chunks
    power_setup(lam_ref[...], base_ref, fre_ref, fim_ref, steps, channels)
    doc_masks(recv_ref, mask_ref, channels, pitch, chunks, docs, False)

    def one(h):
        pair = join(
            recv_ref[pl.ds(h, chunks, stride=2 * pitch), :],
            recv_ref[pl.ds(h + pitch, chunks, stride=2 * pitch), :],
        )
        inputs = halves(spread(pair, mask_ref, docs))
        power = halves(power_tables(h, base_ref, fre_ref, fim_ref, channels))
        yield True
        back = halves(reversed_tables(h, base_ref, fre_ref, fim_ref, channels))
        weight = weight_ref[pl.ds(h, 1), :]
        low = low_lanes((1, LANES))
        signed = halves(jnp.where(low, weight, -weight))
        both = first_rows(signed[0].astype(F32), signed[1].astype(F32)).astype(BF16)
        yield True
        lags = dot(both, below(power), NT)
        lags = lags[0:1] + lags[1:2]
        lags = lags[:, :LANES] + lags[:, LANES:]
        lag_ref[pl.ds(h, 1), :] = lags
        yield True
        table = halves(toeplitz(lags))
        yield True
        out = dot(below(inputs), beside([back[0], table[0]]), NN)
        out = out[:rows] + out[rows:] + dot(inputs[0], beside([back[1], table[1]]), NN)
        yield True
        enter = scan_chunks(
            out[:, :LANES], scan_factors(h, fre_ref, fim_ref, channels, chunks, steps, False), chunks, False
        )
        enter_ref[h] = enter
        yield True
        lam = as_factor(lam_ref[pl.ds(h, 1), :])
        coef = as_factor(times(weight, lam))
        coef = (jnp.where(low, coef[0], -coef[0]), jnp.where(low, coef[1], -coef[1]))
        yield True
        mixed = out[:, LANES:] + mm_turned(halves(times(enter, coef)), power)
        yield True
        first, second = gathered(mixed, mask_ref, chunks, docs)
        skip = skip_ref[pl.ds(h, 1), :]
        even, odd = join(first + skip * pair[0], second + skip * pair[1])
        out_ref[pl.ds(h, chunks, stride=2 * channels), :] = even
        out_ref[pl.ds(h + channels, chunks, stride=2 * channels), :] = odd

    def several(i, carry):
        together([one(i * unroll + k) for k in range(unroll)])
        return carry

    lax.fori_loop(0, channels // unroll, several, 0)


def backward_kernel(
    sizes, recv_ref, grad_ref, enter_ref, lag_ref, lam_ref, weight_ref, skip_ref,
    out_ref, sum_ref, first_ref, lagsum_ref, bias_ref,
    base_ref, fre_ref, fim_ref, mask_ref,
):
    channels, chunks, docs, steps, pitch, unroll = sizes
    rows = docs * 2 * chunks
    power_setup(lam_ref[...], base_ref, fre_ref, fim_ref, steps, channels)
    doc_masks(recv_ref, mask_ref, channels, pitch, chunks, docs, True)
    reach = (LANES - 1 - lax.broadcasted_iota(jnp.int32, (1, LANES), 1)).astype(F32)

    def one(h):
        pair = join(
            recv_ref[pl.ds(h, chunks, stride=2 * pitch), :],
            recv_ref[pl.ds(h + pitch, chunks, stride=2 * pitch), :],
        )
        gpair = join_turned(
            grad_ref[pl.ds(h, chunks, stride=2 * pitch), :],
            grad_ref[pl.ds(h + pitch, chunks, stride=2 * pitch), :],
        )
        inputs = spread(pair, mask_ref, docs)
        grads = spread(gpair, mask_ref, docs, docs * 2)
        ih, il = halves(inputs)
        gh, gl = halves(grads)
        yield True
        lagsum = turned_lag_sums(dot(below([gh, gl, gh]), below([ih, ih, il]), TN))
        lagsum_ref[pl.ds(h, 1), :] = lagsum
        yield True
        power = halves(power_tables(h, base_ref, fre_ref, fim_ref, channels))
        yield True
        back = halves(reversed_tables(h, base_ref, fre_ref, fim_ref, channels))
        weight = weight_ref[pl.ds(h, 1), :]
        lam = as_factor(lam_ref[pl.ds(h, 1), :])
        yield True
        table = halves(toeplitz(lag_ref[pl.ds(h, 1), :]))
        yield True
        enter = enter_ref[h]
        ahead = scan_factors(h, fre_ref, fim_ref, channels, chunks, steps, False)
        astern = scan_factors(h, fre_ref, fim_ref, channels, chunks, steps, True)
        i1h, i1l = halves(inputs * reach)
        g1h, g1l = halves(grads * reach)
        lh, ll = halves(first_rows(lagsum, lagsum * reach))
        yield True
        out = mm((below([i1h, gh, g1h, lh]), below([i1l, gl, g1l, ll])), back)
        yield True
        hop = (
            fre_ref[pl.ds(h + 16 * channels, 1), :] * float(LANES),
            fim_ref[pl.ds(h + 16 * channels, 1), :] * float(LANES),
        )
        turned = swap(enter)
        enter1 = scan_chunks(
            out[:rows] + enter * hop[0] + turned * hop[1], ahead, chunks, False
        )
        yield True
        seen = out[rows : 2 * rows]
        seen1 = seen + out[2 * rows : 3 * rows]
        seen_t = swap(seen)

        def summed_product(plain, crossed):
            plain = jnp.sum(plain, axis=0, keepdims=True)
            crossed = jnp.sum(crossed, axis=0, keepdims=True)
            low = low_lanes((1, LANES))
            plain, crossed = plain - swap(plain), crossed + swap(crossed)
            return times(jnp.where(low, plain, crossed), lam)

        sum_ref[pl.ds(h, 1), :] = (
            summed_product(enter * seen, turned * seen) + out[3 * rows : 3 * rows + 1]
        )
        first_ref[pl.ds(h, 1), :] = summed_product(
            enter1 * seen + enter * seen1, enter1 * seen_t + turned * seen1
        ) + out[3 * rows + 1 : 3 * rows + 2]
        yield True
        coef = as_factor(times(weight, lam))
        leave = scan_chunks(seen * coef[0] + seen_t * coef[1], astern, chunks, True)
        leave = jnp.where(low_lanes(leave.shape), leave, -leave)
        yield True
        inner = mm((gh, gl), table) + mm_turned(halves(leave), power)
        yield True
        gfirst, gsecond = gathered(inner, mask_ref, chunks, docs, docs * 2)
        skip = skip_ref[pl.ds(h, 1), :]
        gfirst = gfirst + skip * gpair[0]
        gsecond = gsecond + skip * gpair[1]
        bias_ref[pl.ds(h, 1), :] = jnp.sum(gfirst + gsecond, axis=0, keepdims=True)
        even, odd = apart_turned(gfirst, gsecond)
        out_ref[pl.ds(h, chunks, stride=2 * channels), :] = even
        out_ref[pl.ds(h + channels, chunks, stride=2 * channels), :] = odd

    def several(i, carry):
        together([one(i * unroll + k) for k in range(unroll)])
        return carry

    lax.fori_loop(0, channels // unroll, several, 0)


REACH = 512


def kernel_sizes(recv_rows, channels, pieces, docs, unroll):
    chunks = pieces // 2
    unroll = min(channels, max(1, unroll * 64 // (docs * 2 * chunks)))
    steps = min((chunks - 1).bit_length(), (REACH // LANES - 1).bit_length())
    return (channels, chunks, docs, steps, channels + 8, unroll)


def scratch(channels, chunks, docs, steps):
    return [
        pltpu.VMEM((8 * channels, LANES), F32),
        pltpu.VMEM(((16 + steps) * channels, LANES), F32),
        pltpu.VMEM(((16 + steps) * channels, LANES), F32),
        pltpu.VMEM((docs * 4, chunks, LANES), F32),
    ]


def recurrence(recv, lam, weight, skip, pieces, docs, unroll=2):
    channels = lam.shape[0]
    sizes = kernel_sizes(recv.shape[0], channels, pieces, docs, unroll)
    chunks, steps = sizes[1], sizes[3]
    rows = docs * 2 * chunks
    return pl.pallas_call(
        lambda *refs: forward_kernel(sizes, *refs),
        out_shape=(
            jax.ShapeDtypeStruct((pieces * channels, LANES), F32),
            jax.ShapeDtypeStruct((channels, rows, LANES), F32),
            jax.ShapeDtypeStruct((channels, LANES), F32),
        ),
        scratch_shapes=scratch(channels, chunks, docs, steps),
        compiler_params=pltpu.CompilerParams(vmem_limit_bytes=48 << 20),
        cost_estimate=estimate(16),
        name="recurrence",
    )(recv, lam, weight, skip)


def recurrence_back(recv, grad, enter, lags, lam, weight, skip, pieces, docs, unroll=2):
    channels = lam.shape[0]
    sizes = kernel_sizes(recv.shape[0], channels, pieces, docs, unroll)
    chunks, steps = sizes[1], sizes[3]
    row = jax.ShapeDtypeStruct((channels, LANES), F32)
    return pl.pallas_call(
        lambda *refs: backward_kernel(sizes, *refs),
        out_shape=(jax.ShapeDtypeStruct((pieces * channels, LANES), F32), row, row, row, row),
        scratch_shapes=scratch(channels, chunks, docs, steps),
        compiler_params=pltpu.CompilerParams(vmem_limit_bytes=48 << 20),
        cost_estimate=estimate(30),
        name="recurrence_back",
    )(recv, grad, enter, lags, lam, weight, skip)


EPSILON = 1e-05
MIB = 1 << 20


def estimate(micros, moved=0):
    return pl.CostEstimate(flops=int(micros * 1e9), transcendentals=0, bytes_accessed=int(moved))


def bell(values):
    share = 0.5 + 0.5 * lax.erf(values * 0.7071067811865476)
    return share, values * jnp.exp(-0.5 * values * values) * 0.3989422804014327


def sent_rows(values, out_ref, channels):
    turned = values.T
    for s in range(out_ref.shape[0]):
        out_ref[s, 0:channels, :] = turned[s * channels : (s + 1) * channels]


def share_rows(length, pieces):
    share = length // pieces
    return max(1, share // LANES), min(share, LANES)


def share_vectors(refs, out_ref, first):
    pieces = out_ref.shape[0]
    at = first
    for s in range(pieces):
        out_ref[s, first : first + 8, :] = jnp.zeros((8, LANES), F32)
    for ref in refs:
        count, wide = share_rows(ref.shape[1], pieces)
        for s in range(pieces):
            for r in range(count):
                start = (s * count + r) * wide
                out_ref[s, at + r : at + r + 1, :wide] = ref[:, start : start + wide]
        at += count


def normalize(values):
    centre = values - jnp.mean(values, axis=1, keepdims=True)
    recip = lax.rsqrt(jnp.mean(centre * centre, axis=1, keepdims=True) + EPSILON)
    return centre * recip, recip


def norm_back(grad, unit, recip):
    return recip * (
        grad
        - jnp.mean(grad, axis=1, keepdims=True)
        - unit * jnp.mean(grad * unit, axis=1, keepdims=True)
    )


def turning(size):
    at = lax.broadcasted_iota(jnp.int32, (size, size), 0)
    to = lax.broadcasted_iota(jnp.int32, (size, size), 1)
    return jnp.where(at + to == size - 1, 1.0, 0.0).astype(BF16)


def first_kernel(tokens_ref, cot_ref, seg_ref, gain_ref, bias_ref, send_ref, up_ref):
    pieces, pitch, rows = send_ref.shape
    channels = pitch - 8
    unit, _ = normalize(tokens_ref[...].astype(F32))
    sent_rows(unit * gain_ref[...] + bias_ref[...], send_ref, channels)
    seg = jnp.broadcast_to(seg_ref[...].astype(F32), (8, rows))
    for s in range(pieces):
        send_ref[s, channels:pitch, :] = seg
    up_ref[...] = cot_ref[...].astype(F32)


def last_kernel(back_ref, tokens_ref, gain_ref, hidden_ref, out_ref):
    unit, recip = normalize(tokens_ref[...].astype(F32))
    turn = turning(tokens_ref.shape[0])
    high, low = halves(back_ref[...])
    grad = (dot(turn, high, NT) + dot(turn, low, NT)) * gain_ref[...]
    out_ref[...] = (hidden_ref[...] + norm_back(grad, unit, recip)).astype(BF16)


def pieces_of(source, target, sems, chunks, rows):
    out = []
    wide = source.shape[0 if rows else 1] // chunks
    for i in range(chunks):
        part = (pl.ds(i * wide, wide), slice(None)) if rows else (slice(None), pl.ds(i * wide, wide))
        out.append(pltpu.make_async_copy(source.at[part], target.at[part], sems.at[i]))
    return out


class Sender:
    def __init__(self, sems):
        self.sems, self.copies = sems, []

    def send(self, source, target):
        self.copies.append(pltpu.make_async_copy(source, target, self.sems.at[len(self.copies)]))
        self.copies[-1].start()

    def finish(self):
        for copy in self.copies:
            copy.wait()


def by_core(values, place_ref, out_ref, pieces):
    wide = values.shape[1] // pieces
    for s in range(pieces):
        out_ref[(s % 2) ^ place_ref[0], :, (s // 2) * wide : (s // 2 + 1) * wide] = (
            values[:, s * wide : (s + 1) * wide]
        )


def by_pair(values, place_ref, out_ref, pieces):
    wide = values.shape[1] // pieces
    for s in range(pieces):
        at = (s // 8 * 2 + s // 2 % 2) * wide
        out_ref[(s // 4 % 2) ^ place_ref[3], (s % 2) ^ place_ref[0], :, at : at + wide] = (
            values[:, s * wide : (s + 1) * wide]
        )


def upward_kernel(
    pieces, place_ref, mixed_ref, tokens_ref, glu_bias_ref, gain_ref, bias_ref, ffn_bias_ref, glu_ref, ffn_ref,
    act_ref, z2_ref, keep_here_ref, keep_there_ref, send_here_ref, send_there_ref, pre_ref, hidden_ref,
    slope1_ref, slope2_ref, low_ref,
    glu_v, ffn_v, parts_v, act_v, z2_v, pre_v, hidden_v, slope1_v, slope2_v, low_v, glu_sem, ffn_sem, out_sem,
):
    rows, features = tokens_ref.shape
    glu_copies = pieces_of(glu_ref, glu_v, glu_sem, 4, False)
    ffn_copies = pieces_of(ffn_ref, ffn_v, ffn_sem, 8, False)
    for copy in glu_copies + ffn_copies[:2]:
        copy.start()
    sender = Sender(out_sem)
    mixed = mixed_ref[...].T
    share, steep = bell(mixed)
    slope1_v[...] = share + steep
    sender.send(slope1_v, slope1_ref)
    act = (mixed * share).astype(BF16)
    by_core(act.astype(F32), place_ref, act_v, pieces)
    sender.send(act_v, act_ref)
    wide = glu_ref.shape[1] // 4
    for i in range(4):
        glu_copies[i].wait()
        ffn_copies[i + 2].start()
        at = slice(i * wide, (i + 1) * wide)
        pre_v[:, at] = jnp.dot(act, glu_v[:, at], preferred_element_type=F32) + glu_bias_ref[:, at]
    sender.send(pre_v, pre_ref)
    hidden = tokens_ref[...].astype(F32) + pre_v[:, :features] * jax.nn.sigmoid(pre_v[:, features:])
    hidden_v[...] = hidden
    sender.send(hidden_v, hidden_ref)
    unit, _ = normalize(hidden)
    normed = (unit * gain_ref[...] + bias_ref[...]).astype(BF16)
    by_pair(normed.astype(F32), place_ref, z2_v, pieces)
    sender.send(z2_v, z2_ref)
    wide = ffn_ref.shape[1] // 8
    block = ffn_ref.shape[1] // pieces // 2
    for i in range(8):
        ffn_copies[i].wait()
        if 6 <= i + 6 < 8:
            ffn_copies[i + 6].start()
        at = slice(i * wide, (i + 1) * wide)
        ffn_pre = jnp.dot(normed, ffn_v[:, at], preferred_element_type=F32) + ffn_bias_ref[:, at]
        share, steep = bell(ffn_pre)
        slope2_v[:, at] = share + steep
        low = (ffn_pre * share).astype(BF16)
        low_v[:, at] = low
        columns = pl.ds(i * wide, wide)
        sender.send(slope2_v.at[:, columns], slope2_ref.at[:, columns])
        sender.send(low_v.at[:, columns], low_ref.at[:, columns])
        wider = low.astype(F32)
        for k in range(wide // block):
            index = (i * wide) // block + k
            piece, half = index // 2, index % 2
            parts_v[
                half ^ place_ref[1], (piece % 2) ^ place_ref[0], :,
                (piece // 2) * block : (piece // 2 + 1) * block,
            ] = wider[:, k * block : (k + 1) * block]
    for k, ref in enumerate((keep_here_ref, keep_there_ref, send_here_ref, send_there_ref)):
        sender.send(parts_v.at[k // 2, k % 2], ref)
    sender.finish()


def downward_kernel(
    place_ref, cot_ref, slope2_ref, hidden_ref, pre_ref, slope1_ref, gain_ref, act_ref, z2_ref,
    out_w_ref, in_w_ref, glu_w_ref,
    in_keep_ref, in_send_ref, glu_keep_ref, glu_send_ref, grad_hidden_ref, turned_ref,
    in_sum_ref, glu_sum_ref, gain_sum_ref, bias_sum_ref, out_sum_ref,
    out_v, in_v, glu_v, slope2_v, hidden_v, pre_v, slope1_v, parts_v, halves_v, grad_v,
    out_sem, in_sem, slope_sem, one_sem, send_sem, half_sem,
):
    rows, features = cot_ref.shape
    inner = out_w_ref.shape[0]
    wide = inner // 8
    out_copies = pieces_of(out_w_ref, out_v, out_sem, 8, True)
    in_copies = pieces_of(in_w_ref, in_v, in_sem, 8, False)
    slope_copies = pieces_of(slope2_ref, slope2_v, slope_sem, 8, False)
    late = [
        pltpu.make_async_copy(source, target, one_sem.at[k])
        for k, (source, target) in enumerate(
            ((hidden_ref, hidden_v), (pre_ref, pre_v), (slope1_ref, slope1_v), (glu_w_ref, glu_v))
        )
    ]
    ahead = 3
    for i in range(ahead):
        out_copies[i].start()
        slope_copies[i].start()
        in_copies[i].start()
    sender = Sender(send_sem)
    quarter, half = features // 4, features // 2
    for k in range(2):
        columns = pl.ds(features + k * half, half)
        sender.send(act_ref.at[k], glu_keep_ref.at[:, columns])
        sender.send(act_ref.at[k], glu_send_ref.at[:, columns])
        columns = pl.ds(inner + k * quarter, quarter)
        sender.send(z2_ref.at[0, k], in_keep_ref.at[:, columns])
        sender.send(z2_ref.at[1, k], in_send_ref.at[:, columns])
    cot = cot_ref[...]
    up = cot.astype(F32)
    out_sum_ref[...] = jnp.sum(up, axis=0, keepdims=True)
    total = jnp.zeros((rows, features), F32)
    for i in range(8):
        at = slice(i * wide, (i + 1) * wide)
        out_copies[i].wait()
        slope_copies[i].wait()
        in_copies[i].wait()
        if i + ahead < 8:
            out_copies[i + ahead].start()
            slope_copies[i + ahead].start()
            in_copies[i + ahead].start()
        elif i + ahead == 8:
            for copy in late:
                copy.start()
        grad = dot(cot, out_v[at, :], NT)
        low = (grad * slope2_v[:, at]).astype(BF16)
        wider = low.astype(F32)
        in_sum_ref[:, at] = jnp.sum(wider, axis=0, keepdims=True)
        parts_v[:, at] = wider
        columns = pl.ds(i * wide, wide)
        sender.send(parts_v.at[:, columns], in_keep_ref.at[:, columns])
        sender.send(parts_v.at[:, columns], in_send_ref.at[:, columns])
        total = total + dot(low, in_v[:, at], NT)
    for copy in late:
        copy.wait()
    unit, recip = normalize(hidden_v[...])
    gain_sum_ref[...] = jnp.sum(total * unit, axis=0, keepdims=True)
    bias_sum_ref[...] = jnp.sum(total, axis=0, keepdims=True)
    grad_hidden = up + norm_back(total * gain_ref[...], unit, recip)
    grad_v[...] = grad_hidden
    sender.send(grad_v, grad_hidden_ref)
    gate = jax.nn.sigmoid(pre_v[:, features:])
    first = (grad_hidden * gate).astype(BF16)
    second = (grad_hidden * pre_v[:, :features] * (gate * (1.0 - gate))).astype(BF16)
    grad_act = None
    for k, part in enumerate((first, second)):
        wider = part.astype(F32)
        at = slice(k * features, (k + 1) * features)
        glu_sum_ref[:, at] = jnp.sum(wider, axis=0, keepdims=True)
        halves_v[k] = wider
        kept = k ^ place_ref[1] == 0
        for ref, chosen in ((glu_keep_ref, kept), (glu_send_ref, jnp.logical_not(kept))):
            copy = pltpu.make_async_copy(halves_v.at[k], ref.at[:, pl.ds(0, features)], half_sem.at[k])
            pl.when(chosen)(copy.start)
        term = dot(part, glu_v[:, at], NT)
        grad_act = term if grad_act is None else grad_act + term
    turn = turning(rows)
    high, low = halves(grad_act * slope1_v[...])
    sent_rows(dot(turn, high, NN) + dot(turn, low, NN), turned_ref, turned_ref.shape[1] - 8)
    share_vectors(
        (in_sum_ref, glu_sum_ref, gain_sum_ref, bias_sum_ref, out_sum_ref), turned_ref, turned_ref.shape[1] - 8
    )
    for k in range(2):
        pltpu.make_async_copy(halves_v.at[k], glu_keep_ref.at[:, pl.ds(0, features)], half_sem.at[k]).wait()
    sender.finish()


def product_kernel(spans, place_ref, *refs):
    many = 1 + max(at for span in spans for at, _ in span)
    values, (keep_ref, send_ref) = refs[:many], refs[many : many + 2]
    left_ref, right_ref, total_ref, in_sem, keep_sem, send_sem = refs[many + 2 :]
    rows = values[0].shape[0]
    copies = []
    for g, span in enumerate(spans):
        for k, ((at, start), target) in enumerate(zip(span, (left_ref, right_ref))):
            copies.append(
                pltpu.make_async_copy(
                    values[at].at[:, pl.ds(start, target.shape[1])], target.at[pl.ds(g * rows, rows), :],
                    in_sem.at[2 * g + k],
                )
            )
            copies[-1].start()
    for copy in copies:
        copy.wait()
    left = left_ref[...].astype(BF16)
    right = right_ref[...].astype(BF16)
    blocks, height, _ = keep_ref.shape
    copies = []
    for i in range(blocks):
        total_ref[2 * i * height : 2 * (i + 1) * height, :] = dot(
            left[:, 2 * i * height : 2 * (i + 1) * height], right, TN
        )
        for k, (ref, sem) in enumerate(((keep_ref, keep_sem), (send_ref, send_sem))):
            block = 2 * i + (place_ref[2] ^ k)
            source = total_ref.at[pl.ds(pl.multiple_of(block * height, 8), height), :]
            copies.append(pltpu.make_async_copy(source, ref.at[i], sem.at[i]))
            copies[-1].start()
    for copy in copies:
        copy.wait()


SMEM = pl.BlockSpec(memory_space=pltpu.SMEM)
VMEM = pl.BlockSpec(memory_space=pltpu.VMEM)
WHOLE = pl.BlockSpec()
HBM = pl.BlockSpec(memory_space=pltpu.HBM)


def shaped(*shape, dtype=F32):
    return jax.ShapeDtypeStruct(shape, dtype)


def params_of(mib):
    return pltpu.CompilerParams(vmem_limit_bytes=mib * MIB)


def first_norm(tokens, cot, seg, gain, bias, pieces):
    rows, features = tokens.shape
    return pl.pallas_call(
        first_kernel,
        out_shape=(shaped(pieces, features // pieces + 8, rows), shaped(rows, features)),
        compiler_params=params_of(16), cost_estimate=estimate(4), name="first_norm",
    )(tokens, cot, seg, gain, bias)


def last_norm(back, tokens, gain, grad_hidden):
    return pl.pallas_call(
        last_kernel, out_shape=shaped(*tokens.shape, dtype=BF16),
        compiler_params=params_of(16), cost_estimate=estimate(4), name="last_norm",
    )(back, tokens, gain, grad_hidden)


def upward(place, mixed, tokens, glu_bias, gain, bias, ffn_bias, glu_weight, ffn_in, pieces):
    rows, features = tokens.shape
    inner = ffn_in.shape[1]
    return pl.pallas_call(
        lambda *refs: upward_kernel(pieces, *refs),
        in_specs=[SMEM] + [WHOLE] * 6 + [HBM] * 2,
        out_specs=(HBM,) * 11,
        out_shape=(
            shaped(2, rows, features // 2), shaped(2, 2, rows, features // 4),
            *(shaped(rows, inner // 4),) * 4, shaped(rows, 2 * features),
            shaped(rows, features), shaped(rows, features), shaped(rows, inner), shaped(rows, inner, dtype=BF16),
        ),
        scratch_shapes=[
            pltpu.VMEM(glu_weight.shape, BF16), pltpu.VMEM(ffn_in.shape, BF16),
            pltpu.VMEM((2, 2, rows, inner // 4), F32), pltpu.VMEM((2, rows, features // 2), F32),
            pltpu.VMEM((2, 2, rows, features // 4), F32), pltpu.VMEM((rows, 2 * features), F32),
            pltpu.VMEM((rows, features), F32), pltpu.VMEM((rows, features), F32),
            pltpu.VMEM((rows, inner), F32), pltpu.VMEM((rows, inner), BF16),
            pltpu.SemaphoreType.DMA((4,)), pltpu.SemaphoreType.DMA((8,)), pltpu.SemaphoreType.DMA((25,)),
        ],
        compiler_params=params_of(56), cost_estimate=estimate(14), name="upward",
    )(place, mixed, tokens, glu_bias, gain, bias, ffn_bias, glu_weight, ffn_in)


def downward(place, cot, slope2, hidden, pre, slope1, gain, act, z2, ffn_out, ffn_in, glu_weight, pieces):
    rows, features = cot.shape
    inner = ffn_in.shape[1]
    return pl.pallas_call(
        downward_kernel,
        in_specs=[SMEM, VMEM] + [HBM] * 4 + [VMEM] * 3 + [HBM] * 3,
        out_specs=(HBM,) * 5 + (WHOLE,),
        out_shape=(
            shaped(rows, inner + features // 2), shaped(rows, inner + features // 2),
            shaped(rows, 2 * features), shaped(rows, 2 * features),
            shaped(rows, features),
            shaped(pieces, features // pieces + 8, rows),
        ),
        scratch_shapes=[
            pltpu.VMEM((1, inner), F32), pltpu.VMEM((1, 2 * features), F32), pltpu.VMEM((1, features), F32),
            pltpu.VMEM((1, features), F32), pltpu.VMEM((1, features), F32),
            pltpu.VMEM(ffn_out.shape, BF16), pltpu.VMEM(ffn_in.shape, BF16), pltpu.VMEM(glu_weight.shape, BF16),
            pltpu.VMEM((rows, inner), F32), pltpu.VMEM((rows, features), F32),
            pltpu.VMEM((rows, 2 * features), F32), pltpu.VMEM((rows, features), F32),
            pltpu.VMEM((rows, inner), F32), pltpu.VMEM((2, rows, features), F32), pltpu.VMEM((rows, features), F32),
            pltpu.SemaphoreType.DMA((8,)), pltpu.SemaphoreType.DMA((8,)), pltpu.SemaphoreType.DMA((8,)),
            pltpu.SemaphoreType.DMA((4,)), pltpu.SemaphoreType.DMA((25,)), pltpu.SemaphoreType.DMA((2,)),
        ],
        compiler_params=params_of(56), cost_estimate=estimate(18), name="downward",
    )(place, cot, slope2, hidden, pre, slope1, gain, act, z2, ffn_out, ffn_in, glu_weight)


def products(place, values, spans, tall, wide, blocks):
    out = shaped(blocks // 2, tall // blocks, wide)
    tokens = len(spans) * values[0].shape[0]
    return pl.pallas_call(
        functools.partial(product_kernel, spans),
        in_specs=[SMEM] + [HBM] * len(values),
        out_specs=(HBM, HBM),
        out_shape=(out, out),
        scratch_shapes=[
            pltpu.VMEM((tokens, tall), F32), pltpu.VMEM((tokens, wide), F32), pltpu.VMEM((tall, wide), F32),
            pltpu.SemaphoreType.DMA((2 * len(spans),)), pltpu.SemaphoreType.DMA((blocks // 2,)),
            pltpu.SemaphoreType.DMA((blocks // 2,)),
        ],
        compiler_params=params_of(60), cost_estimate=estimate(4), name="products",
    )(place, *values)


def assemble_kernel(axis, place_ref, *refs):
    parts, out_ref = refs[:-1], refs[-1]
    many = len(parts) // 2
    half = out_ref.shape[axis] // 2
    for k in range(2):
        start = (place_ref[1] ^ k) * half
        for part in parts[k * many : (k + 1) * many]:
            size = part.shape[axis]
            if axis:
                out_ref[:, pl.ds(pl.multiple_of(start, LANES), size)] = part[...]
            else:
                out_ref[pl.ds(pl.multiple_of(start, 8), size), :] = part[...]
            start = start + size


def assembled(place, own, others, axis):
    shape = list(own[0].shape)
    shape[axis] = 2 * sum(part.shape[axis] for part in own)
    return pl.pallas_call(
        functools.partial(assemble_kernel, axis),
        in_specs=[SMEM] + [VMEM] * (len(own) + len(others)),
        out_shape=shaped(*shape), compiler_params=params_of(16), cost_estimate=estimate(1), name="assembled",
    )(place, *own, *others)


def pull_kernel(lengths, place_ref, own_ref, other_ref, *refs):
    out_c, out_b, weight, out_d, out_a, gain_in, bias_in, skip_in, step_in, real_in, freq_in = refs[:11]
    decay_ref, freq_ref, in_re_ref, in_im_ref, out_re_ref, out_im_ref = refs[11:17]
    step_ref, skip_ref, gain_ref, bias_ref = refs[17:21]
    vector_refs, products_ref, slopes_ref = refs[21:-2], refs[-2], refs[-1]
    blocks, pitch, _ = own_ref.shape
    channels = pitch - 8
    first_core = place_ref[0] == 0
    half = LANES // 2
    for s in range(2 * blocks):
        own, other = own_ref[s // 2], other_ref[s // 2]
        here = first_core if s % 2 == 0 else jnp.logical_not(first_core)
        state = jnp.where(here, own, other)
        at = slice(s * channels, (s + 1) * channels)
        total = as_factor(state[:channels, :LANES])
        moment = as_factor(state[:channels, LANES:])
        grad_c = times(out_c[at, :], total)
        out_re_ref[at, :] = grad_c[:, :half]
        out_im_ref[at, :] = -grad_c[:, half:]
        grad_b = times(out_b[at, :], total)
        in_re_ref[at, :] = grad_b[:, :half]
        in_im_ref[at, :] = -grad_b[:, half:]
        table = weight[at, :]
        products_ref[at, :] = table * total[0] + swap(table) * total[1]
        grad_d = times(table, moment) + times(out_d[at, :], total)
        grad_a = times(out_a[at, :], total) + step_in[at, :] * grad_d
        decay_ref[at, :] = real_in[at, :half] * grad_a[:, :half]
        freq_ref[at, :] = -grad_a[:, half:]
        slopes_ref[at, :] = step_in[at, :] * (real_in[at, :] * grad_d - freq_in[at, :] * swap(grad_d))
        columns = slice(s * channels, (s + 1) * channels)
        skip_ref[:, columns] = state[channels : channels + 1, :channels]
        bias_ref[:, columns] = state[channels : channels + 1, channels : 2 * channels]
        row = channels
        for ref, length in zip(vector_refs, lengths):
            count, wide = share_rows(length, 2 * blocks)
            for r in range(count):
                start = (s * count + r) * wide
                ref[:, start : start + wide] = state[row + r : row + r + 1, LANES : LANES + wide]
            row += count
    ones = jnp.where(low_lanes((8, LANES)), 1.0, 0.0).astype(BF16)
    sums = []
    for ref in (slopes_ref, products_ref):
        high, low = halves(ref[...])
        sums.append((dot(ones, high, NT) + dot(ones, low, NT))[0:1])
    step_ref[...] = sums[0]
    gain_ref[...] = (sums[1] + skip_in[...] * skip_ref[...] - bias_in[...] * bias_ref[...]) / gain_in[...]


def pulled(place, own, other, tables, gain, bias, skip, step, real, freq, lengths):
    features = tables[0].shape[0]
    row = shaped(1, features)
    table = shaped(features, LANES // 2)
    return pl.pallas_call(
        functools.partial(pull_kernel, lengths),
        in_specs=[SMEM] + [WHOLE] * 13,
        out_shape=(table,) * 6 + (row,) * 4 + tuple(shaped(1, length) for length in lengths),
        scratch_shapes=[pltpu.VMEM((features, LANES), F32)] * 2,
        compiler_params=params_of(32), cost_estimate=estimate(4), name="pulled",
    )(place, own, other, *tables, gain, bias, skip, step, real, freq)


def wide_product_kernel(quarter, place_ref, *refs):
    values, outs = refs[:4], refs[4:8]
    left_ref, right_ref, total_ref, left_sem, right_sem, out_sem = refs[8:]
    rows = values[0].shape[0]
    parts = right_ref.shape[0]
    wide = right_ref.shape[2]
    copies = []
    for v, value in enumerate(values):
        at = pl.ds(parts * wide + (quarter if v >= 2 else 0), quarter)
        copies.append(
            pltpu.make_async_copy(value.at[:, at], left_ref.at[pl.ds(v * rows, rows), :], left_sem.at[v])
        )
    for k in range(parts):
        for v, value in enumerate(values):
            copies.append(
                pltpu.make_async_copy(
                    value.at[:, pl.ds(k * wide, wide)], right_ref.at[k, pl.ds(v * rows, rows), :],
                    right_sem.at[4 * k + v],
                )
            )
    for copy in copies:
        copy.start()
    for copy in copies[:4]:
        copy.wait()
    left = left_ref[...].astype(BF16)
    blocks, height, _ = outs[0].shape
    for k in range(parts):
        for copy in copies[4 + 4 * k : 8 + 4 * k]:
            copy.wait()
        total = dot(left, right_ref[k].astype(BF16), TN)
        total_ref[k] = total.reshape(blocks, height, wide)
        here = place_ref[1] == k // 2
        keep, send = outs[2 * (k % 2)], outs[2 * (k % 2) + 1]

        @pl.when(here)
        def _():
            pltpu.make_async_copy(total_ref.at[k], keep, out_sem.at[k]).start()

        @pl.when(jnp.logical_not(here))
        def _():
            pltpu.make_async_copy(total_ref.at[k], send, out_sem.at[k]).start()

    for k in range(parts):
        pltpu.make_async_copy(total_ref.at[k], outs[0], out_sem.at[k]).wait()


def wide_products(place, values, inner, quarter, blocks):
    rows = values[0].shape[0]
    wide = inner // 4
    out = shaped(blocks, quarter // blocks, wide)
    return pl.pallas_call(
        functools.partial(wide_product_kernel, quarter),
        in_specs=[SMEM] + [HBM] * 4,
        out_specs=(HBM,) * 4,
        out_shape=(out,) * 4,
        scratch_shapes=[
            pltpu.VMEM((4 * rows, quarter), F32), pltpu.VMEM((4, 4 * rows, wide), F32),
            pltpu.VMEM((4, blocks, quarter // blocks, wide), F32),
            pltpu.SemaphoreType.DMA((4,)), pltpu.SemaphoreType.DMA((16,)), pltpu.SemaphoreType.DMA((4,)),
        ],
        compiler_params=params_of(60), cost_estimate=estimate(5), name="wide_products",
    )(place, *values)


def flipped(value, axis, bit):
    count = lax.axis_size(axis)
    return lax.ppermute(value, axis, [(i, i ^ bit) for i in range(count)])


def summed(value, axes):
    for axis in axes:
        bit = 1
        while bit < lax.axis_size(axis):
            value = value + flipped(value, axis, bit)
            bit *= 2
    return value


def halved(value, dim, which):
    first = lax.index_in_dim(value, 0, dim, keepdims=False)
    second = lax.index_in_dim(value, 1, dim, keepdims=False)
    pick = which == 0
    return jnp.where(pick, first, second), jnp.where(pick, second, first)


def across(value, bit=1):
    return flipped(value, "seq", bit)


def over_batch(value):
    return flipped(value, "batch", 1)


class Halving:
    def __init__(self, keep, got, mine, bits):
        self.keep, self.got, self.mine, self.bits = keep, got, mine, list(bits)

    def step(self):
        bit = self.bits.pop(0)
        blocks = self.keep + self.got
        pairs = blocks.reshape((blocks.shape[0] // 2, 2) + blocks.shape[1:])
        self.keep, send = halved(pairs, 1, (self.mine // bit) % 2)
        self.got = across(send, bit)

    def finish(self):
        while self.bits:
            self.step()
        return (self.keep + self.got)[0]


def tied(works, *others):
    out = lax.optimization_barrier(tuple(work.got for work in works) + others)
    for work, got in zip(works, out):
        work.got = got
    return out[len(works) :]


def times_pair(left, right):
    return left[0] * right[0] - left[1] * right[1], left[0] * right[1] + left[1] * right[0]


def mode_tables(params):
    decay_log, decay_freq, input_re, input_im, output_re, output_im, step_log = params
    step_size = jnp.exp(step_log)[:, None]
    real_part = -jnp.exp(decay_log)
    delta_re = step_size * real_part
    delta_im = step_size * decay_freq
    magnitude = jnp.exp(delta_re)
    lam = (magnitude * jnp.cos(delta_im), magnitude * jnp.sin(delta_im))
    denominator = real_part * real_part + decay_freq * decay_freq
    inverse = (real_part / denominator, -decay_freq / denominator)
    num_re = lam[0] - 1.0
    ratio = (
        (num_re * real_part + lam[1] * decay_freq) / denominator,
        (lam[1] * real_part - num_re * decay_freq) / denominator,
    )
    doubled = (2.0 * output_re, 2.0 * output_im)
    bbar = times_pair(ratio, (input_re, input_im))
    weight = times_pair(doubled, bbar)
    both = times_pair(times_pair(doubled, (input_re, input_im)), inverse)
    tables = (
        (2.0 * bbar[0], 2.0 * bbar[1]),
        times_pair(doubled, ratio),
        weight,
        times_pair(both, lam),
        tuple(-part for part in times_pair(both, ratio)),
    )
    return lam, weight, tables, step_size, real_part


def packed(real, imag):
    return jnp.concatenate([real, imag], axis=1)


def on_device(
    tokens, segments, norm1_gain, norm1_bias, decay_log, decay_freq, input_re, input_im,
    output_re, output_im, step_log, skip_gain, glu_weight, glu_bias, norm2_gain, norm2_bias,
    ffn_in, ffn_in_bias, ffn_out, ffn_out_bias, cotangent,
):
    contexts, piece_len, features = tokens.shape
    rows = contexts * piece_len
    pieces, mine = lax.axis_size("seq"), lax.axis_index("seq")
    channels = features // pieces
    docs = max(1, pieces * piece_len // 256)
    params = (decay_log, decay_freq, input_re, input_im, output_re, output_im, step_log)
    batch_bit = lax.axis_index("batch") % 2
    place = jnp.stack([mine % 2, batch_bit, (mine // 2) % 2, (mine // 4) % 2]).astype(jnp.int32)
    high_bits = [1 << k for k in range(3, pieces.bit_length() - 1)]

    def own(value):
        return lax.dynamic_slice_in_dim(value, mine * channels, channels, 0)

    def row_of(value):
        return jnp.broadcast_to(own(value)[:, None], (channels, LANES))

    def line(value):
        return value.reshape(1, -1)

    def by_channel(value):
        return lax.all_to_all(value, "seq", 0, 0)

    lam_pair, weight_pair = mode_tables(tuple(own(p) for p in params))[:2]
    lam, weight = packed(*lam_pair), packed(*weight_pair)
    skip = row_of(skip_gain)
    flat = tokens.reshape(rows, features)
    cot = cotangent.reshape(rows, features)

    send, up = first_norm(
        flat, cot, segments.reshape(1, rows), line(norm1_gain), line(norm1_bias), pieces
    )
    recv = by_channel(send)
    _, _, tables, step_size, real_part = mode_tables(params)
    recv = recv.reshape(pieces * (channels + 8), rows)
    up_x = over_batch(up)
    ups = [up, up_x, across(up), across(up_x)]
    mixed_rows, enter, lags = recurrence(recv, lam, weight, skip, pieces, docs, FORWARD_UNROLL)
    mixed = by_channel(mixed_rows.reshape(pieces, channels, rows))
    mixed, tables, *ups = lax.optimization_barrier((mixed, tables, *ups))
    mixed = mixed.reshape(features, rows)
    act_parts, z2_parts, ffn_here, ffn_there, ffn_send_here, ffn_send_there, glu_pre, hidden, slope1, slope2, ffn_low = upward(
        place, mixed, flat, line(glu_bias), line(norm2_gain), line(norm2_bias), line(ffn_in_bias),
        glu_weight, ffn_in, pieces,
    )
    in_keep, in_send, glu_keep, glu_send, grad_hidden, turned = downward(
        place, cot, slope2, hidden, glu_pre, slope1, line(norm2_gain), act_parts, z2_parts, ffn_out, ffn_in, glu_weight, pieces
    )

    inner = ffn_in.shape[1]
    ffn_x, ffn_xo = over_batch(ffn_send_here), over_batch(ffn_send_there)
    in_z = across(in_send, 4)
    glu_send, ffn_x, ffn_xo = lax.optimization_barrier((glu_send, ffn_x, ffn_xo))
    glu_x = over_batch(glu_send)
    values = [ffn_here, ffn_x, across(ffn_there), across(ffn_xo)] + ups
    spans = [[(i, 0), (i + 4, 0)] for i in range(4)]
    keep_out, send_out = products(place, values, spans, inner // 4, features, pieces // 2)
    back = by_channel(turned)
    lags, send_out = lax.optimization_barrier((lags, send_out))
    shares = jnp.sum(back[:, channels:], axis=0)
    out = Halving(keep_out, across(send_out, 2), mine, [4] + high_bits)
    grad_rows, sums, firsts, lagsum, bias_part = recurrence_back(
        recv, back.reshape(pieces * (channels + 8), rows), enter, lags, lam, weight, skip,
        pieces, docs, BACKWARD_UNROLL,
    )
    sums, tables, step_size, real_part = lax.optimization_barrier((sums, tables, step_size, real_part))
    tables = tuple(packed(*pair) for pair in tables)
    around = (
        jnp.broadcast_to(step_size, tables[0].shape),
        packed(real_part, real_part),
        packed(decay_freq, decay_freq),
    )
    vectors = jnp.concatenate([lagsum[:, LANES - 1], jnp.sum(bias_part, axis=1)]).reshape(1, -1)
    vectors = jnp.pad(vectors, ((0, 7), (0, LANES - vectors.shape[1])))
    vectors = jnp.concatenate([vectors, shares], axis=1)
    state = jnp.concatenate([jnp.concatenate([sums, firsts], axis=1), vectors], axis=0)
    state = summed(state, ("batch",))
    in_c = across(in_keep)
    grad_rows, glu_x, in_z, in_c, state, tables, around = tied(
        [out], grad_rows, glu_x, in_z, in_c, state, tables, around
    )
    out.step()
    in_keep, out.keep = lax.optimization_barrier((in_keep, out.keep))
    quarter, half = features // 4, features // 2
    values = [in_keep, in_z, in_c, across(in_z)]
    keep_a, send_a, keep_b, send_b = wide_products(place, values, inner, quarter, pieces // 4)
    grad_rows, keep_a = lax.optimization_barrier((grad_rows, keep_a))
    grad_normed = by_channel(grad_rows.reshape(pieces, channels, rows)).reshape(features, rows)
    first = Halving(keep_a, over_batch(send_a), mine, [2] + high_bits)
    second = Halving(keep_b, over_batch(send_b), mine, [2] + high_bits)
    glu_own = glu_keep
    values = [glu_own, glu_x, across(glu_keep), across(glu_x)]
    spans = [[(i, features if i < 2 else features + half), (i, 0)] for i in range(4)]
    keep_glu, send_glu = products(place, values, spans, half, features, pieces // 2)
    (state,) = tied([out], state)
    out.step()
    glu = Halving(keep_glu, across(send_glu, 2), mine, [4] + high_bits)

    def all_batches(value):
        bit = 2
        while bit < lax.axis_size("batch"):
            value = value + flipped(value, "batch", bit)
            bit *= 2
        return value, over_batch(value)

    groups = [[2 * i + c for i in range(pieces // 2)] for c in range(2)]
    state = jnp.broadcast_to(state[None], (pieces // 2,) + state.shape)
    state = lax.all_to_all(state, "seq", 0, 0, axis_index_groups=groups)

    grad_normed, ffn_low = tied([first], grad_normed, ffn_low)
    first.step()
    ffn_res = jnp.dot(ffn_low, ffn_out, preferred_element_type=F32) + ffn_out_bias
    result = (hidden + ffn_res).astype(BF16).reshape(tokens.shape)
    grad_tokens = last_norm(grad_normed, flat, line(norm1_gain), grad_hidden).reshape(tokens.shape)
    (first.keep,) = tied([glu], first.keep)
    glu.step()

    state, result, grad_tokens = tied([second, first, out, glu], state, result, grad_tokens)
    state_c = across(state)
    second.step()
    first.step()
    half_out, other_out = all_batches(out.finish())
    glu.step()

    lengths = (ffn_in.shape[1], 2 * features, features, features, features)
    small = pulled(
        place, state, state_c, tables, line(norm1_gain), line(norm1_bias), line(skip_gain), *around, lengths
    )
    other_out, *small = tied([second, glu, first], other_out, *small)
    grad_params = small[:6]
    vectors = [value.reshape(-1) for value in small[6:]]
    grad_step, grad_skip, grad_gain1, grad_bias1 = vectors[:4]
    bias_in, bias_glu, grad_g2, grad_b2, bias_out = vectors[4:]
    second.step()
    half_a, other_a = all_batches(first.finish())
    half_glu, other_glu = all_batches(glu.finish())

    other_a, other_glu = tied([second], other_a, other_glu)
    half_b, other_b = all_batches(second.finish())
    sum_out = assembled(place, [half_out], [other_out], 0)
    sum_glu = assembled(place, [half_glu], [other_glu], 1)
    sum_in = assembled(place, [half_a, half_b], [other_a, other_b], 1)
    return (
        result, grad_tokens, grad_gain1, grad_bias1, *grad_params, grad_step, grad_skip,
        sum_glu, bias_glu, grad_g2, grad_b2, sum_in, bias_in, sum_out, bias_out,
    )


def solution(mesh):
    spread_over = P("batch", "seq", None)
    in_specs = (spread_over, P("batch", "seq")) + (P(),) * 18 + (spread_over,)
    rows = P("seq", None)
    out_specs = (spread_over,) * 2 + (P(),) * 10 + (rows,) + (P(),) * 3 + (rows, P(), rows, P())
    return jax.shard_map(
        on_device, mesh=mesh, in_specs=in_specs, out_specs=out_specs, check_vma=False
    )
```

```python
import functools

import jax, jax.numpy as jnp
from jax import lax
from jax.sharding import PartitionSpec as P
from jax.experimental import pallas as pl
from jax.experimental.pallas import tpu as pltpu
F32, BF16 = jnp.float32, jnp.bfloat16
LANES = 128
HALF = 64
FORWARD_UNROLL = 16
BACKWARD_UNROLL = 8
NN = (((1,), (0,)), ((), ()))
NT = (((1,), (1,)), ((), ()))
TN = (((0,), (0,)), ((), ()))


def halves(value):
    high = value.astype(BF16)
    return high, (value - high.astype(F32)).astype(BF16)


def dot(left, right, dims):
    return lax.dot_general(left, right, dims, preferred_element_type=F32)


def beside(parts):
    return jnp.concatenate(parts, axis=1)


def below(parts):
    return jnp.concatenate(parts, axis=0)


def mm(left, right):
    table = beside(right)
    out = dot(beside(left), below([table, table]), NN)
    return out[:, :LANES] + out[:, LANES:]


def mm_turned(left, right):
    out = dot(beside(left), below([beside([right[0]] * 2), beside([right[1]] * 2)]), NT)
    return out[:, :LANES] + out[:, LANES:]


def swap(value):
    return pltpu.roll(value, HALF, value.ndim - 1)


def low_lanes(shape):
    return lax.broadcasted_iota(jnp.int32, shape, len(shape) - 1) < HALF


def as_factor(value):
    turned = swap(value)
    low = low_lanes(value.shape)
    return jnp.where(low, value, turned), jnp.where(low, -turned, value)


def times(value, factor):
    return value * factor[0] + swap(value) * factor[1]


def power_setup(lam, base_ref, fre_ref, fim_ref, steps, channels):
    one = jnp.where(low_lanes(lam.shape), 1.0, 0.0)
    factor = as_factor(lam)
    row = one
    for k in range(8):
        base_ref[pl.ds(k * channels, channels), :] = row
        row = times(row, factor)
    eight = as_factor(row)
    row = one
    for i in range(16):
        fre, fim = as_factor(row)
        fre_ref[pl.ds(i * channels, channels), :] = fre
        fim_ref[pl.ds(i * channels, channels), :] = fim
        row = times(row, eight)
    for s in range(steps):
        fre, fim = as_factor(row)
        fre_ref[pl.ds((16 + s) * channels, channels), :] = fre
        fim_ref[pl.ds((16 + s) * channels, channels), :] = fim
        row = times(row, (fre, fim))


def power_tables(h, base_ref, fre_ref, fim_ref, channels):
    base = base_ref[pl.ds(h, 8, stride=channels), :]
    turned = swap(base)
    return below([
        base * fre_ref[pl.ds(h + i * channels, 1), :] + turned * fim_ref[pl.ds(h + i * channels, 1), :]
        for i in range(16)
    ])


def reversed_tables(h, base_ref, fre_ref, fim_ref, channels):
    base = below([base_ref[pl.ds(h + k * channels, 1), :] for k in range(7, -1, -1)])
    turned = swap(base)
    return below([
        base * fre_ref[pl.ds(h + i * channels, 1), :] + turned * fim_ref[pl.ds(h + i * channels, 1), :]
        for i in range(15, -1, -1)
    ])


def doc_masks(seg_ref, mask_ref, row, pitch, chunks, docs, turn):
    even = seg_ref[pl.ds(row, chunks, stride=2 * pitch), :]
    odd = seg_ref[pl.ds(row + pitch, chunks, stride=2 * pitch), :]
    pair = join(even, odd)
    at = lax.broadcasted_iota(jnp.int32, (LANES, LANES), 0)
    to = lax.broadcasted_iota(jnp.int32, (LANES, LANES), 1)
    turning = jnp.where(at + to == LANES - 1, 1.0, 0.0).astype(BF16)
    for d in range(docs):
        for c in range(2):
            mask = jnp.where(pair[c] == float(d), 1.0, 0.0)
            mask_ref[d * 2 + c] = mask
            if turn:
                mask_ref[(docs + d) * 2 + c] = dot(mask.astype(BF16), turning, NN)


def join(even, odd):
    low = low_lanes(even.shape)
    return jnp.where(low, even, swap(odd)), jnp.where(low, swap(even), odd)


def join_turned(even, odd):
    low = low_lanes(even.shape)
    return jnp.where(low, swap(odd), even), jnp.where(low, odd, swap(even))


def apart_turned(first, second):
    low = low_lanes(first.shape)
    return jnp.where(low, swap(second), first), jnp.where(low, second, swap(first))


def spread(pair, mask_ref, docs, base=0):
    return below([pair[c] * mask_ref[base + d * 2 + c] for d in range(docs) for c in range(2)])


def gathered(rows, mask_ref, chunks, docs, base=0):
    out = []
    for c in range(2):
        total = None
        for d in range(docs):
            at = (d * 2 + c) * chunks
            term = rows[at : at + chunks] * mask_ref[base + d * 2 + c]
            total = term if total is None else total + term
        out.append(total)
    return out


def scan_factors(h, fre_ref, fim_ref, channels, chunks, steps, backward):
    at = lax.broadcasted_iota(jnp.int32, (chunks, LANES), 0)
    out = []
    for s in range(steps):
        keep = at < chunks - (1 << s) if backward else at >= (1 << s)
        fre = fre_ref[pl.ds(h + (16 + s) * channels, 1), :]
        fim = fim_ref[pl.ds(h + (16 + s) * channels, 1), :]
        out.append((jnp.where(keep, fre, 0.0), jnp.where(keep, fim, 0.0)))
    return out


def scan_chunks(rows, factors, chunks, backward):
    at = lax.broadcasted_iota(jnp.int32, (chunks, LANES), 0)
    keep = at < chunks - 1 if backward else at >= 1
    out = []
    for i in range(rows.shape[0] // chunks):
        part = rows[i * chunks : (i + 1) * chunks]
        for s, factor in enumerate(factors):
            moved = pltpu.roll(part, chunks - (1 << s) if backward else 1 << s, 0)
            part = part + times(moved, factor)
        moved = pltpu.roll(part, chunks - 1 if backward else 1, 0)
        out.append(jnp.where(keep, moved, 0.0))
    return jnp.concatenate(out, axis=0)


def toeplitz(row):
    wide = jnp.broadcast_to(row, (LANES, LANES))
    wide = pltpu.roll(wide, 0, 1, stride=1, stride_axis=0)
    j = lax.broadcasted_iota(jnp.int32, (LANES, LANES), 0)
    t = lax.broadcasted_iota(jnp.int32, (LANES, LANES), 1)
    return jnp.where(t >= j, wide, 0.0)


def turned_lag_sums(table):
    moved = pltpu.roll(table, 0, 1, stride=1, stride_axis=0)
    at = lax.broadcasted_iota(jnp.int32, (LANES, LANES), 0)
    lane = lax.broadcasted_iota(jnp.int32, (LANES, LANES), 1)
    return jnp.sum(jnp.where(lane >= at, moved, 0.0), axis=0, keepdims=True)


def together(works):
    while works:
        works = [work for work in works if next(work, None)]


def first_rows(first, second):
    at = lax.broadcasted_iota(jnp.int32, (8, LANES), 0)
    return jnp.where(at == 0, first, jnp.where(at == 1, second, 0.0))


def forward_kernel(
    sizes, recv_ref, lam_ref, weight_ref, skip_ref, out_ref, enter_ref, lag_ref,
    base_ref, fre_ref, fim_ref, mask_ref,
):
    channels, chunks, docs, steps, pitch, unroll = sizes
    rows = docs * 2 * chunks
    power_setup(lam_ref[...], base_ref, fre_ref, fim_ref, steps, channels)
    doc_masks(recv_ref, mask_ref, channels, pitch, chunks, docs, False)

    def one(h):
        pair = join(
            recv_ref[pl.ds(h, chunks, stride=2 * pitch), :],
            recv_ref[pl.ds(h + pitch, chunks, stride=2 * pitch), :],
        )
        inputs = halves(spread(pair, mask_ref, docs))
        power = halves(power_tables(h, base_ref, fre_ref, fim_ref, channels))
        yield True
        back = halves(reversed_tables(h, base_ref, fre_ref, fim_ref, channels))
        weight = weight_ref[pl.ds(h, 1), :]
        low = low_lanes((1, LANES))
        signed = halves(jnp.where(low, weight, -weight))
        both = first_rows(signed[0].astype(F32), signed[1].astype(F32)).astype(BF16)
        yield True
        lags = dot(both, below(power), NT)
        lags = lags[0:1] + lags[1:2]
        lags = lags[:, :LANES] + lags[:, LANES:]
        lag_ref[pl.ds(h, 1), :] = lags
        yield True
        table = halves(toeplitz(lags))
        yield True
        out = dot(below(inputs), beside([back[0], table[0]]), NN)
        out = out[:rows] + out[rows:] + dot(inputs[0], beside([back[1], table[1]]), NN)
        yield True
        enter = scan_chunks(
            out[:, :LANES], scan_factors(h, fre_ref, fim_ref, channels, chunks, steps, False), chunks, False
        )
        enter_ref[h] = enter
        yield True
        lam = as_factor(lam_ref[pl.ds(h, 1), :])
        coef = as_factor(times(weight, lam))
        coef = (jnp.where(low, coef[0], -coef[0]), jnp.where(low, coef[1], -coef[1]))
        yield True
        mixed = out[:, LANES:] + mm_turned(halves(times(enter, coef)), power)
        yield True
        first, second = gathered(mixed, mask_ref, chunks, docs)
        skip = skip_ref[pl.ds(h, 1), :]
        even, odd = join(first + skip * pair[0], second + skip * pair[1])
        out_ref[pl.ds(h, chunks, stride=2 * channels), :] = even
        out_ref[pl.ds(h + channels, chunks, stride=2 * channels), :] = odd

    def several(i, carry):
        together([one(i * unroll + k) for k in range(unroll)])
        return carry

    lax.fori_loop(0, channels // unroll, several, 0)


def backward_kernel(
    sizes, recv_ref, grad_ref, enter_ref, lag_ref, lam_ref, weight_ref, skip_ref,
    out_ref, sum_ref, first_ref, lagsum_ref, bias_ref,
    base_ref, fre_ref, fim_ref, mask_ref,
):
    channels, chunks, docs, steps, pitch, unroll = sizes
    rows = docs * 2 * chunks
    power_setup(lam_ref[...], base_ref, fre_ref, fim_ref, steps, channels)
    doc_masks(recv_ref, mask_ref, channels, pitch, chunks, docs, True)
    reach = (LANES - 1 - lax.broadcasted_iota(jnp.int32, (1, LANES), 1)).astype(F32)

    def one(h):
        pair = join(
            recv_ref[pl.ds(h, chunks, stride=2 * pitch), :],
            recv_ref[pl.ds(h + pitch, chunks, stride=2 * pitch), :],
        )
        gpair = join_turned(
            grad_ref[pl.ds(h, chunks, stride=2 * pitch), :],
            grad_ref[pl.ds(h + pitch, chunks, stride=2 * pitch), :],
        )
        inputs = spread(pair, mask_ref, docs)
        grads = spread(gpair, mask_ref, docs, docs * 2)
        ih, il = halves(inputs)
        gh, gl = halves(grads)
        yield True
        lagsum = turned_lag_sums(dot(below([gh, gl, gh]), below([ih, ih, il]), TN))
        lagsum_ref[pl.ds(h, 1), :] = lagsum
        yield True
        power = halves(power_tables(h, base_ref, fre_ref, fim_ref, channels))
        yield True
        back = halves(reversed_tables(h, base_ref, fre_ref, fim_ref, channels))
        weight = weight_ref[pl.ds(h, 1), :]
        lam = as_factor(lam_ref[pl.ds(h, 1), :])
        yield True
        table = halves(toeplitz(lag_ref[pl.ds(h, 1), :]))
        yield True
        enter = enter_ref[h]
        ahead = scan_factors(h, fre_ref, fim_ref, channels, chunks, steps, False)
        astern = scan_factors(h, fre_ref, fim_ref, channels, chunks, steps, True)
        i1h, i1l = halves(inputs * reach)
        g1h, g1l = halves(grads * reach)
        lh, ll = halves(first_rows(lagsum, lagsum * reach))
        yield True
        out = mm((below([i1h, gh, g1h, lh]), below([i1l, gl, g1l, ll])), back)
        yield True
        hop = (
            fre_ref[pl.ds(h + 16 * channels, 1), :] * float(LANES),
            fim_ref[pl.ds(h + 16 * channels, 1), :] * float(LANES),
        )
        turned = swap(enter)
        enter1 = scan_chunks(
            out[:rows] + enter * hop[0] + turned * hop[1], ahead, chunks, False
        )
        yield True
        seen = out[rows : 2 * rows]
        seen1 = seen + out[2 * rows : 3 * rows]
        seen_t = swap(seen)

        def summed_product(plain, crossed):
            plain = jnp.sum(plain, axis=0, keepdims=True)
            crossed = jnp.sum(crossed, axis=0, keepdims=True)
            low = low_lanes((1, LANES))
            plain, crossed = plain - swap(plain), crossed + swap(crossed)
            return times(jnp.where(low, plain, crossed), lam)

        sum_ref[pl.ds(h, 1), :] = (
            summed_product(enter * seen, turned * seen) + out[3 * rows : 3 * rows + 1]
        )
        first_ref[pl.ds(h, 1), :] = summed_product(
            enter1 * seen + enter * seen1, enter1 * seen_t + turned * seen1
        ) + out[3 * rows + 1 : 3 * rows + 2]
        yield True
        coef = as_factor(times(weight, lam))
        leave = scan_chunks(seen * coef[0] + seen_t * coef[1], astern, chunks, True)
        leave = jnp.where(low_lanes(leave.shape), leave, -leave)
        yield True
        inner = mm((gh, gl), table) + mm_turned(halves(leave), power)
        yield True
        gfirst, gsecond = gathered(inner, mask_ref, chunks, docs, docs * 2)
        skip = skip_ref[pl.ds(h, 1), :]
        gfirst = gfirst + skip * gpair[0]
        gsecond = gsecond + skip * gpair[1]
        bias_ref[pl.ds(h, 1), :] = jnp.sum(gfirst + gsecond, axis=0, keepdims=True)
        even, odd = apart_turned(gfirst, gsecond)
        out_ref[pl.ds(h, chunks, stride=2 * channels), :] = even
        out_ref[pl.ds(h + channels, chunks, stride=2 * channels), :] = odd

    def several(i, carry):
        together([one(i * unroll + k) for k in range(unroll)])
        return carry

    lax.fori_loop(0, channels // unroll, several, 0)


REACH = 512


def kernel_sizes(recv_rows, channels, pieces, docs, unroll):
    chunks = pieces // 2
    unroll = min(channels, max(1, unroll * 64 // (docs * 2 * chunks)))
    steps = min((chunks - 1).bit_length(), (REACH // LANES - 1).bit_length())
    return (channels, chunks, docs, steps, channels + 8, unroll)


def scratch(channels, chunks, docs, steps):
    return [
        pltpu.VMEM((8 * channels, LANES), F32),
        pltpu.VMEM(((16 + steps) * channels, LANES), F32),
        pltpu.VMEM(((16 + steps) * channels, LANES), F32),
        pltpu.VMEM((docs * 4, chunks, LANES), F32),
    ]


def recurrence(recv, lam, weight, skip, pieces, docs, unroll=2):
    channels = lam.shape[0]
    sizes = kernel_sizes(recv.shape[0], channels, pieces, docs, unroll)
    chunks, steps = sizes[1], sizes[3]
    rows = docs * 2 * chunks
    return pl.pallas_call(
        lambda *refs: forward_kernel(sizes, *refs),
        out_shape=(
            jax.ShapeDtypeStruct((pieces * channels, LANES), F32),
            jax.ShapeDtypeStruct((channels, rows, LANES), F32),
            jax.ShapeDtypeStruct((channels, LANES), F32),
        ),
        scratch_shapes=scratch(channels, chunks, docs, steps),
        compiler_params=pltpu.CompilerParams(vmem_limit_bytes=48 << 20),
        cost_estimate=estimate(16),
        name="recurrence",
    )(recv, lam, weight, skip)


def recurrence_back(recv, grad, enter, lags, lam, weight, skip, pieces, docs, unroll=2):
    channels = lam.shape[0]
    sizes = kernel_sizes(recv.shape[0], channels, pieces, docs, unroll)
    chunks, steps = sizes[1], sizes[3]
    row = jax.ShapeDtypeStruct((channels, LANES), F32)
    return pl.pallas_call(
        lambda *refs: backward_kernel(sizes, *refs),
        out_shape=(jax.ShapeDtypeStruct((pieces * channels, LANES), F32), row, row, row, row),
        scratch_shapes=scratch(channels, chunks, docs, steps),
        compiler_params=pltpu.CompilerParams(vmem_limit_bytes=48 << 20),
        cost_estimate=estimate(30),
        name="recurrence_back",
    )(recv, grad, enter, lags, lam, weight, skip)


EPSILON = 1e-05
MIB = 1 << 20


def estimate(micros, moved=0):
    return pl.CostEstimate(flops=int(micros * 1e9), transcendentals=0, bytes_accessed=int(moved))


def bell(values):
    share = 0.5 + 0.5 * lax.erf(values * 0.7071067811865476)
    return share, values * jnp.exp(-0.5 * values * values) * 0.3989422804014327


def sent_rows(values, out_ref, channels):
    turned = values.T
    for s in range(out_ref.shape[0]):
        out_ref[s, 0:channels, :] = turned[s * channels : (s + 1) * channels]


def share_rows(length, pieces):
    share = length // pieces
    return max(1, share // LANES), min(share, LANES)


def share_vectors(refs, out_ref, first):
    pieces = out_ref.shape[0]
    at = first
    for s in range(pieces):
        out_ref[s, first : first + 8, :] = jnp.zeros((8, LANES), F32)
    for ref in refs:
        count, wide = share_rows(ref.shape[1], pieces)
        for s in range(pieces):
            for r in range(count):
                start = (s * count + r) * wide
                out_ref[s, at + r : at + r + 1, :wide] = ref[:, start : start + wide]
        at += count


def normalize(values):
    centre = values - jnp.mean(values, axis=1, keepdims=True)
    recip = lax.rsqrt(jnp.mean(centre * centre, axis=1, keepdims=True) + EPSILON)
    return centre * recip, recip


def norm_back(grad, unit, recip):
    return recip * (
        grad
        - jnp.mean(grad, axis=1, keepdims=True)
        - unit * jnp.mean(grad * unit, axis=1, keepdims=True)
    )


def turning(size):
    at = lax.broadcasted_iota(jnp.int32, (size, size), 0)
    to = lax.broadcasted_iota(jnp.int32, (size, size), 1)
    return jnp.where(at + to == size - 1, 1.0, 0.0).astype(BF16)


def first_kernel(tokens_ref, cot_ref, seg_ref, gain_ref, bias_ref, send_ref, up_ref):
    pieces, pitch, rows = send_ref.shape
    channels = pitch - 8
    unit, _ = normalize(tokens_ref[...].astype(F32))
    sent_rows(unit * gain_ref[...] + bias_ref[...], send_ref, channels)
    seg = jnp.broadcast_to(seg_ref[...].astype(F32), (8, rows))
    for s in range(pieces):
        send_ref[s, channels:pitch, :] = seg
    up_ref[...] = cot_ref[...].astype(F32)


def last_kernel(back_ref, tokens_ref, gain_ref, hidden_ref, out_ref):
    unit, recip = normalize(tokens_ref[...].astype(F32))
    turn = turning(tokens_ref.shape[0])
    high, low = halves(back_ref[...])
    grad = (dot(turn, high, NT) + dot(turn, low, NT)) * gain_ref[...]
    out_ref[...] = (hidden_ref[...] + norm_back(grad, unit, recip)).astype(BF16)


def pieces_of(source, target, sems, chunks, rows):
    out = []
    wide = source.shape[0 if rows else 1] // chunks
    for i in range(chunks):
        part = (pl.ds(i * wide, wide), slice(None)) if rows else (slice(None), pl.ds(i * wide, wide))
        out.append(pltpu.make_async_copy(source.at[part], target.at[part], sems.at[i]))
    return out


class Sender:
    def __init__(self, sems):
        self.sems, self.copies = sems, []

    def send(self, source, target):
        self.copies.append(pltpu.make_async_copy(source, target, self.sems.at[len(self.copies)]))
        self.copies[-1].start()

    def finish(self):
        for copy in self.copies:
            copy.wait()


def by_core(values, place_ref, out_ref, pieces):
    wide = values.shape[1] // pieces
    for s in range(pieces):
        out_ref[(s % 2) ^ place_ref[0], :, (s // 2) * wide : (s // 2 + 1) * wide] = (
            values[:, s * wide : (s + 1) * wide]
        )


def by_pair(values, place_ref, out_ref, pieces):
    wide = values.shape[1] // pieces
    for s in range(pieces):
        at = (s // 8 * 2 + s // 2 % 2) * wide
        out_ref[(s // 4 % 2) ^ place_ref[3], (s % 2) ^ place_ref[0], :, at : at + wide] = (
            values[:, s * wide : (s + 1) * wide]
        )


def upward_kernel(
    pieces, place_ref, mixed_ref, tokens_ref, glu_bias_ref, gain_ref, bias_ref, ffn_bias_ref, glu_ref, ffn_ref,
    act_ref, z2_ref, keep_here_ref, keep_there_ref, send_here_ref, send_there_ref, pre_ref, hidden_ref,
    slope1_ref, slope2_ref, low_ref,
    glu_v, ffn_v, parts_v, act_v, z2_v, pre_v, hidden_v, slope1_v, slope2_v, low_v, glu_sem, ffn_sem, out_sem,
):
    rows, features = tokens_ref.shape
    glu_copies = pieces_of(glu_ref, glu_v, glu_sem, 4, False)
    ffn_copies = pieces_of(ffn_ref, ffn_v, ffn_sem, 8, False)
    for copy in glu_copies + ffn_copies[:2]:
        copy.start()
    sender = Sender(out_sem)
    mixed = mixed_ref[...].T
    share, steep = bell(mixed)
    slope1_v[...] = share + steep
    sender.send(slope1_v, slope1_ref)
    act = (mixed * share).astype(BF16)
    by_core(act.astype(F32), place_ref, act_v, pieces)
    sender.send(act_v, act_ref)
    wide = glu_ref.shape[1] // 4
    for i in range(4):
        glu_copies[i].wait()
        ffn_copies[i + 2].start()
        at = slice(i * wide, (i + 1) * wide)
        pre_v[:, at] = jnp.dot(act, glu_v[:, at], preferred_element_type=F32) + glu_bias_ref[:, at]
    sender.send(pre_v, pre_ref)
    hidden = tokens_ref[...].astype(F32) + pre_v[:, :features] * jax.nn.sigmoid(pre_v[:, features:])
    hidden_v[...] = hidden
    sender.send(hidden_v, hidden_ref)
    unit, _ = normalize(hidden)
    normed = (unit * gain_ref[...] + bias_ref[...]).astype(BF16)
    by_pair(normed.astype(F32), place_ref, z2_v, pieces)
    sender.send(z2_v, z2_ref)
    wide = ffn_ref.shape[1] // 8
    block = ffn_ref.shape[1] // pieces // 2
    for i in range(8):
        ffn_copies[i].wait()
        if 6 <= i + 6 < 8:
            ffn_copies[i + 6].start()
        at = slice(i * wide, (i + 1) * wide)
        ffn_pre = jnp.dot(normed, ffn_v[:, at], preferred_element_type=F32) + ffn_bias_ref[:, at]
        share, steep = bell(ffn_pre)
        slope2_v[:, at] = share + steep
        low = (ffn_pre * share).astype(BF16)
        low_v[:, at] = low
        columns = pl.ds(i * wide, wide)
        sender.send(slope2_v.at[:, columns], slope2_ref.at[:, columns])
        sender.send(low_v.at[:, columns], low_ref.at[:, columns])
        wider = low.astype(F32)
        for k in range(wide // block):
            index = (i * wide) // block + k
            piece, half = index // 2, index % 2
            parts_v[
                half ^ place_ref[1], (piece % 2) ^ place_ref[0], :,
                (piece // 2) * block : (piece // 2 + 1) * block,
            ] = wider[:, k * block : (k + 1) * block]
    for k, ref in enumerate((keep_here_ref, keep_there_ref, send_here_ref, send_there_ref)):
        sender.send(parts_v.at[k // 2, k % 2], ref)
    sender.finish()


def downward_kernel(
    place_ref, cot_ref, slope2_ref, hidden_ref, pre_ref, slope1_ref, gain_ref, act_ref, z2_ref,
    out_w_ref, in_w_ref, glu_w_ref,
    in_keep_ref, in_send_ref, glu_keep_ref, glu_send_ref, grad_hidden_ref, turned_ref,
    in_sum_ref, glu_sum_ref, gain_sum_ref, bias_sum_ref, out_sum_ref,
    out_v, in_v, glu_v, slope2_v, hidden_v, pre_v, slope1_v, parts_v, halves_v, grad_v,
    out_sem, in_sem, slope_sem, one_sem, send_sem, half_sem,
):
    rows, features = cot_ref.shape
    inner = out_w_ref.shape[0]
    wide = inner // 8
    out_copies = pieces_of(out_w_ref, out_v, out_sem, 8, True)
    in_copies = pieces_of(in_w_ref, in_v, in_sem, 8, False)
    slope_copies = pieces_of(slope2_ref, slope2_v, slope_sem, 8, False)
    late = [
        pltpu.make_async_copy(source, target, one_sem.at[k])
        for k, (source, target) in enumerate(
            ((hidden_ref, hidden_v), (pre_ref, pre_v), (slope1_ref, slope1_v), (glu_w_ref, glu_v))
        )
    ]
    ahead = 3
    for i in range(ahead):
        out_copies[i].start()
        slope_copies[i].start()
        in_copies[i].start()
    sender = Sender(send_sem)
    quarter, half = features // 4, features // 2
    for k in range(2):
        columns = pl.ds(features + k * half, half)
        sender.send(act_ref.at[k], glu_keep_ref.at[:, columns])
        sender.send(act_ref.at[k], glu_send_ref.at[:, columns])
        columns = pl.ds(inner + k * quarter, quarter)
        sender.send(z2_ref.at[0, k], in_keep_ref.at[:, columns])
        sender.send(z2_ref.at[1, k], in_send_ref.at[:, columns])
    cot = cot_ref[...]
    up = cot.astype(F32)
    out_sum_ref[...] = jnp.sum(up, axis=0, keepdims=True)
    total = jnp.zeros((rows, features), F32)
    for i in range(8):
        at = slice(i * wide, (i + 1) * wide)
        out_copies[i].wait()
        slope_copies[i].wait()
        in_copies[i].wait()
        if i + ahead < 8:
            out_copies[i + ahead].start()
            slope_copies[i + ahead].start()
            in_copies[i + ahead].start()
        elif i + ahead == 8:
            for copy in late:
                copy.start()
        grad = dot(cot, out_v[at, :], NT)
        low = (grad * slope2_v[:, at]).astype(BF16)
        wider = low.astype(F32)
        in_sum_ref[:, at] = jnp.sum(wider, axis=0, keepdims=True)
        parts_v[:, at] = wider
        columns = pl.ds(i * wide, wide)
        sender.send(parts_v.at[:, columns], in_keep_ref.at[:, columns])
        sender.send(parts_v.at[:, columns], in_send_ref.at[:, columns])
        total = total + dot(low, in_v[:, at], NT)
    for copy in late:
        copy.wait()
    unit, recip = normalize(hidden_v[...])
    gain_sum_ref[...] = jnp.sum(total * unit, axis=0, keepdims=True)
    bias_sum_ref[...] = jnp.sum(total, axis=0, keepdims=True)
    grad_hidden = up + norm_back(total * gain_ref[...], unit, recip)
    grad_v[...] = grad_hidden
    sender.send(grad_v, grad_hidden_ref)
    gate = jax.nn.sigmoid(pre_v[:, features:])
    first = (grad_hidden * gate).astype(BF16)
    second = (grad_hidden * pre_v[:, :features] * (gate * (1.0 - gate))).astype(BF16)
    grad_act = None
    for k, part in enumerate((first, second)):
        wider = part.astype(F32)
        at = slice(k * features, (k + 1) * features)
        glu_sum_ref[:, at] = jnp.sum(wider, axis=0, keepdims=True)
        halves_v[k] = wider
        kept = k ^ place_ref[1] == 0
        for ref, chosen in ((glu_keep_ref, kept), (glu_send_ref, jnp.logical_not(kept))):
            copy = pltpu.make_async_copy(halves_v.at[k], ref.at[:, pl.ds(0, features)], half_sem.at[k])
            pl.when(chosen)(copy.start)
        term = dot(part, glu_v[:, at], NT)
        grad_act = term if grad_act is None else grad_act + term
    turn = turning(rows)
    high, low = halves(grad_act * slope1_v[...])
    sent_rows(dot(turn, high, NN) + dot(turn, low, NN), turned_ref, turned_ref.shape[1] - 8)
    share_vectors(
        (in_sum_ref, glu_sum_ref, gain_sum_ref, bias_sum_ref, out_sum_ref), turned_ref, turned_ref.shape[1] - 8
    )
    for k in range(2):
        pltpu.make_async_copy(halves_v.at[k], glu_keep_ref.at[:, pl.ds(0, features)], half_sem.at[k]).wait()
    sender.finish()


def product_kernel(spans, place_ref, *refs):
    many = 1 + max(at for span in spans for at, _ in span)
    values, (keep_ref, send_ref) = refs[:many], refs[many : many + 2]
    left_ref, right_ref, total_ref, in_sem, keep_sem, send_sem = refs[many + 2 :]
    rows = values[0].shape[0]
    copies = []
    for g, span in enumerate(spans):
        for k, ((at, start), target) in enumerate(zip(span, (left_ref, right_ref))):
            copies.append(
                pltpu.make_async_copy(
                    values[at].at[:, pl.ds(start, target.shape[1])], target.at[pl.ds(g * rows, rows), :],
                    in_sem.at[2 * g + k],
                )
            )
            copies[-1].start()
    for copy in copies:
        copy.wait()
    left = left_ref[...].astype(BF16)
    right = right_ref[...].astype(BF16)
    blocks, height, _ = keep_ref.shape
    copies = []
    for i in range(blocks):
        total_ref[2 * i * height : 2 * (i + 1) * height, :] = dot(
            left[:, 2 * i * height : 2 * (i + 1) * height], right, TN
        )
        for k, (ref, sem) in enumerate(((keep_ref, keep_sem), (send_ref, send_sem))):
            block = 2 * i + (place_ref[2] ^ k)
            source = total_ref.at[pl.ds(pl.multiple_of(block * height, 8), height), :]
            copies.append(pltpu.make_async_copy(source, ref.at[i], sem.at[i]))
            copies[-1].start()
    for copy in copies:
        copy.wait()


SMEM = pl.BlockSpec(memory_space=pltpu.SMEM)
VMEM = pl.BlockSpec(memory_space=pltpu.VMEM)
WHOLE = pl.BlockSpec()
HBM = pl.BlockSpec(memory_space=pltpu.HBM)


def shaped(*shape, dtype=F32):
    return jax.ShapeDtypeStruct(shape, dtype)


def params_of(mib):
    return pltpu.CompilerParams(vmem_limit_bytes=mib * MIB)


def first_norm(tokens, cot, seg, gain, bias, pieces):
    rows, features = tokens.shape
    return pl.pallas_call(
        first_kernel,
        out_shape=(shaped(pieces, features // pieces + 8, rows), shaped(rows, features)),
        compiler_params=params_of(16), cost_estimate=estimate(4), name="first_norm",
    )(tokens, cot, seg, gain, bias)


def last_norm(back, tokens, gain, grad_hidden):
    return pl.pallas_call(
        last_kernel, out_shape=shaped(*tokens.shape, dtype=BF16),
        compiler_params=params_of(16), cost_estimate=estimate(4), name="last_norm",
    )(back, tokens, gain, grad_hidden)


def upward(place, mixed, tokens, glu_bias, gain, bias, ffn_bias, glu_weight, ffn_in, pieces):
    rows, features = tokens.shape
    inner = ffn_in.shape[1]
    return pl.pallas_call(
        lambda *refs: upward_kernel(pieces, *refs),
        in_specs=[SMEM] + [WHOLE] * 6 + [HBM] * 2,
        out_specs=(HBM,) * 11,
        out_shape=(
            shaped(2, rows, features // 2), shaped(2, 2, rows, features // 4),
            *(shaped(rows, inner // 4),) * 4, shaped(rows, 2 * features),
            shaped(rows, features), shaped(rows, features), shaped(rows, inner), shaped(rows, inner, dtype=BF16),
        ),
        scratch_shapes=[
            pltpu.VMEM(glu_weight.shape, BF16), pltpu.VMEM(ffn_in.shape, BF16),
            pltpu.VMEM((2, 2, rows, inner // 4), F32), pltpu.VMEM((2, rows, features // 2), F32),
            pltpu.VMEM((2, 2, rows, features // 4), F32), pltpu.VMEM((rows, 2 * features), F32),
            pltpu.VMEM((rows, features), F32), pltpu.VMEM((rows, features), F32),
            pltpu.VMEM((rows, inner), F32), pltpu.VMEM((rows, inner), BF16),
            pltpu.SemaphoreType.DMA((4,)), pltpu.SemaphoreType.DMA((8,)), pltpu.SemaphoreType.DMA((25,)),
        ],
        compiler_params=params_of(56), cost_estimate=estimate(14), name="upward",
    )(place, mixed, tokens, glu_bias, gain, bias, ffn_bias, glu_weight, ffn_in)


def downward(place, cot, slope2, hidden, pre, slope1, gain, act, z2, ffn_out, ffn_in, glu_weight, pieces):
    rows, features = cot.shape
    inner = ffn_in.shape[1]
    return pl.pallas_call(
        downward_kernel,
        in_specs=[SMEM, VMEM] + [HBM] * 4 + [VMEM] * 3 + [HBM] * 3,
        out_specs=(HBM,) * 5 + (WHOLE,),
        out_shape=(
            shaped(rows, inner + features // 2), shaped(rows, inner + features // 2),
            shaped(rows, 2 * features), shaped(rows, 2 * features),
            shaped(rows, features),
            shaped(pieces, features // pieces + 8, rows),
        ),
        scratch_shapes=[
            pltpu.VMEM((1, inner), F32), pltpu.VMEM((1, 2 * features), F32), pltpu.VMEM((1, features), F32),
            pltpu.VMEM((1, features), F32), pltpu.VMEM((1, features), F32),
            pltpu.VMEM(ffn_out.shape, BF16), pltpu.VMEM(ffn_in.shape, BF16), pltpu.VMEM(glu_weight.shape, BF16),
            pltpu.VMEM((rows, inner), F32), pltpu.VMEM((rows, features), F32),
            pltpu.VMEM((rows, 2 * features), F32), pltpu.VMEM((rows, features), F32),
            pltpu.VMEM((rows, inner), F32), pltpu.VMEM((2, rows, features), F32), pltpu.VMEM((rows, features), F32),
            pltpu.SemaphoreType.DMA((8,)), pltpu.SemaphoreType.DMA((8,)), pltpu.SemaphoreType.DMA((8,)),
            pltpu.SemaphoreType.DMA((4,)), pltpu.SemaphoreType.DMA((25,)), pltpu.SemaphoreType.DMA((2,)),
        ],
        compiler_params=params_of(56), cost_estimate=estimate(18), name="downward",
    )(place, cot, slope2, hidden, pre, slope1, gain, act, z2, ffn_out, ffn_in, glu_weight)


def products(place, values, spans, tall, wide, blocks):
    out = shaped(blocks // 2, tall // blocks, wide)
    tokens = len(spans) * values[0].shape[0]
    return pl.pallas_call(
        functools.partial(product_kernel, spans),
        in_specs=[SMEM] + [HBM] * len(values),
        out_specs=(HBM, HBM),
        out_shape=(out, out),
        scratch_shapes=[
            pltpu.VMEM((tokens, tall), F32), pltpu.VMEM((tokens, wide), F32), pltpu.VMEM((tall, wide), F32),
            pltpu.SemaphoreType.DMA((2 * len(spans),)), pltpu.SemaphoreType.DMA((blocks // 2,)),
            pltpu.SemaphoreType.DMA((blocks // 2,)),
        ],
        compiler_params=params_of(60), cost_estimate=estimate(4), name="products",
    )(place, *values)


def assemble_kernel(axis, place_ref, *refs):
    parts, out_ref = refs[:-1], refs[-1]
    many = len(parts) // 2
    half = out_ref.shape[axis] // 2
    for k in range(2):
        start = (place_ref[1] ^ k) * half
        for part in parts[k * many : (k + 1) * many]:
            size = part.shape[axis]
            if axis:
                out_ref[:, pl.ds(pl.multiple_of(start, LANES), size)] = part[...]
            else:
                out_ref[pl.ds(pl.multiple_of(start, 8), size), :] = part[...]
            start = start + size


def assembled(place, own, others, axis):
    shape = list(own[0].shape)
    shape[axis] = 2 * sum(part.shape[axis] for part in own)
    return pl.pallas_call(
        functools.partial(assemble_kernel, axis),
        in_specs=[SMEM] + [VMEM] * (len(own) + len(others)),
        out_shape=shaped(*shape), compiler_params=params_of(16), cost_estimate=estimate(1), name="assembled",
    )(place, *own, *others)


def pull_kernel(lengths, place_ref, own_ref, other_ref, *refs):
    out_c, out_b, weight, out_d, out_a, gain_in, bias_in, skip_in, step_in, real_in, freq_in = refs[:11]
    decay_ref, freq_ref, in_re_ref, in_im_ref, out_re_ref, out_im_ref = refs[11:17]
    step_ref, skip_ref, gain_ref, bias_ref = refs[17:21]
    vector_refs, products_ref, slopes_ref = refs[21:-2], refs[-2], refs[-1]
    blocks, pitch, _ = own_ref.shape
    channels = pitch - 8
    first_core = place_ref[0] == 0
    half = LANES // 2
    for s in range(2 * blocks):
        own, other = own_ref[s // 2], other_ref[s // 2]
        here = first_core if s % 2 == 0 else jnp.logical_not(first_core)
        state = jnp.where(here, own, other)
        at = slice(s * channels, (s + 1) * channels)
        total = as_factor(state[:channels, :LANES])
        moment = as_factor(state[:channels, LANES:])
        grad_c = times(out_c[at, :], total)
        out_re_ref[at, :] = grad_c[:, :half]
        out_im_ref[at, :] = -grad_c[:, half:]
        grad_b = times(out_b[at, :], total)
        in_re_ref[at, :] = grad_b[:, :half]
        in_im_ref[at, :] = -grad_b[:, half:]
        table = weight[at, :]
        products_ref[at, :] = table * total[0] + swap(table) * total[1]
        grad_d = times(table, moment) + times(out_d[at, :], total)
        grad_a = times(out_a[at, :], total) + step_in[at, :] * grad_d
        decay_ref[at, :] = real_in[at, :half] * grad_a[:, :half]
        freq_ref[at, :] = -grad_a[:, half:]
        slopes_ref[at, :] = step_in[at, :] * (real_in[at, :] * grad_d - freq_in[at, :] * swap(grad_d))
        columns = slice(s * channels, (s + 1) * channels)
        skip_ref[:, columns] = state[channels : channels + 1, :channels]
        bias_ref[:, columns] = state[channels : channels + 1, channels : 2 * channels]
        row = channels
        for ref, length in zip(vector_refs, lengths):
            count, wide = share_rows(length, 2 * blocks)
            for r in range(count):
                start = (s * count + r) * wide
                ref[:, start : start + wide] = state[row + r : row + r + 1, LANES : LANES + wide]
            row += count
    ones = jnp.where(low_lanes((8, LANES)), 1.0, 0.0).astype(BF16)
    sums = []
    for ref in (slopes_ref, products_ref):
        high, low = halves(ref[...])
        sums.append((dot(ones, high, NT) + dot(ones, low, NT))[0:1])
    step_ref[...] = sums[0]
    gain_ref[...] = (sums[1] + skip_in[...] * skip_ref[...] - bias_in[...] * bias_ref[...]) / gain_in[...]


def pulled(place, own, other, tables, gain, bias, skip, step, real, freq, lengths):
    features = tables[0].shape[0]
    row = shaped(1, features)
    table = shaped(features, LANES // 2)
    return pl.pallas_call(
        functools.partial(pull_kernel, lengths),
        in_specs=[SMEM] + [WHOLE] * 13,
        out_shape=(table,) * 6 + (row,) * 4 + tuple(shaped(1, length) for length in lengths),
        scratch_shapes=[pltpu.VMEM((features, LANES), F32)] * 2,
        compiler_params=params_of(32), cost_estimate=estimate(4), name="pulled",
    )(place, own, other, *tables, gain, bias, skip, step, real, freq)


def wide_product_kernel(quarter, place_ref, *refs):
    values, outs = refs[:4], refs[4:8]
    left_ref, right_ref, total_ref, left_sem, right_sem, out_sem = refs[8:]
    rows = values[0].shape[0]
    parts = right_ref.shape[0]
    wide = right_ref.shape[2]
    copies = []
    for v, value in enumerate(values):
        at = pl.ds(parts * wide + (quarter if v >= 2 else 0), quarter)
        copies.append(
            pltpu.make_async_copy(value.at[:, at], left_ref.at[pl.ds(v * rows, rows), :], left_sem.at[v])
        )
    for k in range(parts):
        for v, value in enumerate(values):
            copies.append(
                pltpu.make_async_copy(
                    value.at[:, pl.ds(k * wide, wide)], right_ref.at[k, pl.ds(v * rows, rows), :],
                    right_sem.at[4 * k + v],
                )
            )
    for copy in copies:
        copy.start()
    for copy in copies[:4]:
        copy.wait()
    left = left_ref[...].astype(BF16)
    blocks, height, _ = outs[0].shape
    for k in range(parts):
        for copy in copies[4 + 4 * k : 8 + 4 * k]:
            copy.wait()
        total = dot(left, right_ref[k].astype(BF16), TN)
        total_ref[k] = total.reshape(blocks, height, wide)
        here = place_ref[1] == k // 2
        keep, send = outs[2 * (k % 2)], outs[2 * (k % 2) + 1]

        @pl.when(here)
        def _():
            pltpu.make_async_copy(total_ref.at[k], keep, out_sem.at[k]).start()

        @pl.when(jnp.logical_not(here))
        def _():
            pltpu.make_async_copy(total_ref.at[k], send, out_sem.at[k]).start()

    for k in range(parts):
        pltpu.make_async_copy(total_ref.at[k], outs[0], out_sem.at[k]).wait()


def wide_products(place, values, inner, quarter, blocks):
    rows = values[0].shape[0]
    wide = inner // 4
    out = shaped(blocks, quarter // blocks, wide)
    return pl.pallas_call(
        functools.partial(wide_product_kernel, quarter),
        in_specs=[SMEM] + [HBM] * 4,
        out_specs=(HBM,) * 4,
        out_shape=(out,) * 4,
        scratch_shapes=[
            pltpu.VMEM((4 * rows, quarter), F32), pltpu.VMEM((4, 4 * rows, wide), F32),
            pltpu.VMEM((4, blocks, quarter // blocks, wide), F32),
            pltpu.SemaphoreType.DMA((4,)), pltpu.SemaphoreType.DMA((16,)), pltpu.SemaphoreType.DMA((4,)),
        ],
        compiler_params=params_of(60), cost_estimate=estimate(5), name="wide_products",
    )(place, *values)


def flipped(value, axis, bit):
    count = lax.axis_size(axis)
    return lax.ppermute(value, axis, [(i, i ^ bit) for i in range(count)])


def summed(value, axes):
    for axis in axes:
        bit = 1
        while bit < lax.axis_size(axis):
            value = value + flipped(value, axis, bit)
            bit *= 2
    return value


def halved(value, dim, which):
    first = lax.index_in_dim(value, 0, dim, keepdims=False)
    second = lax.index_in_dim(value, 1, dim, keepdims=False)
    pick = which == 0
    return jnp.where(pick, first, second), jnp.where(pick, second, first)


def across(value, bit=1):
    return flipped(value, "seq", bit)


def over_batch(value):
    return flipped(value, "batch", 1)


class Halving:
    def __init__(self, keep, got, mine, bits):
        self.keep, self.got, self.mine, self.bits = keep, got, mine, list(bits)

    def step(self):
        bit = self.bits.pop(0)
        blocks = self.keep + self.got
        pairs = blocks.reshape((blocks.shape[0] // 2, 2) + blocks.shape[1:])
        self.keep, send = halved(pairs, 1, (self.mine // bit) % 2)
        self.got = across(send, bit)

    def finish(self):
        while self.bits:
            self.step()
        return (self.keep + self.got)[0]


def tied(works, *others):
    out = lax.optimization_barrier(tuple(work.got for work in works) + others)
    for work, got in zip(works, out):
        work.got = got
    return out[len(works) :]


def times_pair(left, right):
    return left[0] * right[0] - left[1] * right[1], left[0] * right[1] + left[1] * right[0]


def mode_tables(params):
    decay_log, decay_freq, input_re, input_im, output_re, output_im, step_log = params
    step_size = jnp.exp(step_log)[:, None]
    real_part = -jnp.exp(decay_log)
    delta_re = step_size * real_part
    delta_im = step_size * decay_freq
    magnitude = jnp.exp(delta_re)
    lam = (magnitude * jnp.cos(delta_im), magnitude * jnp.sin(delta_im))
    denominator = real_part * real_part + decay_freq * decay_freq
    inverse = (real_part / denominator, -decay_freq / denominator)
    num_re = lam[0] - 1.0
    ratio = (
        (num_re * real_part + lam[1] * decay_freq) / denominator,
        (lam[1] * real_part - num_re * decay_freq) / denominator,
    )
    doubled = (2.0 * output_re, 2.0 * output_im)
    bbar = times_pair(ratio, (input_re, input_im))
    weight = times_pair(doubled, bbar)
    both = times_pair(times_pair(doubled, (input_re, input_im)), inverse)
    tables = (
        (2.0 * bbar[0], 2.0 * bbar[1]),
        times_pair(doubled, ratio),
        weight,
        times_pair(both, lam),
        tuple(-part for part in times_pair(both, ratio)),
    )
    return lam, weight, tables, step_size, real_part


def packed(real, imag):
    return jnp.concatenate([real, imag], axis=1)


def on_device(
    tokens, segments, norm1_gain, norm1_bias, decay_log, decay_freq, input_re, input_im,
    output_re, output_im, step_log, skip_gain, glu_weight, glu_bias, norm2_gain, norm2_bias,
    ffn_in, ffn_in_bias, ffn_out, ffn_out_bias, cotangent,
):
    contexts, piece_len, features = tokens.shape
    rows = contexts * piece_len
    pieces, mine = lax.axis_size("seq"), lax.axis_index("seq")
    channels = features // pieces
    docs = max(1, pieces * piece_len // 256)
    params = (decay_log, decay_freq, input_re, input_im, output_re, output_im, step_log)
    batch_bit = lax.axis_index("batch") % 2
    place = jnp.stack([mine % 2, batch_bit, (mine // 2) % 2, (mine // 4) % 2]).astype(jnp.int32)
    high_bits = [1 << k for k in range(3, pieces.bit_length() - 1)]

    def own(value):
        return lax.dynamic_slice_in_dim(value, mine * channels, channels, 0)

    def row_of(value):
        return jnp.broadcast_to(own(value)[:, None], (channels, LANES))

    def line(value):
        return value.reshape(1, -1)

    def by_channel(value):
        return lax.all_to_all(value, "seq", 0, 0)

    lam_pair, weight_pair = mode_tables(tuple(own(p) for p in params))[:2]
    lam, weight = packed(*lam_pair), packed(*weight_pair)
    skip = row_of(skip_gain)
    flat = tokens.reshape(rows, features)
    cot = cotangent.reshape(rows, features)

    send, up = first_norm(
        flat, cot, segments.reshape(1, rows), line(norm1_gain), line(norm1_bias), pieces
    )
    recv = by_channel(send)
    _, _, tables, step_size, real_part = mode_tables(params)
    recv = recv.reshape(pieces * (channels + 8), rows)
    up_x = over_batch(up)
    ups = [up, up_x, across(up), across(up_x)]
    mixed_rows, enter, lags = recurrence(recv, lam, weight, skip, pieces, docs, FORWARD_UNROLL)
    mixed = by_channel(mixed_rows.reshape(pieces, channels, rows))
    mixed, tables, *ups = lax.optimization_barrier((mixed, tables, *ups))
    mixed = mixed.reshape(features, rows)
    act_parts, z2_parts, ffn_here, ffn_there, ffn_send_here, ffn_send_there, glu_pre, hidden, slope1, slope2, ffn_low = upward(
        place, mixed, flat, line(glu_bias), line(norm2_gain), line(norm2_bias), line(ffn_in_bias),
        glu_weight, ffn_in, pieces,
    )
    in_keep, in_send, glu_keep, glu_send, grad_hidden, turned = downward(
        place, cot, slope2, hidden, glu_pre, slope1, line(norm2_gain), act_parts, z2_parts, ffn_out, ffn_in, glu_weight, pieces
    )

    inner = ffn_in.shape[1]
    ffn_x, ffn_xo = over_batch(ffn_send_here), over_batch(ffn_send_there)
    in_z = across(in_send, 4)
    glu_send, ffn_x, ffn_xo = lax.optimization_barrier((glu_send, ffn_x, ffn_xo))
    glu_x = over_batch(glu_send)
    values = [ffn_here, ffn_x, across(ffn_there), across(ffn_xo)] + ups
    spans = [[(i, 0), (i + 4, 0)] for i in range(4)]
    keep_out, send_out = products(place, values, spans, inner // 4, features, pieces // 2)
    back = by_channel(turned)
    lags, send_out = lax.optimization_barrier((lags, send_out))
    shares = jnp.sum(back[:, channels:], axis=0)
    out = Halving(keep_out, across(send_out, 2), mine, [4] + high_bits)
    grad_rows, sums, firsts, lagsum, bias_part = recurrence_back(
        recv, back.reshape(pieces * (channels + 8), rows), enter, lags, lam, weight, skip,
        pieces, docs, BACKWARD_UNROLL,
    )
    sums, tables, step_size, real_part = lax.optimization_barrier((sums, tables, step_size, real_part))
    tables = tuple(packed(*pair) for pair in tables)
    around = (
        jnp.broadcast_to(step_size, tables[0].shape),
        packed(real_part, real_part),
        packed(decay_freq, decay_freq),
    )
    vectors = jnp.concatenate([lagsum[:, LANES - 1], jnp.sum(bias_part, axis=1)]).reshape(1, -1)
    vectors = jnp.pad(vectors, ((0, 7), (0, LANES - vectors.shape[1])))
    vectors = jnp.concatenate([vectors, shares], axis=1)
    state = jnp.concatenate([jnp.concatenate([sums, firsts], axis=1), vectors], axis=0)
    state = summed(state, ("batch",))
    in_c = across(in_keep)
    grad_rows, glu_x, in_z, in_c, state, tables, around = tied(
        [out], grad_rows, glu_x, in_z, in_c, state, tables, around
    )
    out.step()
    in_keep, out.keep = lax.optimization_barrier((in_keep, out.keep))
    quarter, half = features // 4, features // 2
    values = [in_keep, in_z, in_c, across(in_z)]
    keep_a, send_a, keep_b, send_b = wide_products(place, values, inner, quarter, pieces // 4)
    grad_rows, keep_a = lax.optimization_barrier((grad_rows, keep_a))
    grad_normed = by_channel(grad_rows.reshape(pieces, channels, rows)).reshape(features, rows)
    first = Halving(keep_a, over_batch(send_a), mine, [2] + high_bits)
    second = Halving(keep_b, over_batch(send_b), mine, [2] + high_bits)
    glu_own = glu_keep
    values = [glu_own, glu_x, across(glu_keep), across(glu_x)]
    spans = [[(i, features if i < 2 else features + half), (i, 0)] for i in range(4)]
    keep_glu, send_glu = products(place, values, spans, half, features, pieces // 2)
    (state,) = tied([out], state)
    out.step()
    glu = Halving(keep_glu, across(send_glu, 2), mine, [4] + high_bits)

    def all_batches(value):
        bit = 2
        while bit < lax.axis_size("batch"):
            value = value + flipped(value, "batch", bit)
            bit *= 2
        return value, over_batch(value)

    groups = [[2 * i + c for i in range(pieces // 2)] for c in range(2)]
    state = jnp.broadcast_to(state[None], (pieces // 2,) + state.shape)
    state = lax.all_to_all(state, "seq", 0, 0, axis_index_groups=groups)

    (grad_normed,) = tied([first], grad_normed)
    first.step()
    ffn_res = jnp.dot(ffn_low, ffn_out, preferred_element_type=F32) + ffn_out_bias
    result = (hidden + ffn_res).astype(BF16).reshape(tokens.shape)
    grad_tokens = last_norm(grad_normed, flat, line(norm1_gain), grad_hidden).reshape(tokens.shape)
    glu.step()

    state, result, grad_tokens = tied([second, first, out, glu], state, result, grad_tokens)
    state_c = across(state)
    second.step()
    first.step()
    half_out, other_out = all_batches(out.finish())
    glu.step()

    lengths = (ffn_in.shape[1], 2 * features, features, features, features)
    small = pulled(
        place, state, state_c, tables, line(norm1_gain), line(norm1_bias), line(skip_gain), *around, lengths
    )
    other_out, *small = tied([second, glu, first], other_out, *small)
    grad_params = small[:6]
    vectors = [value.reshape(-1) for value in small[6:]]
    grad_step, grad_skip, grad_gain1, grad_bias1 = vectors[:4]
    bias_in, bias_glu, grad_g2, grad_b2, bias_out = vectors[4:]
    second.step()
    half_a, other_a = all_batches(first.finish())
    half_glu, other_glu = all_batches(glu.finish())

    other_a, other_glu = tied([second], other_a, other_glu)
    half_b, other_b = all_batches(second.finish())
    sum_out = assembled(place, [half_out], [other_out], 0)
    sum_glu = assembled(place, [half_glu], [other_glu], 1)
    sum_in = assembled(place, [half_a, half_b], [other_a, other_b], 1)
    return (
        result, grad_tokens, grad_gain1, grad_bias1, *grad_params, grad_step, grad_skip,
        sum_glu, bias_glu, grad_g2, grad_b2, sum_in, bias_in, sum_out, bias_out,
    )


def solution(mesh):
    spread_over = P("batch", "seq", None)
    in_specs = (spread_over, P("batch", "seq")) + (P(),) * 18 + (spread_over,)
    rows = P("seq", None)
    out_specs = (spread_over,) * 2 + (P(),) * 10 + (rows,) + (P(),) * 3 + (rows, P(), rows, P())
    return jax.shard_map(
        on_device, mesh=mesh, in_specs=in_specs, out_specs=out_specs, check_vma=False
    )
```
